32 devices in a mesh: groups: 2 (over y), gx: 4 (over z), gy: 2 (over x), vert: 2 (over core).
Axes of the slice: x: 2, y: 2, z: 4, core: 2. Of those that a mesh axis runs over, the one named last changes fastest.
Arguments:
- tiles: bfloat16 [6, 2, 128, 8, 16, 128], P('vert', 'gy', ('groups', 'gx')), parts along dimension 2, may hold values from 0.19921875 to 5
- tile_block: int32 [6, 2, 128, 1], P(None, None, 'groups'), parts along dimension 2, may hold values from 0 to 3; in each aligned block of 16 rows (0 to 15, 16 to 31, ..., all dimensions but the last counted through in order) at most 8 rows name the same one
- tile_x: int32 [6, 2, 128], P(None, None, 'groups'), parts along dimension 2, may hold values from 0 to 24
- tile_y: int32 [6, 2, 128], P(None, None, 'groups'), parts along dimension 2, may hold values from 0 to 48
- psf: float32 [6, 3, 15], replicated, may hold values from 0.03 to 0.1
- initial: float32 [256, 128, 128], P(('groups', 'gx'), 'gy'), parts along dimension 0, may hold values from 0.5 to 2
Outputs:
- estimate: float32 [256, 128, 128], P(('groups', 'gx'), 'gy'), parts along dimension 0
The draws below stay inside these ranges and needn't reach their ends.
There are 2 independent parts, one for each index of `groups`. The reference program is written for one: setup_inputs(seed, part) draws one part's arguments, and reference() takes and returns one part's arrays. A program takes and returns all parts, laid end to end along the dimension named above; an argument that names none is the same for every part. Nothing has to cross between parts.
Inputs may be any that keep to these rules, and one draw needn't show every extreme that they name: `tile_block`: among the 16 tiles of one view held by one device (tile numbers in aligned groups of 16 within a block row), no block column is named more than 8 times.
All inputs are finite; a program needn't handle non-finite values.
Results may differ from the reference program's by a relative error of at most 0.0009.
Values may be sent and summed in bfloat16 or wider, within the bound.
A program may use at most 128 MiB of HBM per device.

```python
import math
import jax
import jax.numpy as jnp
import numpy as np
from jax import lax

VIEWS = 6
TAPS = 15
TX = 8
TY = 16
NZ = 128
BY = 64
ITERS = 2
BX = 32
NX = 128
NY = 128
TILES_DEV = 16
TCOLS = 64
CAP = 8
N_GX = 4
N_GY = 2


def with_ends(result, own_key, least, top_value):
    index_at = [jax.random.randint(jax.random.fold_in(own_key, axis), (), 0, length) for axis, length in enumerate(result.shape)]
    longest = result.shape.index(max(result.shape))
    next_to = index_at[:longest] + [(index_at[longest] + 1) % result.shape[longest]] + index_at[longest + 1:]
    return result.at[tuple(index_at)].set(least).at[tuple(next_to)].set(top_value)


def steps_of(key, dims, cuts, smallest, high):
    def one(axis_at, parts):
        steps = jax.random.uniform(jax.random.fold_in(jax.random.fold_in(key, 6), axis_at), (parts,), jnp.float32, smallest / len(cuts), high / len(cuts))
        return jnp.repeat(jnp.exp(steps), dims[axis_at] // parts).reshape((-1,) + (1,) * (len(dims) - axis_at - 1))

    loudness = one(*cuts[0])
    for cut in cuts[1:]:
        loudness = loudness * one(*cut)
    return loudness


def shared_out(stream_key, own, number, rows, count, top, limit, lean):
    ranking = jax.random.permutation(stream_key, count)
    packed, ordinary = load_shares(count, rows * top, limit, lean, True), load_shares(count, rows * top, limit, lean, False)
    places = jnp.arange(count)

    def named(sizes, turn):
        used = int((sizes > 0).sum())
        fixed = max(1, used // 4)
        passed = fixed + (places - fixed + turn * (used - fixed)) % max(1, count - fixed)
        return jnp.zeros((count,), jnp.int32).at[ranking[jnp.where(places < fixed, places, passed)]].set(jnp.asarray(sizes, jnp.int32))

    sizes = jnp.where(number % 4 == 0, named(packed, number // 4), named(ordinary, number - number // 4 - 1))
    mixed = jax.random.permutation(jax.random.fold_in(own, 3), count)
    donor, taker = mixed[0:count // 2 * 2:2], mixed[1:count // 2 * 2:2]
    room = jnp.minimum(sizes[donor] - 1, limit - sizes[taker]) // 2
    room = jnp.where((donor == ranking[0]) | (taker == ranking[0]) | (sizes[taker] == 0), 0, jnp.maximum(room, 0))
    passed = jax.random.randint(jax.random.fold_in(own, 4), (count // 2,), 0, 1 << 20) % (room + 1)
    sizes = sizes.at[donor].add(-passed).at[taker].add(passed)
    labels = jnp.searchsorted(jnp.cumsum(sizes), jnp.arange(rows * top), side="right").astype(jnp.int32)
    table = labels.reshape(top, rows).T
    table = table[jax.random.permutation(jax.random.fold_in(own, 1), rows)]
    turn = jax.random.randint(jax.random.fold_in(own, 2), (rows, 1), 0, top)
    return jnp.take_along_axis(table, (jnp.arange(top)[None, :] + turn) % top, axis=1)


def load_shares(amount, total, most, skew, full):
    weights = [(1 << 20) // math.isqrt(rank ** skew) + 1 for rank in range(1, amount + 1)]
    largest = most if full else min(most, max(-(-total // amount), total * weights[0] // sum(weights)))
    least = 1 if total - largest >= amount - 1 else 0
    holding, rest = [largest] + [least] * (amount - 1), total - largest - least * (amount - 1)
    while rest > 0:
        free = [i for i in range(1, amount) if holding[i] < largest] or [i for i in range(1, amount) if holding[i] < most]
        mass, remaining = sum([weights[i] for i in free]), rest
        for i in free:
            addition = min(most - holding[i], max(1, remaining * weights[i] // mass), rest)
            holding[i] = holding[i] + addition
            rest = rest - addition
    return np.array(holding)


def setup_inputs(seed: int = 0, part: int = 0) -> dict:
    keys = jax.random.split(jax.random.key(seed), 7)
    part_keys = jax.random.split(jax.random.fold_in(keys[6], part), 7)
    tiles = jnp.clip(jnp.exp(math.log(5.0) - 3.2227897 * jax.random.uniform(part_keys[0], (VIEWS, N_GY, TCOLS, TX, TY, NZ), jnp.float32) ** steps_of(part_keys[0], (VIEWS, N_GY, TCOLS, TX, TY, NZ), ((0, 2), (1, 2), (2, 4)), -0.2, 0.2)), 0.19921875, 5.0).astype(jnp.bfloat16)
    tile_block_keys = jax.random.split(jax.random.fold_in(part_keys[1], 1), VIEWS * N_GY * TCOLS // TILES_DEV)
    tile_block_turns = jax.random.permutation(jax.random.fold_in(part_keys[1], 3), VIEWS * N_GY * TCOLS // TILES_DEV)
    tile_block = jax.vmap(lambda own, number: shared_out(jax.random.fold_in(part_keys[1], 2), own, number, TILES_DEV, N_GX, 1, CAP, 2))(tile_block_keys, tile_block_turns).reshape((VIEWS, N_GY, TCOLS, 1))
    tile_x = with_ends(jax.random.randint(part_keys[2], (VIEWS, N_GY, TCOLS), 0, BX - TX + 1), jax.random.fold_in(part_keys[2], 1), 0, BX - TX).astype(jnp.int32)
    tile_y = with_ends(jax.random.randint(part_keys[3], (VIEWS, N_GY, TCOLS), 0, BY - TY + 1), jax.random.fold_in(part_keys[3], 1), 0, BY - TY).astype(jnp.int32)
    psf = jnp.clip(jax.random.uniform(keys[4], (VIEWS, 3, TAPS), jnp.float32, 0.03, 0.1), 0.03, 0.1)
    initial = jnp.clip(jnp.exp(math.log(2.0) - 1.3862944 * jax.random.uniform(part_keys[5], (NX, NY, NZ), jnp.float32) ** steps_of(part_keys[5], (NX, NY, NZ), ((0, 4), (1, 2)), -0.2, 0.2)), 0.5, 2.0)
    return {"tiles": tiles, "tile_block": tile_block, "tile_x": tile_x, "tile_y": tile_y, "psf": psf, "initial": initial}


soft_floor = 0.01
damping = 0.5


def valid_pass(volume, kernel, dimension, adjoint):
    radius = kernel.shape[0] // 2
    length = volume.shape[dimension] - 2 * radius
    summed = None
    for tap_index in range(kernel.shape[0]):
        offset = 2 * radius - tap_index if adjoint else tap_index
        weighted = kernel[tap_index] * lax.slice_in_dim(volume, offset, offset + length, axis=dimension)
        summed = weighted if summed is None else summed + weighted
    return summed


def padded_pass(volume, kernel, dimension, adjoint):
    radius = kernel.shape[0] // 2
    margins = [(0, 0)] * volume.ndim
    margins[dimension] = (radius, radius)
    return valid_pass(jnp.pad(volume, margins), kernel, dimension, adjoint)


def blur(volume, kernels):
    volume = padded_pass(volume, kernels[0], 0, False)
    volume = padded_pass(volume, kernels[1], 1, False)
    return padded_pass(volume, kernels[2], 2, False)


def back_project(volume, kernels):
    volume = padded_pass(volume, kernels[2], 2, True)
    volume = padded_pass(volume, kernels[0], 0, True)
    return padded_pass(volume, kernels[1], 1, True)


def assemble(view_tiles, view_blocks, view_x, view_y):
    tile_rows = jnp.repeat(jnp.arange(N_GY, dtype=jnp.int32), TCOLS)
    flat_tiles = view_tiles.reshape(N_GY * TCOLS, TX, TY, NZ)
    start_x = (view_blocks.reshape(-1) * BX + view_x.reshape(-1)).astype(jnp.int32)
    start_y = (tile_rows * BY + view_y.reshape(-1)).astype(jnp.int32)

    def deposit(state_pair, scanned):
        summed, counted = state_pair
        tile_piece, corner_x, corner_y = scanned
        anchor = jnp.zeros((), jnp.int32)
        existing = lax.dynamic_slice(summed, (corner_x, corner_y, anchor), (TX, TY, NZ))
        summed = lax.dynamic_update_slice(summed, existing + tile_piece.astype(jnp.float32), (corner_x, corner_y, anchor))
        covered = lax.dynamic_slice(counted, (corner_x, corner_y), (TX, TY))
        counted = lax.dynamic_update_slice(counted, covered + 1.0, (corner_x, corner_y))
        return (summed, counted), None

    starting = (jnp.zeros((NX, NY, NZ), jnp.float32), jnp.zeros((NX, NY), jnp.float32))
    final_pair, leftover = lax.scan(deposit, starting, (flat_tiles, start_x, start_y))
    return final_pair


def reference(tiles, tile_block, tile_x, tile_y, psf, initial):
    observed_views = []
    norm_field = jnp.zeros((NX, NY, NZ), jnp.float32)
    for view_index in range(VIEWS):
        summed, counted = assemble(tiles[view_index], tile_block[view_index, :, :, 0], tile_x[view_index], tile_y[view_index])
        observed_views.append(summed / jnp.maximum(counted, 1.0)[:, :, None])
        coverage = jnp.broadcast_to(jnp.minimum(counted, 1.0)[:, :, None], (NX, NY, NZ))
        norm_field = norm_field + back_project(coverage, psf[view_index])
    estimate = initial
    for sweep_index in range(ITERS):
        correction = jnp.zeros((NX, NY, NZ), jnp.float32)
        for view_index in range(VIEWS):
            quotient = observed_views[view_index] / (blur(estimate, psf[view_index]) + soft_floor)
            correction = correction + back_project(quotient, psf[view_index])
        estimate = estimate * (correction + damping) / (norm_field + damping)
    return estimate
```

```python
import functools

import jax
import jax.numpy as jnp
from jax import lax
from jax.experimental import pallas as pl
from jax.experimental.pallas import tpu as pltpu
from jax.sharding import PartitionSpec as P

ITERS = 2
HALO_Y = 8

soft_floor = 0.01
damping = 0.5


def split_high_low(matrix):
    high = lax.reduce_precision(matrix, 8, 7)
    return high.astype(jnp.bfloat16), (matrix - high).astype(jnp.bfloat16)


def banded(taps, difference):
    summed = None
    for tap_index in range(taps.shape[-1]):
        term = jnp.where(difference == tap_index, taps[..., tap_index, None, None], 0.0)
        summed = term if summed is None else summed + term
    return summed


class Links:
    def __init__(self, sizes, radius, block_x):
        self.radius = radius
        self.block_x = block_x
        self.me = (lax.axis_index("gx"), lax.axis_index("gy"))
        self.sizes = sizes
        self.directions = [
            (dx, dy) for dx in (-1, 0, 1) for dy in (-1, 0, 1) if (dx, dy) != (0, 0)
        ]

    def exists(self, dx, dy):
        good = None
        for step, me, count in zip((dx, dy), self.me, self.sizes):
            if step == 0:
                continue
            test = me > 0 if step == -1 else me < count - 1
            good = test if good is None else jnp.logical_and(good, test)
        return good

    def device(self, dx, dy):
        return {"gx": self.me[0] + dx, "gy": self.me[1] + dy}

    def greet(self, others=()):
        barrier = pltpu.get_barrier_semaphore()
        for dx, dy in self.directions:

            @pl.when(self.exists(dx, dy))
            def _():
                pl.semaphore_signal(
                    barrier,
                    inc=1,
                    device_id=self.device(dx, dy),
                    device_id_type=pl.DeviceIdType.MESH,
                )

        for other in others:
            pl.semaphore_signal(
                barrier, inc=1, device_id=other, device_id_type=pl.DeviceIdType.MESH
            )

    def await_greetings(self, others=0):
        peers = others
        for dx, dy in self.directions:
            peers = peers + self.exists(dx, dy).astype(jnp.int32)
        pl.semaphore_wait(pltpu.get_barrier_semaphore(), peers)

    def span(self, step):
        if step == 0:
            return pl.ds(self.radius, self.block_x)
        return pl.ds(self.radius if step == -1 else self.block_x, self.radius)

    def ghost(self, step):
        if step == 0:
            return pl.ds(self.radius, self.block_x)
        return pl.ds(0 if step == -1 else self.block_x + self.radius, self.radius)

    def part(self, step):
        if step == 0:
            return pl.ds(0, self.block_x)
        return pl.ds(0 if step == -1 else self.block_x - self.radius, self.radius)

    def exchange(self, make, send_sem, recv_sem):
        self.start(make, send_sem, recv_sem, self.directions)
        self.finish(make, send_sem, recv_sem, self.directions)

    def across_x(self):
        return [one for one in self.directions if one[0] != 0]

    def along_y_only(self):
        return [one for one in self.directions if one[0] == 0]

    def copy(self, make, send_sem, recv_sem, dx, dy):
        index = self.directions.index((dx, dy))
        src, dst = make(dx, dy)
        return pltpu.make_async_remote_copy(
            src_ref=src,
            dst_ref=dst,
            send_sem=send_sem.at[index],
            recv_sem=recv_sem.at[index],
            device_id=self.device(dx, dy),
            device_id_type=pl.DeviceIdType.MESH,
        )

    def start(self, make, send_sem, recv_sem, directions):
        for dx, dy in directions:

            @pl.when(self.exists(dx, dy))
            def _():
                self.copy(make, send_sem, recv_sem, dx, dy).start()

    def finish(self, make, send_sem, recv_sem, directions):
        for dx, dy in directions:

            @pl.when(self.exists(dx, dy))
            def _():
                self.copy(make, send_sem, recv_sem, dx, dy).wait_send()

            @pl.when(self.exists(-dx, -dy))
            def _():
                self.copy(make, send_sem, recv_sem, dx, dy).wait_recv()


def ghosts_of_estimate(links, center, low, high, send_low, send_high):
    def make(dx, dy):
        if dy == 0:
            return center.at[links.span(dx)], center.at[links.ghost(-dx)]
        if dy == -1:
            return send_low.at[links.part(dx)], high.at[links.ghost(-dx)]
        return send_high.at[links.part(dx)], low.at[links.ghost(-dx)]

    return make


def ghosts_of_sums(links, out_x, out_y, in_x, in_y):
    def make(dx, dy):
        if dy == 0:
            side = 0 if dx == -1 else 1
            return out_x.at[side], in_x.at[1 - side]
        side = 0 if dy == -1 else 1
        return out_y.at[side, links.ghost(dx)], in_y.at[1 - side, links.ghost(-dx)]

    return make


def clear_missing(links, center, low, high):
    radius = links.radius
    for step in (-1, 1):

        @pl.when(jnp.logical_not(links.exists(step, 0)))
        def _():
            for rows in (center, low, high):
                rows[links.ghost(step)] = jnp.zeros((radius,) + rows.shape[1:], rows.dtype)

        @pl.when(jnp.logical_not(links.exists(0, step)))
        def _():
            rows = low if step == -1 else high
            rows[...] = jnp.zeros(rows.shape, rows.dtype)

    tail = links.block_x + 2 * radius
    for rows in (center, low, high):
        rows[tail:] = jnp.zeros((rows.shape[0] - tail,) + rows.shape[1:], rows.dtype)


def publish(links, center, send_low, send_high, x, plane):
    center[links.radius + x] = plane.astype(jnp.bfloat16)
    send_low[x] = plane[:HALO_Y].astype(jnp.bfloat16)
    send_high[x] = plane[plane.shape[0] - HALO_Y :].astype(jnp.bfloat16)


def pass_along_y(center, low, high, along_y, passed_y, views):
    block_y, depth = center.shape[1:]

    @pl.loop(0, center.shape[0] // 4)
    def _(step):
        for first in (4 * step, 4 * step + 2):
            columns = []
            for x in (first, first + 1):
                edges = jnp.concatenate(
                    [low[x].astype(jnp.float32), high[x].astype(jnp.float32)], axis=0
                ).astype(jnp.bfloat16)
                columns.append(jnp.concatenate([center[x], edges], axis=0))
            both = jnp.concatenate(columns, axis=1)
            both = jnp.concatenate([both, both], axis=0)
            result = jnp.dot(along_y[...], both, preferred_element_type=jnp.float32)
            for view in range(views):
                rows = slice(view * block_y, (view + 1) * block_y)
                passed_y[view, first] = result[rows, :depth]
                passed_y[view, first + 1] = result[rows, depth:]


def pass_along_xz(taps_x, passed_y, along_z, view, first, group):
    planes = []
    for inner in range(group):
        x = first + inner
        value = taps_x[view, 0] * passed_y[view, x]
        for tap in range(1, taps_x.shape[1]):
            value = value + taps_x[view, tap] * passed_y[view, x + tap]
        planes.append(value.astype(jnp.bfloat16))
    stacked = jnp.concatenate(planes, axis=0)
    stacked = jnp.concatenate([stacked, stacked], axis=1)
    return jnp.dot(stacked, along_z, preferred_element_type=jnp.float32)


def spread_quotient(measured, blurred, back_z):
    quotient = (measured / (blurred + soft_floor)).astype(jnp.bfloat16)
    quotient = jnp.concatenate([quotient, quotient], axis=1)
    return jnp.dot(quotient, back_z, preferred_element_type=jnp.float32)


def group_of(block_x):
    group = 4
    while block_x % group:
        group //= 2
    return group


def halo_kernel(
    sizes, radius, initial, center, low, high, all_center, all_low, all_high, *scratch
):
    send_low, send_high, send_sem, recv_sem = scratch
    block_x = initial.shape[0]
    links = Links(sizes, radius, block_x)
    links.greet()

    @pl.loop(0, block_x)
    def _(x):
        publish(links, all_center, send_low, send_high, x, initial[x])

    clear_missing(links, all_center, all_low, all_high)
    links.await_greetings()
    links.exchange(
        ghosts_of_estimate(links, all_center, all_low, all_high, send_low, send_high),
        send_sem,
        recv_sem,
    )

    @pl.loop(0, center.shape[0])
    def _(x):
        center[x] = all_center[x]
        low[x] = all_low[x]
        high[x] = all_high[x]


def blur_kernel(taps_x, center, low, high, along_y, along_z, blurred, passed_y):
    views, block_x, block_y, depth = blurred.shape
    pass_along_y(center, low, high, along_y, passed_y, views)
    group = group_of(block_x)

    @pl.loop(0, block_x // group)
    def _(step):
        for view in range(views):
            value = pass_along_xz(taps_x, passed_y, along_z[view], view, step * group, group)
            blurred[view, pl.ds(step * group, group)] = value.reshape(group, block_y, depth)


def estimate_scratch(planes, block_x, block_y, depth):
    return [
        pltpu.VMEM((planes, block_y, depth), jnp.bfloat16),
        pltpu.VMEM((planes, HALO_Y, depth), jnp.bfloat16),
        pltpu.VMEM((planes, HALO_Y, depth), jnp.bfloat16),
        pltpu.VMEM((block_x, HALO_Y, depth), jnp.bfloat16),
        pltpu.VMEM((block_x, HALO_Y, depth), jnp.bfloat16),
    ]


def planes_of(block_x, radius):
    return -(-(block_x + 2 * radius) // 4) * 4


def first_halos(sizes, radius, initial):
    block_x, block_y, depth = initial.shape
    vmem = pl.BlockSpec(memory_space=pltpu.VMEM)
    scratch = estimate_scratch(planes_of(block_x, radius), block_x, block_y, depth)
    return pl.pallas_call(
        functools.partial(halo_kernel, sizes, radius),
        out_shape=[jax.ShapeDtypeStruct(one.shape, one.dtype) for one in scratch[:3]],
        in_specs=[vmem],
        out_specs=[vmem] * 3,
        scratch_shapes=scratch
        + [pltpu.SemaphoreType.DMA((8,)), pltpu.SemaphoreType.DMA((8,))],
        compiler_params=pltpu.CompilerParams(
            collective_id=0, has_side_effects=True, vmem_limit_bytes=12 << 20
        ),
    )(initial)


def first_blur(taps_x, halos, along_y, along_z, block_x):
    planes, block_y, depth = halos[0].shape
    views = taps_x.shape[0]
    vmem = pl.BlockSpec(memory_space=pltpu.VMEM)
    shape = (views, block_x, block_y, depth)
    return pl.pallas_call(
        blur_kernel,
        out_shape=jax.ShapeDtypeStruct(shape, jnp.float32),
        in_specs=[pl.BlockSpec(memory_space=pltpu.SMEM)] + [vmem] * 5,
        out_specs=vmem,
        scratch_shapes=[pltpu.VMEM((views, planes, block_y, depth), jnp.float32)],
        cost_estimate=pl.CostEstimate(
            flops=10_000_000_000, bytes_accessed=40_000_000, transcendentals=0
        ),
        compiler_params=pltpu.CompilerParams(vmem_limit_bytes=20 << 20),
    )(taps_x, *halos, along_y, along_z)


def place_kernel(
    below, filled, corner_x, corner_y, tiles, blurred, back_z, observed, spread, summed, counted
):
    view = pl.program_id(0)
    sources, _, capacity, wide, tall, depth = tiles.shape
    _, block_x, block_y, _ = observed.shape
    summed[...] = jnp.zeros_like(summed)
    counted[...] = jnp.zeros_like(counted)

    @pl.loop(0, sources)
    def _(source):
        @pl.loop(0, capacity)
        def _(slot):
            at = source * capacity + slot

            @pl.when(filled[view, at] > 0)
            def _():
                x = corner_x[view, at]
                y = corner_y[view, at]
                where = (pl.ds(x, wide), pl.ds(y, tall), slice(None))
                summed[where] = summed[where] + tiles[source, 0, slot].astype(jnp.float32)
                counted[where] = counted[where] + 1.0

    group = group_of(block_x)
    beyond = spread.shape[1] - below - block_x
    spread[0, :below] = jnp.zeros((below, block_y, depth), jnp.float32)
    spread[0, below + block_x :] = jnp.zeros((beyond, block_y, depth), jnp.float32)

    @pl.loop(0, block_x // group)
    def _(step):
        planes = pl.ds(step * group, group)
        measured = summed[planes] / jnp.maximum(counted[planes], 1.0)
        observed[0, planes] = measured
        flat = (group * block_y, depth)
        result = spread_quotient(
            measured.reshape(flat), blurred[0, planes].reshape(flat), back_z[0]
        )
        spread[0, pl.ds(below + step * group, group)] = result.reshape(group, block_y, depth)


def place(filled, corner_x, corner_y, arrived, blurred, back_z, radius):
    sources, views, capacity, wide, tall, depth = arrived.shape
    shape = blurred.shape
    volume = pl.BlockSpec((1,) + shape[1:], lambda v, *_: (v, 0, 0, 0))
    padded = (views, planes_of(shape[1], radius) + 2 * radius) + shape[2:]
    return pl.pallas_call(
        functools.partial(place_kernel, 2 * radius),
        out_shape=[
            jax.ShapeDtypeStruct(shape, jnp.float32),
            jax.ShapeDtypeStruct(padded, jnp.float32),
        ],
        grid_spec=pltpu.PrefetchScalarGridSpec(
            num_scalar_prefetch=3,
            grid=(views,),
            in_specs=[
                pl.BlockSpec(
                    (sources, 1, capacity, wide, tall, depth), lambda v, *_: (0, v, 0, 0, 0, 0)
                ),
                volume,
                pl.BlockSpec((1,) + back_z.shape[1:], lambda v, *_: (v, 0, 0)),
            ],
            out_specs=[
                volume,
                pl.BlockSpec((1,) + padded[1:], lambda v, *_: (v, 0, 0, 0)),
            ],
            scratch_shapes=[pltpu.VMEM(shape[1:], jnp.float32)] * 2,
        ),
        compiler_params=pltpu.CompilerParams(vmem_limit_bytes=20 << 20),
    )(filled, corner_x, corner_y, arrived, blurred, back_z)


def sweep_kernel(sizes, *refs):
    (
        taps_x,
        observed,
        spreads,
        initial,
        inverse_norm,
        along_y,
        back_y,
        along_z,
        back_z,
        estimate,
        center,
        low,
        high,
        send_low,
        send_high,
        passed_y,
        passed_z,
        acc,
        out_x,
        out_y,
        in_x,
        in_y,
        far_x,
        far_y,
        vert_in,
        est_send,
        est_recv,
        acc_send,
        acc_recv,
        vert_send,
        vert_recv,
        far_send,
        far_recv,
    ) = refs
    views, block_x, block_y, depth = observed.shape
    tap_count = taps_x.shape[1]
    radius = tap_count // 2
    planes = center.shape[1]
    bf16 = jnp.bfloat16
    f32 = jnp.float32
    links = Links(sizes, radius, block_x)
    partner = {"vert": 1 - lax.axis_index("vert")}
    links.greet((partner,))
    for sweep in range(ITERS):
        if sweep > 0:
            at = sweep - 1
            clear_missing(links, center.at[at], low.at[at], high.at[at])
        for step in (-1, 1):
            side = 0 if step == -1 else 1

            @pl.when(jnp.logical_not(links.exists(step, 0)))
            def _():
                in_x[sweep, side] = jnp.zeros(in_x.shape[2:], bf16)
                for other in range(2):
                    in_y[sweep, other, links.ghost(step)] = jnp.zeros(
                        (radius,) + in_y.shape[3:], bf16
                    )

            @pl.when(jnp.logical_not(links.exists(0, step)))
            def _():
                in_y[sweep, side] = jnp.zeros(in_y.shape[2:], bf16)

    below = 2 * radius
    beyond = passed_z.shape[1] - below - block_x
    passed_z[:, :below] = jnp.zeros((views, below, block_y, depth), f32)
    passed_z[:, below + block_x :] = jnp.zeros((views, beyond, block_y, depth), f32)
    group = group_of(block_x)

    for sweep in range(ITERS):
        if sweep > 0:
            at = sweep - 1
            pass_along_y(center.at[at], low.at[at], high.at[at], along_y, passed_y, views)

            @pl.loop(0, block_x // group)
            def _(step):
                first = step * group
                for view in range(views):
                    blurred = pass_along_xz(taps_x, passed_y, along_z[view], view, first, group)
                    measured = observed[view, pl.ds(first, group)].reshape(blurred.shape)
                    result = spread_quotient(measured, blurred, back_z[view])
                    passed_z[view, pl.ds(below + first, group)] = result.reshape(
                        group, block_y, depth
                    )

        if sweep == 0:
            links.await_greetings(1)

        def vert(start, size):
            chunk = pl.ds(start, size)
            return pltpu.make_async_remote_copy(
                src_ref=acc.at[sweep, chunk],
                dst_ref=vert_in.at[sweep, chunk],
                send_sem=vert_send.at[sweep],
                recv_sem=vert_recv.at[sweep],
                device_id=partner,
                device_id_type=pl.DeviceIdType.MESH,
            )

        first_chunk = radius // 4
        last_chunk = (radius + block_x - 1) // 4

        source = spreads if sweep == 0 else passed_z
        far_chunk = (radius + block_x) // 4
        edge_turns = planes // 4 - far_chunk + -(-radius // 4)
        def adjoint(turn):
            step = lax.rem(turn + far_chunk, planes // 4)
            for first in (4 * step, 4 * step + 2):
                columns = []
                for x in (first, first + 1):
                    stack = []
                    for view in range(views):
                        value = taps_x[view, 0] * source[view, x + below]
                        for tap in range(1, tap_count):
                            value = value + taps_x[view, tap] * source[view, x + below - tap]
                        stack.append(value.astype(bf16))
                    columns.append(jnp.concatenate(stack, axis=0))
                both = jnp.concatenate(columns, axis=1)
                result = jnp.dot(back_y[...], both, preferred_element_type=f32)
                rows = block_y + 2 * HALO_Y
                result = result[:rows] + result[rows:]
                for side in range(2):
                    x = first + side
                    lanes = slice(side * depth, (side + 1) * depth)
                    acc[sweep, x] = result[:block_y, lanes]
                    out_y[sweep, 0, x] = result[block_y : block_y + HALO_Y, lanes].astype(bf16)
                    out_y[sweep, 1, x] = result[block_y + HALO_Y :, lanes].astype(bf16)

            @pl.when(jnp.logical_and(step >= first_chunk, step <= last_chunk))
            def _():
                vert(4 * step, 4).start()

        sums = (
            ghosts_of_sums(
                links, out_x.at[sweep], out_y.at[sweep], in_x.at[sweep], in_y.at[sweep]
            ),
            acc_send.at[sweep],
            acc_recv.at[sweep],
        )

        @pl.loop(0, edge_turns)
        def _(turn):
            adjoint(turn)

        @pl.loop(0, radius)
        def _(x):
            out_x[sweep, 0, x] = acc[sweep, x].astype(bf16)
            out_x[sweep, 1, x] = acc[sweep, radius + block_x + x].astype(bf16)

        links.start(*sums, links.across_x())

        @pl.loop(edge_turns, planes // 4)
        def _(turn):
            adjoint(turn)

        links.start(*sums, links.along_y_only())
        links.finish(*sums, links.across_x())
        links.finish(*sums, links.along_y_only())
        forwards = [
            pltpu.make_async_remote_copy(
                src_ref=near.at[sweep],
                dst_ref=far.at[sweep],
                send_sem=far_send.at[sweep, index],
                recv_sem=far_recv.at[sweep, index],
                device_id=partner,
                device_id_type=pl.DeviceIdType.MESH,
            )
            for index, (near, far) in enumerate(((in_x, far_x), (in_y, far_y)))
        ]
        for forward in forwards:
            forward.start()
        vert(4 * first_chunk, 4 * (last_chunk - first_chunk + 1)).wait()

        @pl.loop(0, block_x)
        def _(x):
            acc[sweep, radius + x] = acc[sweep, radius + x] + vert_in[sweep, radius + x]

        for forward in forwards:
            forward.wait()

        def beyond_y(side, plane):
            return in_y[sweep, side, plane].astype(f32) + far_y[sweep, side, plane].astype(f32)

        @pl.loop(0, radius)
        def _(x):
            for side, at, beside in ((0, radius + x, x), (1, block_x + x, radius + block_x + x)):
                plane = acc[sweep, at] + (
                    in_x[sweep, side, x].astype(f32) + far_x[sweep, side, x].astype(f32)
                )
                first = plane[:HALO_Y] + beyond_y(0, beside)
                last = plane[block_y - HALO_Y :] + beyond_y(1, beside)
                acc[sweep, at] = jnp.concatenate(
                    [first, plane[HALO_Y : block_y - HALO_Y], last], axis=0
                )

        def update(x):
            plane = acc[sweep, radius + x]
            first = plane[:HALO_Y] + beyond_y(0, radius + x)
            last = plane[block_y - HALO_Y :] + beyond_y(1, radius + x)
            combined = jnp.concatenate([first, plane[HALO_Y : block_y - HALO_Y], last], axis=0)
            before = initial[x] if sweep == 0 else estimate[x]
            after = before * (combined + damping) * inverse_norm[x]
            estimate[x] = after
            if sweep + 1 < ITERS:
                publish(
                    links, center.at[sweep], send_low.at[sweep], send_high.at[sweep], x, after
                )

        if sweep + 1 < ITERS:
            news = (
                ghosts_of_estimate(
                    links,
                    center.at[sweep],
                    low.at[sweep],
                    high.at[sweep],
                    send_low.at[sweep],
                    send_high.at[sweep],
                ),
                est_send.at[sweep],
                est_recv.at[sweep],
            )

            @pl.loop(0, radius)
            def _(x):
                update(x)
                update(block_x - radius + x)

            links.start(*news, links.across_x())

            @pl.loop(radius, block_x - radius)
            def _(x):
                update(x)

            links.start(*news, links.along_y_only())
            links.finish(*news, links.directions)
        else:

            @pl.loop(0, block_x)
            def _(x):
                update(x)


def sweeps(
    sizes, taps_x, observed, spreads, initial, inverse_norm, along_y, back_y, along_z, back_z
):
    block_x, block_y, depth = initial.shape
    views = observed.shape[0]
    radius = taps_x.shape[1] // 2
    planes = planes_of(block_x, radius)
    extended_x = block_x + 2 * radius
    vmem = pl.BlockSpec(memory_space=pltpu.VMEM)
    bf16 = jnp.bfloat16
    f32 = jnp.float32
    repeats = ITERS - 1
    return pl.pallas_call(
        functools.partial(sweep_kernel, sizes),
        out_shape=jax.ShapeDtypeStruct(initial.shape, f32),
        in_specs=[pl.BlockSpec(memory_space=pltpu.SMEM)] + [vmem] * 8,
        out_specs=vmem,
        scratch_shapes=[
            pltpu.VMEM((repeats,) + scratch.shape, scratch.dtype)
            for scratch in estimate_scratch(planes, block_x, block_y, depth)
        ]
        + [
            pltpu.VMEM((views, planes, block_y, depth), f32),
            pltpu.VMEM((views, planes + 2 * radius, block_y, depth), f32),
            pltpu.VMEM((ITERS, planes, block_y, depth), f32),
            pltpu.VMEM((ITERS, 2, radius, block_y, depth), bf16),
            pltpu.VMEM((ITERS, 2, planes, HALO_Y, depth), bf16),
            pltpu.VMEM((ITERS, 2, radius, block_y, depth), bf16),
            pltpu.VMEM((ITERS, 2, extended_x, HALO_Y, depth), bf16),
            pltpu.VMEM((ITERS, 2, radius, block_y, depth), bf16),
            pltpu.VMEM((ITERS, 2, extended_x, HALO_Y, depth), bf16),
            pltpu.VMEM((ITERS, planes, block_y, depth), f32),
            pltpu.SemaphoreType.DMA((repeats, 8)),
            pltpu.SemaphoreType.DMA((repeats, 8)),
            pltpu.SemaphoreType.DMA((ITERS, 8)),
            pltpu.SemaphoreType.DMA((ITERS, 8)),
            pltpu.SemaphoreType.DMA((ITERS,)),
            pltpu.SemaphoreType.DMA((ITERS,)),
            pltpu.SemaphoreType.DMA((ITERS, 2)),
            pltpu.SemaphoreType.DMA((ITERS, 2)),
        ],
        compiler_params=pltpu.CompilerParams(
            collective_id=1, has_side_effects=True, vmem_limit_bytes=40 << 20
        ),
    )(taps_x, observed, spreads, initial, inverse_norm, along_y, back_y, along_z, back_z)


PAIR_SLOTS = 8
ROW = 40
FAR_AWAY = -1000
MESH = pl.DeviceIdType.MESH


def far_slots(per_device):
    return 3 * per_device // 4


def plan_kernel(per_device, block, xs, ys, pack, slot, entry_x, entry_y):
    views = pack.shape[0]
    me = lax.axis_index("gx")
    row = lax.axis_index("gy")
    first = lax.axis_index("vert") * views
    in_low = me < 2
    beside = jnp.where(lax.rem(me, 2) == 0, me + 1, me - 1)
    far_base = jnp.where(in_low, 2, 0)
    far_outer = jnp.where(in_low, 3, 0)
    far_gate = jnp.where(in_low, 2, 1)
    my_outer = jnp.where(in_low, 0, 3)
    spare = 4 * PAIR_SLOTS
    one, zero = jnp.int32(1), jnp.int32(0)
    for view in range(views):
        for at in range(spare):
            pack[view, at] = zero
            slot[view, at] = zero
            entry_x[view, at] = zero
            entry_y[view, at] = jnp.int32(FAR_AWAY)

        def enter(at, where, column):
            slot[view, at] = where
            entry_x[view, at] = xs[first + view, row, column]
            entry_y[view, at] = ys[first + view, row, column]

        mine = near = outer = zero
        for j in range(per_device):
            column = me * per_device + j
            target = block[first + view, row, column]
            enter(jnp.where(target == me, mine, spare), jnp.int32(j), column)
            at = jnp.where(
                target == beside,
                near,
                jnp.where(target == far_outer, PAIR_SLOTS + outer, spare),
            )
            pack[view, at] = jnp.int32(j)
            mine = mine + jnp.where(target == me, one, zero)
            near = near + jnp.where(target == beside, one, zero)
            outer = outer + jnp.where(target == far_outer, one, zero)
        for j in range(per_device):
            target = block[first + view, row, me * per_device + j]
            pack[view, jnp.where(target == far_gate, PAIR_SLOTS + outer, spare)] = jnp.int32(j)
            outer = outer + jnp.where(target == far_gate, one, zero)
        found = zero
        for j in range(per_device):
            column = beside * per_device + j
            hit = block[first + view, row, column] == me
            enter(jnp.where(hit, PAIR_SLOTS + found, spare), found, column)
            found = found + jnp.where(hit, one, zero)
        for side in range(2):
            base = (2 + side) * PAIR_SLOTS
            found = ahead = zero
            for j in range(per_device):
                column = (far_base + side) * per_device + j
                target = block[first + view, row, column]
                hit = target == me
                enter(jnp.where(hit, base + found, spare), found, column)
                found = found + jnp.where(hit, one, zero)
                ahead = ahead + jnp.where(target == my_outer, one, zero)
            ahead = jnp.where(me == my_outer, zero, ahead)
            for at in range(base, base + PAIR_SLOTS):
                slot[view, at] = jnp.minimum(slot[view, at] + ahead, far_slots(per_device) - 1)


def plan(views, per_device, block, xs, ys):
    smem = pl.BlockSpec(memory_space=pltpu.SMEM)
    return pl.pallas_call(
        functools.partial(plan_kernel, per_device),
        out_shape=[jax.ShapeDtypeStruct((views, ROW), jnp.int32)] * 4,
        in_specs=[smem] * 3,
        out_specs=[smem] * 4,
    )(block, xs, ys)


def band_of(psf, view, dim, difference):
    summed = jnp.zeros(difference.shape, jnp.float32)
    for tap in range(psf.shape[2]):
        summed = jnp.where(difference == tap, psf[view, dim, tap], summed)
    return summed


def halves(value):
    high = value.astype(jnp.bfloat16)
    return high, (value - high.astype(jnp.float32)).astype(jnp.bfloat16)


def iota(shape, dim):
    return lax.broadcasted_iota(jnp.int32, shape, dim)


def make_bands(psf, first, radius, block_y, along_y, back_y, back_one, along_z, back_z):
    views = along_z.shape[0]
    depth = along_z.shape[2]
    wide = block_y + 2 * HALO_Y

    def place_of(index):
        inside = jnp.where(index >= wide, index - wide, index)
        return jnp.where(
            inside < block_y,
            inside,
            jnp.where(inside < block_y + HALO_Y, inside - block_y - HALO_Y, inside - HALO_Y),
        )

    backs = []
    for view in range(views):
        shape = (block_y, 2 * wide)
        column = iota(shape, 1)
        high, low = halves(
            band_of(psf, first + view, 1, place_of(column) - iota(shape, 0) + radius)
        )
        f32 = jnp.float32
        rows = slice(view * block_y, (view + 1) * block_y)
        along_y[rows] = jnp.where(column < wide, high.astype(f32), low.astype(f32)).astype(
            jnp.bfloat16
        )
        shape = (2 * wide, block_y)
        row = iota(shape, 0)
        high, low = halves(band_of(psf, first + view, 1, place_of(row) - iota(shape, 1) + radius))
        back = jnp.where(row < wide, high.astype(f32), low.astype(f32))
        backs.append(back)
        back_one[view] = back.astype(jnp.bfloat16)
        shape = (depth, depth)
        difference = iota(shape, 0) - iota(shape, 1)
        along_z[view] = jnp.concatenate(
            halves(band_of(psf, first + view, 2, difference + radius)), axis=0
        )
        back_z[view] = jnp.concatenate(
            halves(band_of(psf, first + view, 2, radius - difference)), axis=0
        )
    back_y[...] = jnp.concatenate(backs, axis=1).astype(jnp.bfloat16)


def contract_last(left, right):
    return lax.dot_general(
        left, right, (((1,), (1,)), ((), ())), preferred_element_type=jnp.float32
    )


def make_norm(psf, first, radius, tile_shape, block, xs, ys, counts, spread, inverse_norm, scale):
    all_views, rows, tiles_row = block.shape
    block_x, block_y, depth = inverse_norm.shape
    views = scale.shape[0]
    tile_wide, tile_tall = tile_shape
    f32 = jnp.float32
    bf16 = jnp.bfloat16
    edge = 8
    near_x = block_x + 2 * edge
    near_y = block_y + 2 * edge
    start_x = lax.axis_index("gx") * block_x - edge
    start_y = lax.axis_index("gy") * block_y - edge
    profiles = []
    for view in range(all_views):
        summed = None
        for row in range(rows):
            left = block[view, row : row + 1] * block_x + xs[view, row : row + 1]
            top = ys[view, row : row + 1] + row * block_y
            from_x = iota((near_x, tiles_row), 0) + start_x - left
            from_y = iota((near_y, tiles_row), 0) + start_y - top
            in_x = jnp.where((from_x >= 0) & (from_x < tile_wide), f32(1), f32(0)).astype(bf16)
            in_y = jnp.where((from_y >= 0) & (from_y < tile_tall), f32(1), f32(0)).astype(bf16)
            term = contract_last(in_y, in_x)
            summed = term if summed is None else summed + term
        counts[view] = summed
        covered = jnp.minimum(summed, 1.0).astype(bf16)
        shape = (block_y, near_y)
        high, low = halves(
            band_of(psf, view, 1, iota(shape, 0) - (iota(shape, 1) - edge) + radius)
        )
        value = jnp.dot(high, covered, preferred_element_type=f32)
        value = value + jnp.dot(low, covered, preferred_element_type=f32)
        shape = (near_x, block_x)
        high, low = halves(
            band_of(psf, view, 0, iota(shape, 1) - (iota(shape, 0) - edge) + radius)
        )
        value_high, value_low = halves(value)
        result = jnp.dot(value_high, high, preferred_element_type=f32)
        result = result + jnp.dot(value_low, high, preferred_element_type=f32)
        result = result + jnp.dot(value_high, low, preferred_element_type=f32)
        spread[view] = result
        profile = jnp.zeros((1, depth), f32)
        place = iota((1, depth), 1)
        for tap in range(psf.shape[2]):
            source = place - tap + radius
            profile = profile + jnp.where(
                (source >= 0) & (source < depth), psf[view, 2, tap], f32(0)
            )
        profiles.append(profile)
    shares = [
        1.0 / jnp.maximum(counts[first + view, edge : edge + block_y], 1.0)
        for view in range(views)
    ]
    for view in range(views):
        counts[first + view, edge : edge + block_y] = shares[view]
    shape = (block_y, depth)
    for x in range(block_x):
        summed = None
        for view in range(all_views):
            term = jnp.broadcast_to(spread[view, :, x : x + 1], shape) * profiles[view]
            summed = term if summed is None else summed + term
        inverse_norm[x] = 1.0 / (summed + damping)
        at = edge + x
        for view in range(views):
            scale[view, x] = jnp.broadcast_to(
                counts[first + view, edge : edge + block_y, at : at + 1], shape
            )


class Route:
    def __init__(self, tx_near, tx_far, rx_near, rx_far, sems):
        self.me = lax.axis_index("gx")
        low = self.me < 2
        self.inside = lax.rem(self.me, 2)
        self.beside = jnp.where(self.inside == 0, self.me + 1, self.me - 1)
        self.gate = jnp.where(low, 2, 1)
        self.is_gate = jnp.logical_or(self.me == 1, self.me == 2)
        self.tx_near, self.tx_far, self.rx_near, self.rx_far = tx_near, tx_far, rx_near, rx_far
        self.near_send, self.near_recv, self.far_send, self.far_recv, self.on_send = sems
        self.pieces = ((0, 4), (4, 4), (8, tx_far.shape[1] - 8))

    def near(self, view):
        return pltpu.make_async_remote_copy(
            src_ref=self.tx_near.at[view],
            dst_ref=self.rx_near[view],
            send_sem=self.near_send.at[view],
            recv_sem=self.near_recv.at[view],
            device_id={"gx": self.beside},
            device_id_type=MESH,
        )

    def far(self, view, piece, side):
        span = pl.ds(*self.pieces[piece])
        return pltpu.make_async_remote_copy(
            src_ref=self.tx_far.at[view, span],
            dst_ref=self.rx_far[view].at[side, span],
            send_sem=self.far_send.at[view, piece],
            recv_sem=self.far_recv.at[view, side, piece],
            device_id={"gx": self.gate},
            device_id_type=MESH,
        )

    def onward(self, view, piece, side):
        span = pl.ds(*self.pieces[piece])
        return pltpu.make_async_remote_copy(
            src_ref=self.rx_far[view].at[side, span],
            dst_ref=self.rx_far[view].at[side, span],
            send_sem=self.on_send.at[view, side, piece],
            recv_sem=self.far_recv.at[view, side, piece],
            device_id={"gx": self.beside},
            device_id_type=MESH,
        )

    def send(self, view, tiles, pack):
        for piece, (start, size) in enumerate(self.pieces):
            for at in range(start, start + size):
                self.tx_far[view, at] = tiles[view, 0, pack[view, PAIR_SLOTS + at]]
            self.far(view, piece, self.inside).start()
        for at in range(PAIR_SLOTS):
            self.tx_near[view, at] = tiles[view, 0, pack[view, at]]
        self.near(view).start()

    def receive(self, view):
        @pl.when(self.is_gate)
        def _():
            for piece in range(2):
                for side in range(2):
                    self.far(view, piece, side).wait_recv()
                    self.onward(view, piece, side).start()

            for side in range(2):
                self.far(view, 2, side).wait_recv()

        @pl.when(jnp.logical_not(self.is_gate))
        def _():
            for piece in range(2):
                for side in range(2):
                    self.onward(view, piece, side).wait_recv()

        self.near(view).wait_recv()

    def drain(self, views):
        for view in range(views):
            for piece in range(3):
                self.far(view, piece, self.inside).wait_send()
            self.near(view).wait_send()

        @pl.when(self.is_gate)
        def _():
            for view in range(views):
                for piece in range(2):
                    for side in range(2):
                        self.onward(view, piece, side).wait_send()


def place_view(view, tile_shape, groups, slot, entry_x, entry_y, scale, per_blur, back_z, observed, spread, below):
    block_x, block_y, depth = observed.shape[1:]
    bf16 = jnp.bfloat16
    f32 = jnp.float32
    tile_wide, tile_tall = tile_shape
    entries = len(groups) * PAIR_SLOTS
    lane = iota((8, entries * tile_tall), 1)
    target = jnp.zeros(lane.shape, jnp.int32)
    for entry in range(entries):
        inside = (lane >= entry * tile_tall) & (lane < (entry + 1) * tile_tall)
        target = jnp.where(inside, entry_y[view, entry] + lane - entry * tile_tall, target)
    target = target[:1]
    chooser = jnp.where(iota((block_y, target.shape[1]), 0) == target, f32(1), f32(0)).astype(bf16)

    @pl.loop(0, block_x // 2)
    def _(step):
        columns = []
        for side in range(2):
            x = 2 * step + side
            rows = []
            for entry in range(entries):
                offset = x - entry_x[view, entry]
                inside = (offset >= 0) & (offset < tile_wide)
                read = groups[entry // PAIR_SLOTS]
                row = read(slot[view, entry], jnp.clip(offset, 0, tile_wide - 1))
                rows.append(jnp.where(inside, row, jnp.zeros_like(row)))
            columns.append(jnp.concatenate(rows, axis=0))
        both = jnp.concatenate(columns, axis=1)
        summed = jnp.dot(chooser, both, preferred_element_type=f32)
        quotients = []
        for side in range(2):
            x = 2 * step + side
            plane = summed[:, side * depth : (side + 1) * depth]
            observed[view, x] = plane * scale[view, x]
            quotients.append((plane * per_blur[view, x]).astype(bf16))
        stacked = jnp.concatenate(quotients, axis=0)
        stacked = jnp.concatenate([stacked, stacked], axis=1)
        result = jnp.dot(stacked, back_z[view], preferred_element_type=f32)
        for side in range(2):
            spread[view, below + 2 * step + side] = result[side * block_y : (side + 1) * block_y]


def routed_kernel(sizes, *refs):
    (
        psf,
        pack,
        slot,
        entry_x,
        entry_y,
        tiles,
        block,
        xs,
        ys,
        initial,
        estimate,
        fullest,
        start_center,
        start_low,
        start_high,
        start_send_low,
        start_send_high,
        start_send,
        start_recv,
        center,
        low,
        high,
        send_low,
        send_high,
        passed_y,
        passed_z,
        acc,
        acc_y,
        out_x,
        out_y,
        in_x,
        in_y,
        far_x,
        far_y,
        vert_in,
        est_send,
        est_recv,
        acc_send,
        acc_recv,
        vert_send,
        vert_recv,
        far_send,
        far_recv,
        taps_x,
        along_y,
        back_y,
        back_one,
        along_z,
        back_z,
        counts,
        norm_spread,
        inverse_norm,
        scale,
        per_blur,
        observed,
        fill_mine,
        fill_other,
        fill_send,
        fill_recv,
        tx_near,
        tx_far,
        *rest,
    ) = refs
    views, block_x, block_y, depth = observed.shape
    rx_near, rx_far, route_sems = rest[:views], rest[views : 2 * views], rest[2 * views :]
    tap_count = psf.shape[2]
    radius = tap_count // 2
    planes = center.shape[1]
    per_device = tiles.shape[2]
    tile_shape = tiles.shape[3:5]
    bf16 = jnp.bfloat16
    f32 = jnp.float32
    links = Links(sizes, radius, block_x)
    column = lax.axis_index("gx")
    first_view = lax.axis_index("vert") * views
    partner = {"vert": 1 - lax.axis_index("vert")}
    part_count = lax.axis_size("groups")
    parts = [
        {"groups": lax.rem(lax.axis_index("groups") + step, part_count)}
        for step in range(1, part_count)
    ]
    route = Route(tx_near, tx_far, rx_near, rx_far, route_sems)

    barrier = pltpu.get_barrier_semaphore()
    others = [partner] + parts
    others += [{"gx": lax.rem(column + step, sizes[0])} for step in range(1, sizes[0])]
    for other in others:
        pl.semaphore_signal(barrier, inc=1, device_id=other, device_id_type=MESH)
    peers = len(others)
    for dx, dy in links.directions:
        if dy == 0:
            continue
        peers = peers + links.exists(dx, dy).astype(jnp.int32)

        @pl.when(links.exists(dx, dy))
        def _():
            pl.semaphore_signal(
                barrier, inc=1, device_id=links.device(dx, dy), device_id_type=MESH
            )

    @pl.loop(0, block_x)
    def _(x):
        publish(links, start_center, start_send_low, start_send_high, x, initial[x])

    clear_missing(links, start_center, start_low, start_high)
    pl.semaphore_wait(barrier, peers)
    start = (
        ghosts_of_estimate(
            links, start_center, start_low, start_high, start_send_low, start_send_high
        ),
        start_send,
        start_recv,
    )
    links.start(*start, links.directions)
    for view in range(views):
        route.send(view, tiles, pack)

    number = iota(block.shape[1:], 1)
    most = jnp.zeros((block.shape[1], 1), f32)
    for view in range(block.shape[0]):
        beyond = (block[view] >= sizes[0] // 2) != (number >= block.shape[2] // 2)
        for source in range(sizes[0]):
            within = (number >= source * per_device) & (number < (source + 1) * per_device)
            count = jnp.sum(jnp.where(beyond & within, f32(1), f32(0)), axis=1, keepdims=True)
            most = jnp.maximum(most, count)
    fill_mine[...] = jnp.broadcast_to(jnp.max(most, axis=0, keepdims=True), fill_mine.shape)
    fills = [
        pltpu.make_async_remote_copy(
            src_ref=fill_mine,
            dst_ref=fill_other.at[index],
            send_sem=fill_send.at[index],
            recv_sem=fill_recv.at[index],
            device_id=other,
            device_id_type=MESH,
        )
        for index, other in enumerate(parts)
    ]
    for fill in fills:
        fill.start()

    make_bands(psf, first_view, radius, block_y, along_y, back_y, back_one, along_z, back_z)
    for view in range(views):
        for tap in range(tap_count):
            taps_x[view, tap] = psf[first_view + view, 0, tap]
    for sweep in range(ITERS):
        if sweep > 0:
            at = sweep - 1
            clear_missing(links, center.at[at], low.at[at], high.at[at])
        for step in (-1, 1):
            side = 0 if step == -1 else 1

            @pl.when(jnp.logical_not(links.exists(step, 0)))
            def _():
                in_x[sweep, side] = jnp.zeros(in_x.shape[2:], bf16)
                for other in range(2):
                    in_y[sweep, other, links.ghost(step)] = jnp.zeros(
                        (radius,) + in_y.shape[3:], bf16
                    )

            @pl.when(jnp.logical_not(links.exists(0, step)))
            def _():
                in_y[sweep, side] = jnp.zeros(in_y.shape[2:], bf16)

    below = 2 * radius
    beyond = passed_z.shape[1] - below - block_x
    passed_z[:, :below] = jnp.zeros((views, below, block_y, depth), f32)
    passed_z[:, below + block_x :] = jnp.zeros((views, beyond, block_y, depth), f32)
    group = group_of(block_x)

    make_norm(
        psf,
        first_view,
        radius,
        tile_shape,
        block,
        xs,
        ys,
        counts,
        norm_spread,
        inverse_norm,
        scale,
    )
    links.finish(*start, links.directions)
    pass_along_y(start_center, start_low, start_high, along_y, passed_y, views)

    @pl.loop(0, block_x // group)
    def _(step):
        first = step * group
        for view in range(views):
            blurred = pass_along_xz(taps_x, passed_y, along_z[view], view, first, group)
            blurred = blurred.reshape(group, block_y, depth)
            chunk = pl.ds(first, group)
            per_blur[view, chunk] = scale[view, chunk] / (blurred + soft_floor)

    for fill in fills:
        fill.wait()
    greatest = fill_mine[...]
    for index in range(len(fills)):
        greatest = jnp.maximum(greatest, fill_other[index])
    fullest[...] = greatest

    def vert_copy(sweep, start, size):
        chunk = pl.ds(start, size)
        return pltpu.make_async_remote_copy(
            src_ref=acc.at[sweep, chunk],
            dst_ref=vert_in.at[sweep, chunk],
            send_sem=vert_send.at[sweep],
            recv_sem=vert_recv.at[sweep],
            device_id=partner,
            device_id_type=MESH,
        )

    first_chunk = radius // 4
    last_chunk = (radius + block_x - 1) // 4
    far_chunk = (radius + block_x) // 4
    edge_turns = planes // 4 - far_chunk + -(-radius // 4)
    rows = block_y + 2 * HALO_Y

    def adjoint(sweep, chosen, begins, ends, turn):
        step = lax.rem(turn + far_chunk, planes // 4)
        matrix = back_y[...] if len(chosen) == views else back_one[chosen[0]]
        for first in (4 * step, 4 * step + 2):
            columns = []
            for x in (first, first + 1):
                stack = []
                for view in chosen:
                    value = taps_x[view, 0] * passed_z[view, x + below]
                    for tap in range(1, tap_count):
                        value = value + taps_x[view, tap] * passed_z[view, x + below - tap]
                    stack.append(value.astype(bf16))
                columns.append(jnp.concatenate(stack, axis=0))
            both = jnp.concatenate(columns, axis=1)
            result = jnp.dot(matrix, both, preferred_element_type=f32)
            result = result[:rows] + result[rows:]
            for side in range(2):
                x = first + side
                lanes = slice(side * depth, (side + 1) * depth)
                middle, edges = result[:block_y, lanes], result[block_y:, lanes]
                if not begins:
                    middle = middle + acc[sweep, x]
                    edges = edges + acc_y[x]
                acc[sweep, x] = middle
                if ends:
                    out_y[sweep, 0, x] = edges[:HALO_Y].astype(bf16)
                    out_y[sweep, 1, x] = edges[HALO_Y:].astype(bf16)
                else:
                    acc_y[x] = edges

        if ends:

            @pl.when(jnp.logical_and(step >= first_chunk, step <= last_chunk))
            def _():
                vert_copy(sweep, 4 * step, 4).start()

    for sweep in range(ITERS):
        if sweep == 0:
            for view in range(views):
                route.receive(view)
                groups = [
                    lambda at, a: tiles[view, 0, at, a],
                    lambda at, a: rx_near[view][at, a],
                    lambda at, a: rx_far[view][0, at, a],
                    lambda at, a: rx_far[view][1, at, a],
                ]
                place_view(
                    view,
                    tile_shape,
                    groups,
                    slot,
                    entry_x,
                    entry_y,
                    scale,
                    per_blur,
                    back_z,
                    observed,
                    passed_z,
                    below,
                )
                if view + 1 < views:

                    @pl.loop(0, planes // 4)
                    def _(turn):
                        adjoint(sweep, (view,), view == 0, False, turn)

            chosen, begins = (views - 1,), views == 1
        else:
            at = sweep - 1
            pass_along_y(center.at[at], low.at[at], high.at[at], along_y, passed_y, views)

            @pl.loop(0, block_x // group)
            def _(step):
                first = step * group
                for view in range(views):
                    blurred = pass_along_xz(taps_x, passed_y, along_z[view], view, first, group)
                    measured = observed[view, pl.ds(first, group)].reshape(blurred.shape)
                    result = spread_quotient(measured, blurred, back_z[view])
                    passed_z[view, pl.ds(below + first, group)] = result.reshape(
                        group, block_y, depth
                    )

            chosen, begins = tuple(range(views)), True

        sums = (
            ghosts_of_sums(
                links, out_x.at[sweep], out_y.at[sweep], in_x.at[sweep], in_y.at[sweep]
            ),
            acc_send.at[sweep],
            acc_recv.at[sweep],
        )

        @pl.loop(0, edge_turns)
        def _(turn):
            adjoint(sweep, chosen, begins, True, turn)

        @pl.loop(0, radius)
        def _(x):
            out_x[sweep, 0, x] = acc[sweep, x].astype(bf16)
            out_x[sweep, 1, x] = acc[sweep, radius + block_x + x].astype(bf16)

        links.start(*sums, links.across_x())

        @pl.loop(edge_turns, planes // 4)
        def _(turn):
            adjoint(sweep, chosen, begins, True, turn)

        links.start(*sums, links.along_y_only())
        links.finish(*sums, links.across_x())
        links.finish(*sums, links.along_y_only())
        forwards = [
            pltpu.make_async_remote_copy(
                src_ref=near.at[sweep],
                dst_ref=far.at[sweep],
                send_sem=far_send.at[sweep, index],
                recv_sem=far_recv.at[sweep, index],
                device_id=partner,
                device_id_type=pl.DeviceIdType.MESH,
            )
            for index, (near, far) in enumerate(((in_x, far_x), (in_y, far_y)))
        ]
        for forward in forwards:
            forward.start()
        vert_copy(sweep, 4 * first_chunk, 4 * (last_chunk - first_chunk + 1)).wait()

        @pl.loop(0, block_x)
        def _(x):
            acc[sweep, radius + x] = acc[sweep, radius + x] + vert_in[sweep, radius + x]

        for forward in forwards:
            forward.wait()

        def beyond_y(side, plane):
            return in_y[sweep, side, plane].astype(f32) + far_y[sweep, side, plane].astype(f32)

        @pl.loop(0, radius)
        def _(x):
            for side, at, beside in ((0, radius + x, x), (1, block_x + x, radius + block_x + x)):
                plane = acc[sweep, at] + (
                    in_x[sweep, side, x].astype(f32) + far_x[sweep, side, x].astype(f32)
                )
                first = plane[:HALO_Y] + beyond_y(0, beside)
                last = plane[block_y - HALO_Y :] + beyond_y(1, beside)
                acc[sweep, at] = jnp.concatenate(
                    [first, plane[HALO_Y : block_y - HALO_Y], last], axis=0
                )

        def update(x):
            plane = acc[sweep, radius + x]
            first = plane[:HALO_Y] + beyond_y(0, radius + x)
            last = plane[block_y - HALO_Y :] + beyond_y(1, radius + x)
            combined = jnp.concatenate([first, plane[HALO_Y : block_y - HALO_Y], last], axis=0)
            before = initial[x] if sweep == 0 else estimate[x]
            after = before * (combined + damping) * inverse_norm[x]
            estimate[x] = after
            if sweep + 1 < ITERS:
                publish(
                    links, center.at[sweep], send_low.at[sweep], send_high.at[sweep], x, after
                )

        if sweep + 1 < ITERS:
            news = (
                ghosts_of_estimate(
                    links,
                    center.at[sweep],
                    low.at[sweep],
                    high.at[sweep],
                    send_low.at[sweep],
                    send_high.at[sweep],
                ),
                est_send.at[sweep],
                est_recv.at[sweep],
            )

            @pl.loop(0, radius)
            def _(x):
                update(x)
                update(block_x - radius + x)

            links.start(*news, links.across_x())

            @pl.loop(radius, block_x - radius)
            def _(x):
                update(x)

            links.start(*news, links.along_y_only())
            links.finish(*news, links.directions)
        else:

            @pl.loop(0, block_x)
            def _(x):
                update(x)

    route.drain(views)


def routed(tiles, tile_block, tile_x, tile_y, psf, initial):
    block_x, block_y, depth = initial.shape
    views, _, per_device = tiles.shape[:3]
    all_views, rows, tiles_row = tile_x.shape
    tile = tiles.shape[3:]
    radius = psf.shape[2] // 2
    planes = planes_of(block_x, radius)
    extended_x = block_x + 2 * radius
    wide = block_y + 2 * HALO_Y
    sizes = (lax.axis_size("gx"), lax.axis_size("gy"))
    part_count = lax.axis_size("groups")
    cap = far_slots(per_device)
    block = tile_block.reshape(tile_x.shape)
    tables = plan(views, per_device, block, tile_x, tile_y)
    vmem = pl.BlockSpec(memory_space=pltpu.VMEM)
    smem = pl.BlockSpec(memory_space=pltpu.SMEM)
    dma = pltpu.SemaphoreType.DMA
    bf16 = jnp.bfloat16
    f32 = jnp.float32
    repeats = ITERS - 1
    volume = (views, block_x, block_y, depth)
    return pl.pallas_call(
        functools.partial(routed_kernel, sizes),
        out_shape=[
            jax.ShapeDtypeStruct(initial.shape, f32),
            jax.ShapeDtypeStruct((8, 128), f32),
        ],
        in_specs=[smem] * 5 + [vmem] * 5,
        out_specs=[vmem] * 2,
        scratch_shapes=estimate_scratch(planes, block_x, block_y, depth)
        + [dma((8,)), dma((8,))]
        + [
            pltpu.VMEM((repeats,) + scratch.shape, scratch.dtype)
            for scratch in estimate_scratch(planes, block_x, block_y, depth)
        ]
        + [
            pltpu.VMEM((views, planes, block_y, depth), f32),
            pltpu.VMEM((views, planes + 2 * radius, block_y, depth), f32),
            pltpu.VMEM((ITERS, planes, block_y, depth), f32),
            pltpu.VMEM((planes, 2 * HALO_Y, depth), f32),
            pltpu.VMEM((ITERS, 2, radius, block_y, depth), bf16),
            pltpu.VMEM((ITERS, 2, planes, HALO_Y, depth), bf16),
            pltpu.VMEM((ITERS, 2, radius, block_y, depth), bf16),
            pltpu.VMEM((ITERS, 2, extended_x, HALO_Y, depth), bf16),
            pltpu.VMEM((ITERS, 2, radius, block_y, depth), bf16),
            pltpu.VMEM((ITERS, 2, extended_x, HALO_Y, depth), bf16),
            pltpu.VMEM((ITERS, planes, block_y, depth), f32),
            dma((repeats, 8)),
            dma((repeats, 8)),
            dma((ITERS, 8)),
            dma((ITERS, 8)),
            dma((ITERS,)),
            dma((ITERS,)),
            dma((ITERS, 2)),
            dma((ITERS, 2)),
            pltpu.SMEM((views, psf.shape[2]), f32),
            pltpu.VMEM((views * block_y, 2 * wide), bf16),
            pltpu.VMEM((2 * wide, views * block_y), bf16),
            pltpu.VMEM((views, 2 * wide, block_y), bf16),
            pltpu.VMEM((views, 2 * depth, depth), bf16),
            pltpu.VMEM((views, 2 * depth, depth), bf16),
            pltpu.VMEM((all_views, block_y + 16, block_x + 16), f32),
            pltpu.VMEM((all_views, block_y, block_x), f32),
            pltpu.VMEM(initial.shape, f32),
            pltpu.VMEM(volume, f32),
            pltpu.VMEM(volume, f32),
            pltpu.VMEM(volume, f32),
            pltpu.VMEM((8, 128), f32),
            pltpu.VMEM((part_count - 1, 8, 128), f32),
            dma((part_count - 1,)),
            dma((part_count - 1,)),
            pltpu.VMEM((views, PAIR_SLOTS) + tile, bf16),
            pltpu.VMEM((views, cap) + tile, bf16),
        ]
        + [pltpu.VMEM((PAIR_SLOTS,) + tile, bf16)] * views
        + [pltpu.VMEM((2, cap) + tile, bf16)] * views
        + [dma((views,)), dma((views,)), dma((views, 3)), dma((views, 2, 3)), dma((views, 2, 2))],
        compiler_params=pltpu.CompilerParams(
            collective_id=2, has_side_effects=True, vmem_limit_bytes=56 << 20
        ),
    )(psf, *tables, tiles, block, tile_x, tile_y, initial)


def general(tiles, tile_block, tile_x, tile_y, psf, initial):
    column_count = lax.axis_size("gx")
    column_index = lax.axis_index("gx")
    row_index = lax.axis_index("gy")
    core_index = lax.axis_index("vert")
    local_views = tiles.shape[0]
    all_views = psf.shape[0]
    per_device = tiles.shape[2]
    tile_wide = tiles.shape[3]
    tile_tall = tiles.shape[4]
    block_x, block_y, depth = initial.shape
    capacity = max(2, 2 * per_device // column_count)
    radius = psf.shape[2] // 2
    first_view = core_index * local_views
    mine_psf = lax.dynamic_slice_in_dim(psf, first_view, local_views, 0)

    def my_rows(table):
        chosen = lax.dynamic_slice_in_dim(table, first_view, local_views, 0)
        chosen = lax.dynamic_slice_in_dim(chosen, row_index, 1, 1)[:, 0]
        return chosen.reshape(local_views, column_count, per_device)

    targets = my_rows(tile_block[:, :, :, 0])
    offsets_x = my_rows(tile_x)
    offsets_y = my_rows(tile_y)
    columns_iota = jnp.arange(column_count, dtype=jnp.int32)
    hits = (targets[..., None] == columns_iota).astype(jnp.int32)
    ranks = jnp.cumsum(hits, axis=2, dtype=jnp.int32)
    slot_ids = jnp.arange(capacity, dtype=jnp.int32) + 1
    sent_hits = jnp.swapaxes(lax.dynamic_slice_in_dim(hits, column_index, 1, 1)[:, 0], 1, 2)
    sent_ranks = jnp.swapaxes(lax.dynamic_slice_in_dim(ranks, column_index, 1, 1)[:, 0], 1, 2)
    chooser = sent_hits[:, :, None, :] * (
        sent_ranks[:, :, None, :] == slot_ids[None, None, :, None]
    ).astype(jnp.int32)
    outgoing = jnp.einsum(
        "vgkj,vjabz->gvkabz",
        chooser.astype(jnp.bfloat16),
        tiles[:, 0],
        preferred_element_type=jnp.bfloat16,
    )
    sizes = (column_count, lax.axis_size("gy"))
    halos = first_halos(sizes, radius, initial)
    outgoing, halos = lax.optimization_barrier((outgoing, halos))
    arrived = lax.all_to_all(outgoing, "gx", split_axis=0, concat_axis=0, tiled=True)
    from_hits = lax.dynamic_slice_in_dim(hits, column_index, 1, 3)[..., 0]
    from_ranks = lax.dynamic_slice_in_dim(ranks, column_index, 1, 3)[..., 0]
    picks = from_hits[:, :, None, :] * (
        from_ranks[:, :, None, :] == slot_ids[None, None, :, None]
    ).astype(jnp.int32)
    filled = jnp.sum(picks, axis=3).reshape(local_views, -1)
    corner_x = jnp.sum(picks * offsets_x[:, :, None, :], axis=3).reshape(local_views, -1)
    corner_y = jnp.sum(picks * offsets_y[:, :, None, :], axis=3).reshape(local_views, -1)

    row_iota = jnp.arange(tile_block.shape[1], dtype=jnp.int32)
    global_x = (tile_block[..., 0] * block_x + tile_x).reshape(all_views, -1)
    global_y = (row_iota[None, :, None] * block_y + tile_y).reshape(all_views, -1)
    near_x = jnp.arange(block_x + 2 * radius, dtype=jnp.int32) - radius
    near_y = jnp.arange(block_y + 2 * radius, dtype=jnp.int32) - radius
    cells_x = column_index * block_x + near_x
    cells_y = row_index * block_y + near_y
    cover_x = (
        (cells_x >= global_x[..., None]) & (cells_x < global_x[..., None] + tile_wide)
    ).astype(jnp.bfloat16)
    cover_y = (
        (cells_y >= global_y[..., None]) & (cells_y < global_y[..., None] + tile_tall)
    ).astype(jnp.bfloat16)
    counts = jnp.einsum("vti,vtj->vij", cover_x, cover_y, preferred_element_type=jnp.float32)
    coverage = jnp.minimum(counts, 1.0)
    iota_x = jnp.arange(block_x, dtype=jnp.int32)
    iota_y = jnp.arange(block_y, dtype=jnp.int32)
    iota_z = jnp.arange(depth, dtype=jnp.int32)
    adjoint_x = banded(psf[:, 0], iota_x[:, None] - near_x[None, :] + radius)
    adjoint_y = banded(psf[:, 1], iota_y[:, None] - near_y[None, :] + radius)
    exact = lax.Precision.HIGHEST
    spread = jnp.einsum("vij,vyj->viy", coverage, adjoint_y, precision=exact)
    spread = jnp.einsum("vxi,viy->vxy", adjoint_x, spread, precision=exact)
    profile = jnp.sum(banded(psf[:, 2], iota_z[:, None] - iota_z[None, :] + radius), axis=2)
    norm_field = jnp.einsum("vxy,vz->xyz", spread, profile, precision=exact)
    inverse_norm = 1.0 / (norm_field + damping)

    places_y = jnp.concatenate(
        [
            iota_y,
            jnp.arange(HALO_Y, dtype=jnp.int32) - HALO_Y,
            jnp.arange(HALO_Y, dtype=jnp.int32) + block_y,
        ]
    )
    band_y = banded(mine_psf[:, 1], places_y[None, :] - iota_y[:, None] + radius)
    high, low = split_high_low(band_y)
    flat = (local_views * block_y, places_y.shape[0])
    along_y = jnp.concatenate([high.reshape(flat), low.reshape(flat)], axis=1)
    back_y = jnp.concatenate([high.reshape(flat).T, low.reshape(flat).T], axis=0)
    band_z = banded(mine_psf[:, 2], iota_z[:, None] - iota_z[None, :] + radius)
    along_z = jnp.concatenate(split_high_low(band_z), axis=1)
    back_z = jnp.concatenate(split_high_low(jnp.swapaxes(band_z, 1, 2)), axis=1)
    taps_x = mine_psf[:, 0]
    blurred = first_blur(taps_x, halos, along_y, along_z, block_x)
    observed, spreads = place(filled, corner_x, corner_y, arrived, blurred, back_z, radius)
    return sweeps(
        sizes,
        taps_x,
        observed,
        spreads,
        initial,
        inverse_norm,
        along_y,
        back_y,
        along_z,
        back_z,
    )


def shards(tiles, tile_block, tile_x, tile_y, psf, initial):
    arguments = (tiles, tile_block, tile_x, tile_y, psf, initial)
    if lax.axis_size("gx") != 4:
        return general(*arguments)
    estimate, fullest = routed(*arguments)
    return lax.cond(
        fullest[0, 0] > far_slots(tiles.shape[2]),
        lambda result, *rest: general(*rest),
        lambda result, *rest: result,
        estimate,
        *arguments,
    )


def solution(mesh):
    in_specs = (
        P("vert", "gy", ("groups", "gx"), None, None, None),
        P(None, None, "groups", None),
        P(None, None, "groups"),
        P(None, None, "groups"),
        P(),
        P(("groups", "gx"), "gy", None),
    )
    out_specs = P(("groups", "gx"), "gy", None)
    return jax.shard_map(shards, mesh=mesh, in_specs=in_specs, out_specs=out_specs, check_vma=False)
```

```python
import functools

import jax
import jax.numpy as jnp
from jax import lax
from jax.experimental import pallas as pl
from jax.experimental.pallas import tpu as pltpu
from jax.sharding import PartitionSpec as P

ITERS = 2
HALO_Y = 8

soft_floor = 0.01
damping = 0.5


def split_high_low(matrix):
    high = lax.reduce_precision(matrix, 8, 7)
    return high.astype(jnp.bfloat16), (matrix - high).astype(jnp.bfloat16)


def banded(taps, difference):
    summed = None
    for tap_index in range(taps.shape[-1]):
        term = jnp.where(difference == tap_index, taps[..., tap_index, None, None], 0.0)
        summed = term if summed is None else summed + term
    return summed


class Links:
    def __init__(self, sizes, radius, block_x):
        self.radius = radius
        self.block_x = block_x
        self.me = (lax.axis_index("gx"), lax.axis_index("gy"))
        self.sizes = sizes
        self.directions = [
            (dx, dy) for dx in (-1, 0, 1) for dy in (-1, 0, 1) if (dx, dy) != (0, 0)
        ]

    def exists(self, dx, dy):
        good = None
        for step, me, count in zip((dx, dy), self.me, self.sizes):
            if step == 0:
                continue
            test = me > 0 if step == -1 else me < count - 1
            good = test if good is None else jnp.logical_and(good, test)
        return good

    def device(self, dx, dy):
        return {"gx": self.me[0] + dx, "gy": self.me[1] + dy}

    def greet(self, others=()):
        barrier = pltpu.get_barrier_semaphore()
        for dx, dy in self.directions:

            @pl.when(self.exists(dx, dy))
            def _():
                pl.semaphore_signal(
                    barrier,
                    inc=1,
                    device_id=self.device(dx, dy),
                    device_id_type=pl.DeviceIdType.MESH,
                )

        for other in others:
            pl.semaphore_signal(
                barrier, inc=1, device_id=other, device_id_type=pl.DeviceIdType.MESH
            )

    def await_greetings(self, others=0):
        peers = others
        for dx, dy in self.directions:
            peers = peers + self.exists(dx, dy).astype(jnp.int32)
        pl.semaphore_wait(pltpu.get_barrier_semaphore(), peers)

    def span(self, step):
        if step == 0:
            return pl.ds(self.radius, self.block_x)
        return pl.ds(self.radius if step == -1 else self.block_x, self.radius)

    def ghost(self, step):
        if step == 0:
            return pl.ds(self.radius, self.block_x)
        return pl.ds(0 if step == -1 else self.block_x + self.radius, self.radius)

    def part(self, step):
        if step == 0:
            return pl.ds(0, self.block_x)
        return pl.ds(0 if step == -1 else self.block_x - self.radius, self.radius)

    def exchange(self, make, send_sem, recv_sem):
        self.start(make, send_sem, recv_sem, self.directions)
        self.finish(make, send_sem, recv_sem, self.directions)

    def across_x(self):
        return [one for one in self.directions if one[0] != 0]

    def along_y_only(self):
        return [one for one in self.directions if one[0] == 0]

    def copy(self, make, send_sem, recv_sem, dx, dy):
        index = self.directions.index((dx, dy))
        src, dst = make(dx, dy)
        return pltpu.make_async_remote_copy(
            src_ref=src,
            dst_ref=dst,
            send_sem=send_sem.at[index],
            recv_sem=recv_sem.at[index],
            device_id=self.device(dx, dy),
            device_id_type=pl.DeviceIdType.MESH,
        )

    def start(self, make, send_sem, recv_sem, directions):
        for dx, dy in directions:

            @pl.when(self.exists(dx, dy))
            def _():
                self.copy(make, send_sem, recv_sem, dx, dy).start()

    def finish(self, make, send_sem, recv_sem, directions):
        for dx, dy in directions:

            @pl.when(self.exists(dx, dy))
            def _():
                self.copy(make, send_sem, recv_sem, dx, dy).wait_send()

            @pl.when(self.exists(-dx, -dy))
            def _():
                self.copy(make, send_sem, recv_sem, dx, dy).wait_recv()


def ghosts_of_estimate(links, center, low, high, send_low, send_high):
    def make(dx, dy):
        if dy == 0:
            return center.at[links.span(dx)], center.at[links.ghost(-dx)]
        if dy == -1:
            return send_low.at[links.part(dx)], high.at[links.ghost(-dx)]
        return send_high.at[links.part(dx)], low.at[links.ghost(-dx)]

    return make


def ghosts_of_sums(links, out_x, out_y, in_x, in_y):
    def make(dx, dy):
        if dy == 0:
            side = 0 if dx == -1 else 1
            return out_x.at[side], in_x.at[1 - side]
        side = 0 if dy == -1 else 1
        return out_y.at[side, links.ghost(dx)], in_y.at[1 - side, links.ghost(-dx)]

    return make


def clear_missing(links, center, low, high):
    radius = links.radius
    for step in (-1, 1):

        @pl.when(jnp.logical_not(links.exists(step, 0)))
        def _():
            for rows in (center, low, high):
                rows[links.ghost(step)] = jnp.zeros((radius,) + rows.shape[1:], rows.dtype)

        @pl.when(jnp.logical_not(links.exists(0, step)))
        def _():
            rows = low if step == -1 else high
            rows[...] = jnp.zeros(rows.shape, rows.dtype)

    tail = links.block_x + 2 * radius
    for rows in (center, low, high):
        rows[tail:] = jnp.zeros((rows.shape[0] - tail,) + rows.shape[1:], rows.dtype)


def publish(links, center, send_low, send_high, x, plane):
    center[links.radius + x] = plane.astype(jnp.bfloat16)
    send_low[x] = plane[:HALO_Y].astype(jnp.bfloat16)
    send_high[x] = plane[plane.shape[0] - HALO_Y :].astype(jnp.bfloat16)


def pass_along_y(center, low, high, along_y, passed_y, views):
    block_y, depth = center.shape[1:]

    @pl.loop(0, center.shape[0] // 4)
    def _(step):
        for first in (4 * step, 4 * step + 2):
            columns = []
            for x in (first, first + 1):
                edges = jnp.concatenate(
                    [low[x].astype(jnp.float32), high[x].astype(jnp.float32)], axis=0
                ).astype(jnp.bfloat16)
                columns.append(jnp.concatenate([center[x], edges], axis=0))
            both = jnp.concatenate(columns, axis=1)
            both = jnp.concatenate([both, both], axis=0)
            result = jnp.dot(along_y[...], both, preferred_element_type=jnp.float32)
            for view in range(views):
                rows = slice(view * block_y, (view + 1) * block_y)
                passed_y[view, first] = result[rows, :depth]
                passed_y[view, first + 1] = result[rows, depth:]


def pass_along_xz(taps_x, passed_y, along_z, view, first, group):
    planes = []
    for inner in range(group):
        x = first + inner
        value = taps_x[view, 0] * passed_y[view, x]
        for tap in range(1, taps_x.shape[1]):
            value = value + taps_x[view, tap] * passed_y[view, x + tap]
        planes.append(value.astype(jnp.bfloat16))
    stacked = jnp.concatenate(planes, axis=0)
    stacked = jnp.concatenate([stacked, stacked], axis=1)
    return jnp.dot(stacked, along_z, preferred_element_type=jnp.float32)


def spread_quotient(measured, blurred, back_z):
    quotient = (measured / (blurred + soft_floor)).astype(jnp.bfloat16)
    quotient = jnp.concatenate([quotient, quotient], axis=1)
    return jnp.dot(quotient, back_z, preferred_element_type=jnp.float32)


def group_of(block_x):
    group = 4
    while block_x % group:
        group //= 2
    return group


def halo_kernel(
    sizes, radius, initial, center, low, high, all_center, all_low, all_high, *scratch
):
    send_low, send_high, send_sem, recv_sem = scratch
    block_x = initial.shape[0]
    links = Links(sizes, radius, block_x)
    links.greet()

    @pl.loop(0, block_x)
    def _(x):
        publish(links, all_center, send_low, send_high, x, initial[x])

    clear_missing(links, all_center, all_low, all_high)
    links.await_greetings()
    links.exchange(
        ghosts_of_estimate(links, all_center, all_low, all_high, send_low, send_high),
        send_sem,
        recv_sem,
    )

    @pl.loop(0, center.shape[0])
    def _(x):
        center[x] = all_center[x]
        low[x] = all_low[x]
        high[x] = all_high[x]


def blur_kernel(taps_x, center, low, high, along_y, along_z, blurred, passed_y):
    views, block_x, block_y, depth = blurred.shape
    pass_along_y(center, low, high, along_y, passed_y, views)
    group = group_of(block_x)

    @pl.loop(0, block_x // group)
    def _(step):
        for view in range(views):
            value = pass_along_xz(taps_x, passed_y, along_z[view], view, step * group, group)
            blurred[view, pl.ds(step * group, group)] = value.reshape(group, block_y, depth)


def estimate_scratch(planes, block_x, block_y, depth):
    return [
        pltpu.VMEM((planes, block_y, depth), jnp.bfloat16),
        pltpu.VMEM((planes, HALO_Y, depth), jnp.bfloat16),
        pltpu.VMEM((planes, HALO_Y, depth), jnp.bfloat16),
        pltpu.VMEM((block_x, HALO_Y, depth), jnp.bfloat16),
        pltpu.VMEM((block_x, HALO_Y, depth), jnp.bfloat16),
    ]


def planes_of(block_x, radius):
    return -(-(block_x + 2 * radius) // 4) * 4


def first_halos(sizes, radius, initial):
    block_x, block_y, depth = initial.shape
    vmem = pl.BlockSpec(memory_space=pltpu.VMEM)
    scratch = estimate_scratch(planes_of(block_x, radius), block_x, block_y, depth)
    return pl.pallas_call(
        functools.partial(halo_kernel, sizes, radius),
        out_shape=[jax.ShapeDtypeStruct(one.shape, one.dtype) for one in scratch[:3]],
        in_specs=[vmem],
        out_specs=[vmem] * 3,
        scratch_shapes=scratch
        + [pltpu.SemaphoreType.DMA((8,)), pltpu.SemaphoreType.DMA((8,))],
        compiler_params=pltpu.CompilerParams(
            collective_id=0, has_side_effects=True, vmem_limit_bytes=12 << 20
        ),
    )(initial)


def first_blur(taps_x, halos, along_y, along_z, block_x):
    planes, block_y, depth = halos[0].shape
    views = taps_x.shape[0]
    vmem = pl.BlockSpec(memory_space=pltpu.VMEM)
    shape = (views, block_x, block_y, depth)
    return pl.pallas_call(
        blur_kernel,
        out_shape=jax.ShapeDtypeStruct(shape, jnp.float32),
        in_specs=[pl.BlockSpec(memory_space=pltpu.SMEM)] + [vmem] * 5,
        out_specs=vmem,
        scratch_shapes=[pltpu.VMEM((views, planes, block_y, depth), jnp.float32)],
        cost_estimate=pl.CostEstimate(
            flops=10_000_000_000, bytes_accessed=40_000_000, transcendentals=0
        ),
        compiler_params=pltpu.CompilerParams(vmem_limit_bytes=20 << 20),
    )(taps_x, *halos, along_y, along_z)


def place_kernel(
    below, filled, corner_x, corner_y, tiles, blurred, back_z, observed, spread, summed, counted
):
    view = pl.program_id(0)
    sources, _, capacity, wide, tall, depth = tiles.shape
    _, block_x, block_y, _ = observed.shape
    summed[...] = jnp.zeros_like(summed)
    counted[...] = jnp.zeros_like(counted)

    @pl.loop(0, sources)
    def _(source):
        @pl.loop(0, capacity)
        def _(slot):
            at = source * capacity + slot

            @pl.when(filled[view, at] > 0)
            def _():
                x = corner_x[view, at]
                y = corner_y[view, at]
                where = (pl.ds(x, wide), pl.ds(y, tall), slice(None))
                summed[where] = summed[where] + tiles[source, 0, slot].astype(jnp.float32)
                counted[where] = counted[where] + 1.0

    group = group_of(block_x)
    beyond = spread.shape[1] - below - block_x
    spread[0, :below] = jnp.zeros((below, block_y, depth), jnp.float32)
    spread[0, below + block_x :] = jnp.zeros((beyond, block_y, depth), jnp.float32)

    @pl.loop(0, block_x // group)
    def _(step):
        planes = pl.ds(step * group, group)
        measured = summed[planes] / jnp.maximum(counted[planes], 1.0)
        observed[0, planes] = measured
        flat = (group * block_y, depth)
        result = spread_quotient(
            measured.reshape(flat), blurred[0, planes].reshape(flat), back_z[0]
        )
        spread[0, pl.ds(below + step * group, group)] = result.reshape(group, block_y, depth)


def place(filled, corner_x, corner_y, arrived, blurred, back_z, radius):
    sources, views, capacity, wide, tall, depth = arrived.shape
    shape = blurred.shape
    volume = pl.BlockSpec((1,) + shape[1:], lambda v, *_: (v, 0, 0, 0))
    padded = (views, planes_of(shape[1], radius) + 2 * radius) + shape[2:]
    return pl.pallas_call(
        functools.partial(place_kernel, 2 * radius),
        out_shape=[
            jax.ShapeDtypeStruct(shape, jnp.float32),
            jax.ShapeDtypeStruct(padded, jnp.float32),
        ],
        grid_spec=pltpu.PrefetchScalarGridSpec(
            num_scalar_prefetch=3,
            grid=(views,),
            in_specs=[
                pl.BlockSpec(
                    (sources, 1, capacity, wide, tall, depth), lambda v, *_: (0, v, 0, 0, 0, 0)
                ),
                volume,
                pl.BlockSpec((1,) + back_z.shape[1:], lambda v, *_: (v, 0, 0)),
            ],
            out_specs=[
                volume,
                pl.BlockSpec((1,) + padded[1:], lambda v, *_: (v, 0, 0, 0)),
            ],
            scratch_shapes=[pltpu.VMEM(shape[1:], jnp.float32)] * 2,
        ),
        compiler_params=pltpu.CompilerParams(vmem_limit_bytes=20 << 20),
    )(filled, corner_x, corner_y, arrived, blurred, back_z)


def sweep_kernel(sizes, *refs):
    (
        taps_x,
        observed,
        spreads,
        initial,
        inverse_norm,
        along_y,
        back_y,
        along_z,
        back_z,
        estimate,
        center,
        low,
        high,
        send_low,
        send_high,
        passed_y,
        passed_z,
        acc,
        out_x,
        out_y,
        in_x,
        in_y,
        far_x,
        far_y,
        vert_in,
        est_send,
        est_recv,
        acc_send,
        acc_recv,
        vert_send,
        vert_recv,
        far_send,
        far_recv,
    ) = refs
    views, block_x, block_y, depth = observed.shape
    tap_count = taps_x.shape[1]
    radius = tap_count // 2
    planes = center.shape[1]
    bf16 = jnp.bfloat16
    f32 = jnp.float32
    links = Links(sizes, radius, block_x)
    partner = {"vert": 1 - lax.axis_index("vert")}
    links.greet((partner,))
    for sweep in range(ITERS):
        if sweep > 0:
            at = sweep - 1
            clear_missing(links, center.at[at], low.at[at], high.at[at])
        for step in (-1, 1):
            side = 0 if step == -1 else 1

            @pl.when(jnp.logical_not(links.exists(step, 0)))
            def _():
                in_x[sweep, side] = jnp.zeros(in_x.shape[2:], bf16)
                for other in range(2):
                    in_y[sweep, other, links.ghost(step)] = jnp.zeros(
                        (radius,) + in_y.shape[3:], bf16
                    )

            @pl.when(jnp.logical_not(links.exists(0, step)))
            def _():
                in_y[sweep, side] = jnp.zeros(in_y.shape[2:], bf16)

    below = 2 * radius
    beyond = passed_z.shape[1] - below - block_x
    passed_z[:, :below] = jnp.zeros((views, below, block_y, depth), f32)
    passed_z[:, below + block_x :] = jnp.zeros((views, beyond, block_y, depth), f32)
    group = group_of(block_x)

    for sweep in range(ITERS):
        if sweep > 0:
            at = sweep - 1
            pass_along_y(center.at[at], low.at[at], high.at[at], along_y, passed_y, views)

            @pl.loop(0, block_x // group)
            def _(step):
                first = step * group
                for view in range(views):
                    blurred = pass_along_xz(taps_x, passed_y, along_z[view], view, first, group)
                    measured = observed[view, pl.ds(first, group)].reshape(blurred.shape)
                    result = spread_quotient(measured, blurred, back_z[view])
                    passed_z[view, pl.ds(below + first, group)] = result.reshape(
                        group, block_y, depth
                    )

        if sweep == 0:
            links.await_greetings(1)

        def vert(start, size):
            chunk = pl.ds(start, size)
            return pltpu.make_async_remote_copy(
                src_ref=acc.at[sweep, chunk],
                dst_ref=vert_in.at[sweep, chunk],
                send_sem=vert_send.at[sweep],
                recv_sem=vert_recv.at[sweep],
                device_id=partner,
                device_id_type=pl.DeviceIdType.MESH,
            )

        first_chunk = radius // 4
        last_chunk = (radius + block_x - 1) // 4

        source = spreads if sweep == 0 else passed_z
        far_chunk = (radius + block_x) // 4
        edge_turns = planes // 4 - far_chunk + -(-radius // 4)
        def adjoint(turn):
            step = lax.rem(turn + far_chunk, planes // 4)
            for first in (4 * step, 4 * step + 2):
                columns = []
                for x in (first, first + 1):
                    stack = []
                    for view in range(views):
                        value = taps_x[view, 0] * source[view, x + below]
                        for tap in range(1, tap_count):
                            value = value + taps_x[view, tap] * source[view, x + below - tap]
                        stack.append(value.astype(bf16))
                    columns.append(jnp.concatenate(stack, axis=0))
                both = jnp.concatenate(columns, axis=1)
                result = jnp.dot(back_y[...], both, preferred_element_type=f32)
                rows = block_y + 2 * HALO_Y
                result = result[:rows] + result[rows:]
                for side in range(2):
                    x = first + side
                    lanes = slice(side * depth, (side + 1) * depth)
                    acc[sweep, x] = result[:block_y, lanes]
                    out_y[sweep, 0, x] = result[block_y : block_y + HALO_Y, lanes].astype(bf16)
                    out_y[sweep, 1, x] = result[block_y + HALO_Y :, lanes].astype(bf16)

            @pl.when(jnp.logical_and(step >= first_chunk, step <= last_chunk))
            def _():
                vert(4 * step, 4).start()

        sums = (
            ghosts_of_sums(
                links, out_x.at[sweep], out_y.at[sweep], in_x.at[sweep], in_y.at[sweep]
            ),
            acc_send.at[sweep],
            acc_recv.at[sweep],
        )

        @pl.loop(0, edge_turns)
        def _(turn):
            adjoint(turn)

        @pl.loop(0, radius)
        def _(x):
            out_x[sweep, 0, x] = acc[sweep, x].astype(bf16)
            out_x[sweep, 1, x] = acc[sweep, radius + block_x + x].astype(bf16)

        links.start(*sums, links.across_x())

        @pl.loop(edge_turns, planes // 4)
        def _(turn):
            adjoint(turn)

        links.start(*sums, links.along_y_only())
        links.finish(*sums, links.across_x())
        links.finish(*sums, links.along_y_only())
        forwards = [
            pltpu.make_async_remote_copy(
                src_ref=near.at[sweep],
                dst_ref=far.at[sweep],
                send_sem=far_send.at[sweep, index],
                recv_sem=far_recv.at[sweep, index],
                device_id=partner,
                device_id_type=pl.DeviceIdType.MESH,
            )
            for index, (near, far) in enumerate(((in_x, far_x), (in_y, far_y)))
        ]
        for forward in forwards:
            forward.start()
        vert(4 * first_chunk, 4 * (last_chunk - first_chunk + 1)).wait()

        @pl.loop(0, block_x)
        def _(x):
            acc[sweep, radius + x] = acc[sweep, radius + x] + vert_in[sweep, radius + x]

        for forward in forwards:
            forward.wait()

        def beyond_y(side, plane):
            return in_y[sweep, side, plane].astype(f32) + far_y[sweep, side, plane].astype(f32)

        @pl.loop(0, radius)
        def _(x):
            for side, at, beside in ((0, radius + x, x), (1, block_x + x, radius + block_x + x)):
                plane = acc[sweep, at] + (
                    in_x[sweep, side, x].astype(f32) + far_x[sweep, side, x].astype(f32)
                )
                first = plane[:HALO_Y] + beyond_y(0, beside)
                last = plane[block_y - HALO_Y :] + beyond_y(1, beside)
                acc[sweep, at] = jnp.concatenate(
                    [first, plane[HALO_Y : block_y - HALO_Y], last], axis=0
                )

        def update(x):
            plane = acc[sweep, radius + x]
            first = plane[:HALO_Y] + beyond_y(0, radius + x)
            last = plane[block_y - HALO_Y :] + beyond_y(1, radius + x)
            combined = jnp.concatenate([first, plane[HALO_Y : block_y - HALO_Y], last], axis=0)
            before = initial[x] if sweep == 0 else estimate[x]
            after = before * (combined + damping) * inverse_norm[x]
            estimate[x] = after
            if sweep + 1 < ITERS:
                publish(
                    links, center.at[sweep], send_low.at[sweep], send_high.at[sweep], x, after
                )

        if sweep + 1 < ITERS:
            news = (
                ghosts_of_estimate(
                    links,
                    center.at[sweep],
                    low.at[sweep],
                    high.at[sweep],
                    send_low.at[sweep],
                    send_high.at[sweep],
                ),
                est_send.at[sweep],
                est_recv.at[sweep],
            )

            @pl.loop(0, radius)
            def _(x):
                update(x)
                update(block_x - radius + x)

            links.start(*news, links.across_x())

            @pl.loop(radius, block_x - radius)
            def _(x):
                update(x)

            links.start(*news, links.along_y_only())
            links.finish(*news, links.directions)
        else:

            @pl.loop(0, block_x)
            def _(x):
                update(x)


def sweeps(
    sizes, taps_x, observed, spreads, initial, inverse_norm, along_y, back_y, along_z, back_z
):
    block_x, block_y, depth = initial.shape
    views = observed.shape[0]
    radius = taps_x.shape[1] // 2
    planes = planes_of(block_x, radius)
    extended_x = block_x + 2 * radius
    vmem = pl.BlockSpec(memory_space=pltpu.VMEM)
    bf16 = jnp.bfloat16
    f32 = jnp.float32
    repeats = ITERS - 1
    return pl.pallas_call(
        functools.partial(sweep_kernel, sizes),
        out_shape=jax.ShapeDtypeStruct(initial.shape, f32),
        in_specs=[pl.BlockSpec(memory_space=pltpu.SMEM)] + [vmem] * 8,
        out_specs=vmem,
        scratch_shapes=[
            pltpu.VMEM((repeats,) + scratch.shape, scratch.dtype)
            for scratch in estimate_scratch(planes, block_x, block_y, depth)
        ]
        + [
            pltpu.VMEM((views, planes, block_y, depth), f32),
            pltpu.VMEM((views, planes + 2 * radius, block_y, depth), f32),
            pltpu.VMEM((ITERS, planes, block_y, depth), f32),
            pltpu.VMEM((ITERS, 2, radius, block_y, depth), bf16),
            pltpu.VMEM((ITERS, 2, planes, HALO_Y, depth), bf16),
            pltpu.VMEM((ITERS, 2, radius, block_y, depth), bf16),
            pltpu.VMEM((ITERS, 2, extended_x, HALO_Y, depth), bf16),
            pltpu.VMEM((ITERS, 2, radius, block_y, depth), bf16),
            pltpu.VMEM((ITERS, 2, extended_x, HALO_Y, depth), bf16),
            pltpu.VMEM((ITERS, planes, block_y, depth), f32),
            pltpu.SemaphoreType.DMA((repeats, 8)),
            pltpu.SemaphoreType.DMA((repeats, 8)),
            pltpu.SemaphoreType.DMA((ITERS, 8)),
            pltpu.SemaphoreType.DMA((ITERS, 8)),
            pltpu.SemaphoreType.DMA((ITERS,)),
            pltpu.SemaphoreType.DMA((ITERS,)),
            pltpu.SemaphoreType.DMA((ITERS, 2)),
            pltpu.SemaphoreType.DMA((ITERS, 2)),
        ],
        compiler_params=pltpu.CompilerParams(
            collective_id=1, has_side_effects=True, vmem_limit_bytes=40 << 20
        ),
    )(taps_x, observed, spreads, initial, inverse_norm, along_y, back_y, along_z, back_z)


PAIR_SLOTS = 8
ROW = 40
FAR_AWAY = -1000
MESH = pl.DeviceIdType.MESH


def far_slots(per_device):
    return 3 * per_device // 4


def plan_kernel(per_device, block, xs, ys, pack, slot, entry_x, entry_y):
    views = pack.shape[0]
    me = lax.axis_index("gx")
    row = lax.axis_index("gy")
    first = lax.axis_index("vert") * views
    in_low = me < 2
    beside = jnp.where(lax.rem(me, 2) == 0, me + 1, me - 1)
    far_base = jnp.where(in_low, 2, 0)
    far_outer = jnp.where(in_low, 3, 0)
    far_gate = jnp.where(in_low, 2, 1)
    my_outer = jnp.where(in_low, 0, 3)
    spare = 4 * PAIR_SLOTS
    one, zero = jnp.int32(1), jnp.int32(0)
    for view in range(views):
        for at in range(spare):
            pack[view, at] = zero
            slot[view, at] = zero
            entry_x[view, at] = zero
            entry_y[view, at] = jnp.int32(FAR_AWAY)

        def enter(at, where, column):
            slot[view, at] = where
            entry_x[view, at] = xs[first + view, row, column]
            entry_y[view, at] = ys[first + view, row, column]

        mine = near = outer = zero
        for j in range(per_device):
            column = me * per_device + j
            target = block[first + view, row, column]
            enter(jnp.where(target == me, mine, spare), jnp.int32(j), column)
            at = jnp.where(
                target == beside,
                near,
                jnp.where(target == far_outer, PAIR_SLOTS + outer, spare),
            )
            pack[view, at] = jnp.int32(j)
            mine = mine + jnp.where(target == me, one, zero)
            near = near + jnp.where(target == beside, one, zero)
            outer = outer + jnp.where(target == far_outer, one, zero)
        for j in range(per_device):
            target = block[first + view, row, me * per_device + j]
            pack[view, jnp.where(target == far_gate, PAIR_SLOTS + outer, spare)] = jnp.int32(j)
            outer = outer + jnp.where(target == far_gate, one, zero)
        found = zero
        for j in range(per_device):
            column = beside * per_device + j
            hit = block[first + view, row, column] == me
            enter(jnp.where(hit, PAIR_SLOTS + found, spare), found, column)
            found = found + jnp.where(hit, one, zero)
        for side in range(2):
            base = (2 + side) * PAIR_SLOTS
            found = ahead = zero
            for j in range(per_device):
                column = (far_base + side) * per_device + j
                target = block[first + view, row, column]
                hit = target == me
                enter(jnp.where(hit, base + found, spare), found, column)
                found = found + jnp.where(hit, one, zero)
                ahead = ahead + jnp.where(target == my_outer, one, zero)
            ahead = jnp.where(me == my_outer, zero, ahead)
            for at in range(base, base + PAIR_SLOTS):
                slot[view, at] = jnp.minimum(slot[view, at] + ahead, far_slots(per_device) - 1)


def plan(views, per_device, block, xs, ys):
    smem = pl.BlockSpec(memory_space=pltpu.SMEM)
    return pl.pallas_call(
        functools.partial(plan_kernel, per_device),
        out_shape=[jax.ShapeDtypeStruct((views, ROW), jnp.int32)] * 4,
        in_specs=[smem] * 3,
        out_specs=[smem] * 4,
    )(block, xs, ys)


def band_of(psf, view, dim, difference):
    summed = jnp.zeros(difference.shape, jnp.float32)
    for tap in range(psf.shape[2]):
        summed = jnp.where(difference == tap, psf[view, dim, tap], summed)
    return summed


def halves(value):
    high = value.astype(jnp.bfloat16)
    return high, (value - high.astype(jnp.float32)).astype(jnp.bfloat16)


def iota(shape, dim):
    return lax.broadcasted_iota(jnp.int32, shape, dim)


def make_bands(psf, first, radius, block_y, along_y, back_y, back_one, along_z, back_z):
    views = along_z.shape[0]
    depth = along_z.shape[2]
    wide = block_y + 2 * HALO_Y

    def place_of(index):
        inside = jnp.where(index >= wide, index - wide, index)
        return jnp.where(
            inside < block_y,
            inside,
            jnp.where(inside < block_y + HALO_Y, inside - block_y - HALO_Y, inside - HALO_Y),
        )

    backs = []
    for view in range(views):
        shape = (block_y, 2 * wide)
        column = iota(shape, 1)
        high, low = halves(
            band_of(psf, first + view, 1, place_of(column) - iota(shape, 0) + radius)
        )
        f32 = jnp.float32
        rows = slice(view * block_y, (view + 1) * block_y)
        along_y[rows] = jnp.where(column < wide, high.astype(f32), low.astype(f32)).astype(
            jnp.bfloat16
        )
        shape = (2 * wide, block_y)
        row = iota(shape, 0)
        high, low = halves(band_of(psf, first + view, 1, place_of(row) - iota(shape, 1) + radius))
        back = jnp.where(row < wide, high.astype(f32), low.astype(f32))
        backs.append(back)
        back_one[view] = back.astype(jnp.bfloat16)
        shape = (depth, depth)
        difference = iota(shape, 0) - iota(shape, 1)
        along_z[view] = jnp.concatenate(
            halves(band_of(psf, first + view, 2, difference + radius)), axis=0
        )
        back_z[view] = jnp.concatenate(
            halves(band_of(psf, first + view, 2, radius - difference)), axis=0
        )
    back_y[...] = jnp.concatenate(backs, axis=1).astype(jnp.bfloat16)


def contract_last(left, right):
    return lax.dot_general(
        left, right, (((1,), (1,)), ((), ())), preferred_element_type=jnp.float32
    )


def make_norm(psf, first, radius, tile_shape, block, xs, ys, counts, spread, inverse_norm, scale):
    all_views, rows, tiles_row = block.shape
    block_x, block_y, depth = inverse_norm.shape
    views = scale.shape[0]
    tile_wide, tile_tall = tile_shape
    f32 = jnp.float32
    bf16 = jnp.bfloat16
    edge = 8
    near_x = block_x + 2 * edge
    near_y = block_y + 2 * edge
    start_x = lax.axis_index("gx") * block_x - edge
    start_y = lax.axis_index("gy") * block_y - edge
    profiles = []
    for view in range(all_views):
        summed = None
        for row in range(rows):
            left = block[view, row : row + 1] * block_x + xs[view, row : row + 1]
            top = ys[view, row : row + 1] + row * block_y
            from_x = iota((near_x, tiles_row), 0) + start_x - left
            from_y = iota((near_y, tiles_row), 0) + start_y - top
            in_x = jnp.where((from_x >= 0) & (from_x < tile_wide), f32(1), f32(0)).astype(bf16)
            in_y = jnp.where((from_y >= 0) & (from_y < tile_tall), f32(1), f32(0)).astype(bf16)
            term = contract_last(in_y, in_x)
            summed = term if summed is None else summed + term
        counts[view] = summed
        covered = jnp.minimum(summed, 1.0).astype(bf16)
        shape = (block_y, near_y)
        high, low = halves(
            band_of(psf, view, 1, iota(shape, 0) - (iota(shape, 1) - edge) + radius)
        )
        value = jnp.dot(high, covered, preferred_element_type=f32)
        value = value + jnp.dot(low, covered, preferred_element_type=f32)
        shape = (near_x, block_x)
        high, low = halves(
            band_of(psf, view, 0, iota(shape, 1) - (iota(shape, 0) - edge) + radius)
        )
        value_high, value_low = halves(value)
        result = jnp.dot(value_high, high, preferred_element_type=f32)
        result = result + jnp.dot(value_low, high, preferred_element_type=f32)
        result = result + jnp.dot(value_high, low, preferred_element_type=f32)
        spread[view] = result
        profile = jnp.zeros((1, depth), f32)
        place = iota((1, depth), 1)
        for tap in range(psf.shape[2]):
            source = place - tap + radius
            profile = profile + jnp.where(
                (source >= 0) & (source < depth), psf[view, 2, tap], f32(0)
            )
        profiles.append(profile)
    shares = [
        1.0 / jnp.maximum(counts[first + view, edge : edge + block_y], 1.0)
        for view in range(views)
    ]
    for view in range(views):
        counts[first + view, edge : edge + block_y] = shares[view]
    shape = (block_y, depth)
    for x in range(block_x):
        summed = None
        for view in range(all_views):
            term = jnp.broadcast_to(spread[view, :, x : x + 1], shape) * profiles[view]
            summed = term if summed is None else summed + term
        inverse_norm[x] = 1.0 / (summed + damping)
        at = edge + x
        for view in range(views):
            scale[view, x] = jnp.broadcast_to(
                counts[first + view, edge : edge + block_y, at : at + 1], shape
            )


class Route:
    def __init__(self, tx_near, tx_far, rx_near, rx_far, sems):
        self.me = lax.axis_index("gx")
        low = self.me < 2
        self.inside = lax.rem(self.me, 2)
        self.beside = jnp.where(self.inside == 0, self.me + 1, self.me - 1)
        self.gate = jnp.where(low, 2, 1)
        self.is_gate = jnp.logical_or(self.me == 1, self.me == 2)
        self.tx_near, self.tx_far, self.rx_near, self.rx_far = tx_near, tx_far, rx_near, rx_far
        self.near_send, self.near_recv, self.far_send, self.far_recv, self.on_send = sems
        self.pieces = ((0, 4), (4, 4), (8, tx_far.shape[1] - 8))

    def near(self, view):
        return pltpu.make_async_remote_copy(
            src_ref=self.tx_near.at[view],
            dst_ref=self.rx_near[view],
            send_sem=self.near_send.at[view],
            recv_sem=self.near_recv.at[view],
            device_id={"gx": self.beside},
            device_id_type=MESH,
        )

    def far(self, view, piece, side):
        span = pl.ds(*self.pieces[piece])
        return pltpu.make_async_remote_copy(
            src_ref=self.tx_far.at[view, span],
            dst_ref=self.rx_far[view].at[side, span],
            send_sem=self.far_send.at[view, piece],
            recv_sem=self.far_recv.at[view, side, piece],
            device_id={"gx": self.gate},
            device_id_type=MESH,
        )

    def onward(self, view, piece, side):
        span = pl.ds(*self.pieces[piece])
        return pltpu.make_async_remote_copy(
            src_ref=self.rx_far[view].at[side, span],
            dst_ref=self.rx_far[view].at[side, span],
            send_sem=self.on_send.at[view, side, piece],
            recv_sem=self.far_recv.at[view, side, piece],
            device_id={"gx": self.beside},
            device_id_type=MESH,
        )

    def pack_near(self, view, tiles, pack):
        for at in range(PAIR_SLOTS):
            self.tx_near[view, at] = tiles[view, 0, pack[view, at]]

    def pack_far(self, view, tiles, pack):
        for at in range(self.tx_far.shape[1]):
            self.tx_far[view, at] = tiles[view, 0, pack[view, PAIR_SLOTS + at]]

    def send(self, view, pieces):
        for piece in pieces:
            self.far(view, piece, self.inside).start()

    def sent(self, view, piece):
        self.far(view, piece, self.inside).wait_send()

    def hand_on(self, view, piece):
        @pl.when(self.is_gate)
        def _():
            for side in range(2):
                self.far(view, piece, side).wait_recv()
                self.onward(view, piece, side).start()

    def receive_far(self, view):
        @pl.when(self.is_gate)
        def _():
            for side in range(2):
                self.far(view, 2, side).wait_recv()

        @pl.when(jnp.logical_not(self.is_gate))
        def _():
            for piece in range(2):
                for side in range(2):
                    self.onward(view, piece, side).wait_recv()

    def drain(self, views):
        for view in range(views):
            for piece in range(3):
                if piece == 0 or view in (0, views - 1):
                    self.sent(view, piece)
            self.near(view).wait_send()

        @pl.when(self.is_gate)
        def _():
            for view in range(views):
                for piece in range(2):
                    for side in range(2):
                        self.onward(view, piece, side).wait_send()


def chooser_of(view, chosen, entry_y, tile_tall, block_y):
    entries = len(chosen)
    lane = iota((8, entries * tile_tall), 1)
    target = jnp.zeros(lane.shape, jnp.int32)
    for index, entry in enumerate(chosen):
        inside = (lane >= index * tile_tall) & (lane < (index + 1) * tile_tall)
        target = jnp.where(inside, entry_y[view, entry] + lane - index * tile_tall, target)
    target = target[:1]
    one, zero = jnp.float32(1), jnp.float32(0)
    rows = iota((block_y, target.shape[1]), 0)
    return jnp.where(rows == target, one, zero).astype(jnp.bfloat16)


def place_view(view, sources, groups, tables, padded, partial, begins, ends, refs, below):
    slot, entry_x, entry_y = tables
    scale, per_blur, back_z, observed, spread = refs
    block_x, block_y, depth = observed.shape[1:]
    bf16 = jnp.bfloat16
    f32 = jnp.float32
    padded_planes, tile_tall = padded.shape[1:3]
    margin = padded_planes - block_x
    tile_wide = block_x - margin
    chosen = [g * PAIR_SLOTS + at for g in sources for at in range(PAIR_SLOTS)]
    for entry in chosen:
        read = groups[entry // PAIR_SLOTS]
        padded[entry, margin : margin + tile_wide] = read(slot[view, entry])
    chooser = chooser_of(view, chosen, entry_y, tile_tall, block_y)

    @pl.loop(0, block_x // 2)
    def _(step):
        columns = []
        for side in range(2):
            x = 2 * step + side
            rows = [padded[entry, x + margin - entry_x[view, entry]] for entry in chosen]
            columns.append(jnp.concatenate(rows, axis=0))
        both = jnp.concatenate(columns, axis=1)
        summed = jnp.dot(chooser, both, preferred_element_type=f32)
        quotients = []
        for side in range(2):
            x = 2 * step + side
            plane = summed[:, side * depth : (side + 1) * depth]
            if not begins:
                plane = plane + partial[x]
            if not ends:
                partial[x] = plane
                continue
            observed[view, x] = plane * scale[view, x]
            quotients.append((plane * per_blur[view, x]).astype(bf16))
        if ends:
            stacked = jnp.concatenate(quotients, axis=0)
            stacked = jnp.concatenate([stacked, stacked], axis=1)
            result = jnp.dot(stacked, back_z[view], preferred_element_type=f32)
            for side in range(2):
                rows = slice(side * block_y, (side + 1) * block_y)
                spread[view, below + 2 * step + side] = result[rows]


def routed_kernel(sizes, *refs):
    (
        psf,
        pack,
        slot,
        entry_x,
        entry_y,
        tiles,
        block,
        xs,
        ys,
        initial,
        estimate,
        fullest,
        start_center,
        start_low,
        start_high,
        start_send_low,
        start_send_high,
        start_send,
        start_recv,
        center,
        low,
        high,
        send_low,
        send_high,
        passed_y,
        passed_z,
        acc,
        acc_y,
        out_x,
        out_y,
        in_x,
        in_y,
        far_x,
        far_y,
        vert_in,
        est_send,
        est_recv,
        acc_send,
        acc_recv,
        vert_send,
        vert_recv,
        far_send,
        far_recv,
        taps_x,
        along_y,
        back_y,
        back_one,
        along_z,
        back_z,
        counts,
        norm_spread,
        inverse_norm,
        scale,
        per_blur,
        observed,
        fill_mine,
        fill_other,
        fill_send,
        fill_recv,
        padded,
        partial,
        tx_near,
        tx_far,
        *rest,
    ) = refs
    views, block_x, block_y, depth = observed.shape
    rx_near, rx_far, route_sems = rest[:views], rest[views : 2 * views], rest[2 * views :]
    tap_count = psf.shape[2]
    radius = tap_count // 2
    planes = center.shape[1]
    per_device = tiles.shape[2]
    tile_shape = tiles.shape[3:5]
    bf16 = jnp.bfloat16
    f32 = jnp.float32
    links = Links(sizes, radius, block_x)
    column = lax.axis_index("gx")
    first_view = lax.axis_index("vert") * views
    partner = {"vert": 1 - lax.axis_index("vert")}
    part_count = lax.axis_size("groups")
    parts = [
        {"groups": lax.rem(lax.axis_index("groups") + step, part_count)}
        for step in range(1, part_count)
    ]
    route = Route(tx_near, tx_far, rx_near, rx_far, route_sems)

    barrier = pltpu.get_barrier_semaphore()
    others = [partner] + parts
    others += [{"gx": lax.rem(column + step, sizes[0])} for step in range(1, sizes[0])]
    for other in others:
        pl.semaphore_signal(barrier, inc=1, device_id=other, device_id_type=MESH)
    peers = len(others)
    for dx, dy in links.directions:
        if dy == 0:
            continue
        peers = peers + links.exists(dx, dy).astype(jnp.int32)

        @pl.when(links.exists(dx, dy))
        def _():
            pl.semaphore_signal(
                barrier, inc=1, device_id=links.device(dx, dy), device_id_type=MESH
            )

    @pl.loop(0, block_x)
    def _(x):
        publish(links, start_center, start_send_low, start_send_high, x, initial[x])

    clear_missing(links, start_center, start_low, start_high)
    pl.semaphore_wait(barrier, peers)
    start = (
        ghosts_of_estimate(
            links, start_center, start_low, start_high, start_send_low, start_send_high
        ),
        start_send,
        start_recv,
    )
    links.start(*start, links.directions)
    for view in range(views):
        route.pack_near(view, tiles, pack)
        route.near(view).start()
        route.pack_far(view, tiles, pack)
        if view < 2:
            route.send(view, range(3) if view == 0 else (0,))

    number = iota(block.shape[1:], 1)
    most = jnp.zeros((block.shape[1], 1), f32)
    for view in range(block.shape[0]):
        beyond = (block[view] >= sizes[0] // 2) != (number >= block.shape[2] // 2)
        for source in range(sizes[0]):
            within = (number >= source * per_device) & (number < (source + 1) * per_device)
            count = jnp.sum(jnp.where(beyond & within, f32(1), f32(0)), axis=1, keepdims=True)
            most = jnp.maximum(most, count)
    fill_mine[...] = jnp.broadcast_to(jnp.max(most, axis=0, keepdims=True), fill_mine.shape)
    fills = [
        pltpu.make_async_remote_copy(
            src_ref=fill_mine,
            dst_ref=fill_other.at[index],
            send_sem=fill_send.at[index],
            recv_sem=fill_recv.at[index],
            device_id=other,
            device_id_type=MESH,
        )
        for index, other in enumerate(parts)
    ]
    for fill in fills:
        fill.start()

    make_bands(psf, first_view, radius, block_y, along_y, back_y, back_one, along_z, back_z)
    for view in range(views):
        for tap in range(tap_count):
            taps_x[view, tap] = psf[first_view + view, 0, tap]
    for sweep in range(ITERS):
        if sweep > 0:
            at = sweep - 1
            clear_missing(links, center.at[at], low.at[at], high.at[at])
        for step in (-1, 1):
            side = 0 if step == -1 else 1

            @pl.when(jnp.logical_not(links.exists(step, 0)))
            def _():
                in_x[sweep, side] = jnp.zeros(in_x.shape[2:], bf16)
                for other in range(2):
                    in_y[sweep, other, links.ghost(step)] = jnp.zeros(
                        (radius,) + in_y.shape[3:], bf16
                    )

            @pl.when(jnp.logical_not(links.exists(0, step)))
            def _():
                in_y[sweep, side] = jnp.zeros(in_y.shape[2:], bf16)

    for entry in range(padded.shape[0]):
        padded[entry] = jnp.zeros(padded.shape[1:], bf16)
    below = 2 * radius
    beyond = passed_z.shape[1] - below - block_x
    passed_z[:, :below] = jnp.zeros((views, below, block_y, depth), f32)
    passed_z[:, below + block_x :] = jnp.zeros((views, beyond, block_y, depth), f32)
    group = group_of(block_x)

    make_norm(
        psf,
        first_view,
        radius,
        tile_shape,
        block,
        xs,
        ys,
        counts,
        norm_spread,
        inverse_norm,
        scale,
    )
    links.finish(*start, links.directions)
    pass_along_y(start_center, start_low, start_high, along_y, passed_y, views)

    @pl.loop(0, block_x // group)
    def _(step):
        first = step * group
        for view in range(views):
            blurred = pass_along_xz(taps_x, passed_y, along_z[view], view, first, group)
            blurred = blurred.reshape(group, block_y, depth)
            chunk = pl.ds(first, group)
            per_blur[view, chunk] = scale[view, chunk] / (blurred + soft_floor)

    if views > 1:
        route.send(1, (1, 2))
    for fill in fills:
        fill.wait()
    greatest = fill_mine[...]
    for index in range(len(fills)):
        greatest = jnp.maximum(greatest, fill_other[index])
    fullest[0, 0] = jnp.max(greatest)

    def vert_copy(sweep, start, size):
        chunk = pl.ds(start, size)
        return pltpu.make_async_remote_copy(
            src_ref=acc.at[sweep, chunk],
            dst_ref=vert_in.at[sweep, chunk],
            send_sem=vert_send.at[sweep],
            recv_sem=vert_recv.at[sweep],
            device_id=partner,
            device_id_type=MESH,
        )

    first_chunk = radius // 4
    last_chunk = (radius + block_x - 1) // 4
    far_chunk = (radius + block_x) // 4
    edge_turns = planes // 4 - far_chunk + -(-radius // 4)
    rows = block_y + 2 * HALO_Y

    def adjoint(sweep, chosen, begins, ends, turn):
        step = lax.rem(turn + far_chunk, planes // 4)
        matrix = back_y[...] if len(chosen) == views else back_one[chosen[0]]
        for first in (4 * step, 4 * step + 2):
            columns = []
            for x in (first, first + 1):
                stack = []
                for view in chosen:
                    value = taps_x[view, 0] * passed_z[view, x + below]
                    for tap in range(1, tap_count):
                        value = value + taps_x[view, tap] * passed_z[view, x + below - tap]
                    stack.append(value.astype(bf16))
                columns.append(jnp.concatenate(stack, axis=0))
            both = jnp.concatenate(columns, axis=1)
            result = jnp.dot(matrix, both, preferred_element_type=f32)
            result = result[:rows] + result[rows:]
            for side in range(2):
                x = first + side
                lanes = slice(side * depth, (side + 1) * depth)
                middle, edges = result[:block_y, lanes], result[block_y:, lanes]
                if not begins:
                    middle = middle + acc[sweep, x]
                    edges = edges + acc_y[x]
                acc[sweep, x] = middle
                if ends:
                    out_y[sweep, 0, x] = edges[:HALO_Y].astype(bf16)
                    out_y[sweep, 1, x] = edges[HALO_Y:].astype(bf16)
                else:
                    acc_y[x] = edges

        if ends:

            @pl.when(jnp.logical_and(step >= first_chunk, step <= last_chunk))
            def _():
                vert_copy(sweep, 4 * step, 4).start()

    for sweep in range(ITERS):
        if sweep == 0:
            for view in range(views):
                groups = [
                    lambda at: tiles[view, 0, at],
                    lambda at: rx_near[view][at],
                    lambda at: rx_far[view][0, at],
                    lambda at: rx_far[view][1, at],
                ]
                place = functools.partial(
                    place_view,
                    groups=groups,
                    tables=(slot, entry_x, entry_y),
                    padded=padded,
                    partial=partial,
                    refs=(scale, per_blur, back_z, observed, passed_z),
                    below=below,
                )
                last = view + 1 == views
                if last:
                    route.near(view).wait_recv()
                    place(view, (0, 1), begins=True, ends=False)
                if view == 0:
                    route.hand_on(view, 0)
                paced = view > 0 and not last
                for piece in (1, 2):
                    if paced:
                        route.sent(view, piece)
                        route.send(view + 1, (piece,))
                    if piece == 1:
                        route.hand_on(view, piece)
                route.receive_far(view)
                if last:
                    place(view, (2, 3), begins=False, ends=True)
                else:
                    route.near(view).wait_recv()
                    place(view, (0, 1, 2, 3), begins=True, ends=True)
                    if view + 2 < views:
                        route.send(view + 2, (0,))
                    if view > 0:
                        route.hand_on(view + 1, 0)

                    @pl.loop(0, planes // 4)
                    def _(turn):
                        adjoint(sweep, (view,), view == 0, False, turn)

                    if view == 0:
                        route.hand_on(view + 1, 0)

            chosen, begins = (views - 1,), views == 1
        else:
            at = sweep - 1
            pass_along_y(center.at[at], low.at[at], high.at[at], along_y, passed_y, views)

            @pl.loop(0, block_x // group)
            def _(step):
                first = step * group
                for view in range(views):
                    blurred = pass_along_xz(taps_x, passed_y, along_z[view], view, first, group)
                    measured = observed[view, pl.ds(first, group)].reshape(blurred.shape)
                    result = spread_quotient(measured, blurred, back_z[view])
                    passed_z[view, pl.ds(below + first, group)] = result.reshape(
                        group, block_y, depth
                    )

            chosen, begins = tuple(range(views)), True

        sums = (
            ghosts_of_sums(
                links, out_x.at[sweep], out_y.at[sweep], in_x.at[sweep], in_y.at[sweep]
            ),
            acc_send.at[sweep],
            acc_recv.at[sweep],
        )

        @pl.loop(0, edge_turns)
        def _(turn):
            adjoint(sweep, chosen, begins, True, turn)

        @pl.loop(0, radius)
        def _(x):
            out_x[sweep, 0, x] = acc[sweep, x].astype(bf16)
            out_x[sweep, 1, x] = acc[sweep, radius + block_x + x].astype(bf16)

        links.start(*sums, links.across_x())

        @pl.loop(edge_turns, planes // 4)
        def _(turn):
            adjoint(sweep, chosen, begins, True, turn)

        links.start(*sums, links.along_y_only())
        links.finish(*sums, links.across_x())
        links.finish(*sums, links.along_y_only())
        forwards = [
            pltpu.make_async_remote_copy(
                src_ref=near.at[sweep],
                dst_ref=far.at[sweep],
                send_sem=far_send.at[sweep, index],
                recv_sem=far_recv.at[sweep, index],
                device_id=partner,
                device_id_type=pl.DeviceIdType.MESH,
            )
            for index, (near, far) in enumerate(((in_x, far_x), (in_y, far_y)))
        ]
        for forward in forwards:
            forward.start()
        vert_copy(sweep, 4 * first_chunk, 4 * (last_chunk - first_chunk + 1)).wait()

        @pl.loop(0, block_x)
        def _(x):
            acc[sweep, radius + x] = acc[sweep, radius + x] + vert_in[sweep, radius + x]

        for forward in forwards:
            forward.wait()

        def beyond_y(side, plane):
            return in_y[sweep, side, plane].astype(f32) + far_y[sweep, side, plane].astype(f32)

        @pl.loop(0, radius)
        def _(x):
            for side, at, beside in ((0, radius + x, x), (1, block_x + x, radius + block_x + x)):
                plane = acc[sweep, at] + (
                    in_x[sweep, side, x].astype(f32) + far_x[sweep, side, x].astype(f32)
                )
                first = plane[:HALO_Y] + beyond_y(0, beside)
                last = plane[block_y - HALO_Y :] + beyond_y(1, beside)
                acc[sweep, at] = jnp.concatenate(
                    [first, plane[HALO_Y : block_y - HALO_Y], last], axis=0
                )

        def update(x):
            plane = acc[sweep, radius + x]
            first = plane[:HALO_Y] + beyond_y(0, radius + x)
            last = plane[block_y - HALO_Y :] + beyond_y(1, radius + x)
            combined = jnp.concatenate([first, plane[HALO_Y : block_y - HALO_Y], last], axis=0)
            before = initial[x] if sweep == 0 else estimate[x]
            after = before * (combined + damping) * inverse_norm[x]
            estimate[x] = after
            if sweep + 1 < ITERS:
                publish(
                    links, center.at[sweep], send_low.at[sweep], send_high.at[sweep], x, after
                )

        if sweep + 1 < ITERS:
            news = (
                ghosts_of_estimate(
                    links,
                    center.at[sweep],
                    low.at[sweep],
                    high.at[sweep],
                    send_low.at[sweep],
                    send_high.at[sweep],
                ),
                est_send.at[sweep],
                est_recv.at[sweep],
            )

            @pl.loop(0, radius)
            def _(x):
                update(x)
                update(block_x - radius + x)

            links.start(*news, links.across_x())

            @pl.loop(radius, block_x - radius)
            def _(x):
                update(x)

            links.start(*news, links.along_y_only())
            links.finish(*news, links.directions)
        else:

            @pl.loop(0, block_x)
            def _(x):
                update(x)

    route.drain(views)


def routed(tiles, tile_block, tile_x, tile_y, psf, initial):
    block_x, block_y, depth = initial.shape
    views, _, per_device = tiles.shape[:3]
    all_views, rows, tiles_row = tile_x.shape
    tile = tiles.shape[3:]
    radius = psf.shape[2] // 2
    planes = planes_of(block_x, radius)
    extended_x = block_x + 2 * radius
    wide = block_y + 2 * HALO_Y
    sizes = (lax.axis_size("gx"), lax.axis_size("gy"))
    part_count = lax.axis_size("groups")
    cap = far_slots(per_device)
    block = tile_block.reshape(tile_x.shape)
    tables = plan(views, per_device, block, tile_x, tile_y)
    vmem = pl.BlockSpec(memory_space=pltpu.VMEM)
    smem = pl.BlockSpec(memory_space=pltpu.SMEM)
    dma = pltpu.SemaphoreType.DMA
    bf16 = jnp.bfloat16
    f32 = jnp.float32
    repeats = ITERS - 1
    volume = (views, block_x, block_y, depth)
    return pl.pallas_call(
        functools.partial(routed_kernel, sizes),
        out_shape=[
            jax.ShapeDtypeStruct(initial.shape, f32),
            jax.ShapeDtypeStruct((1, 1), f32),
        ],
        in_specs=[smem] * 5 + [vmem] * 5,
        out_specs=[vmem, smem],
        scratch_shapes=estimate_scratch(planes, block_x, block_y, depth)
        + [dma((8,)), dma((8,))]
        + [
            pltpu.VMEM((repeats,) + scratch.shape, scratch.dtype)
            for scratch in estimate_scratch(planes, block_x, block_y, depth)
        ]
        + [
            pltpu.VMEM((views, planes, block_y, depth), f32),
            pltpu.VMEM((views, planes + 2 * radius, block_y, depth), f32),
            pltpu.VMEM((ITERS, planes, block_y, depth), f32),
            pltpu.VMEM((planes, 2 * HALO_Y, depth), f32),
            pltpu.VMEM((ITERS, 2, radius, block_y, depth), bf16),
            pltpu.VMEM((ITERS, 2, planes, HALO_Y, depth), bf16),
            pltpu.VMEM((ITERS, 2, radius, block_y, depth), bf16),
            pltpu.VMEM((ITERS, 2, extended_x, HALO_Y, depth), bf16),
            pltpu.VMEM((ITERS, 2, radius, block_y, depth), bf16),
            pltpu.VMEM((ITERS, 2, extended_x, HALO_Y, depth), bf16),
            pltpu.VMEM((ITERS, planes, block_y, depth), f32),
            dma((repeats, 8)),
            dma((repeats, 8)),
            dma((ITERS, 8)),
            dma((ITERS, 8)),
            dma((ITERS,)),
            dma((ITERS,)),
            dma((ITERS, 2)),
            dma((ITERS, 2)),
            pltpu.SMEM((views, psf.shape[2]), f32),
            pltpu.VMEM((views * block_y, 2 * wide), bf16),
            pltpu.VMEM((2 * wide, views * block_y), bf16),
            pltpu.VMEM((views, 2 * wide, block_y), bf16),
            pltpu.VMEM((views, 2 * depth, depth), bf16),
            pltpu.VMEM((views, 2 * depth, depth), bf16),
            pltpu.VMEM((all_views, block_y + 16, block_x + 16), f32),
            pltpu.VMEM((all_views, block_y, block_x), f32),
            pltpu.VMEM(initial.shape, f32),
            pltpu.VMEM(volume, f32),
            pltpu.VMEM(volume, f32),
            pltpu.VMEM(volume, f32),
            pltpu.VMEM((8, 128), f32),
            pltpu.VMEM((part_count - 1, 8, 128), f32),
            dma((part_count - 1,)),
            dma((part_count - 1,)),
            pltpu.VMEM((4 * PAIR_SLOTS, 2 * block_x - tile[0]) + tile[1:], bf16),
            pltpu.VMEM(volume[1:], f32),
            pltpu.VMEM((views, PAIR_SLOTS) + tile, bf16),
            pltpu.VMEM((views, cap) + tile, bf16),
        ]
        + [pltpu.VMEM((PAIR_SLOTS,) + tile, bf16)] * views
        + [pltpu.VMEM((2, cap) + tile, bf16)] * views
        + [dma((views,)), dma((views,)), dma((views, 3)), dma((views, 2, 3)), dma((views, 2, 2))],
        compiler_params=pltpu.CompilerParams(
            collective_id=2, has_side_effects=True, vmem_limit_bytes=56 << 20
        ),
    )(psf, *tables, tiles, block, tile_x, tile_y, initial)


def general(tiles, tile_block, tile_x, tile_y, psf, initial):
    column_count = lax.axis_size("gx")
    column_index = lax.axis_index("gx")
    row_index = lax.axis_index("gy")
    core_index = lax.axis_index("vert")
    local_views = tiles.shape[0]
    all_views = psf.shape[0]
    per_device = tiles.shape[2]
    tile_wide = tiles.shape[3]
    tile_tall = tiles.shape[4]
    block_x, block_y, depth = initial.shape
    capacity = max(2, 2 * per_device // column_count)
    radius = psf.shape[2] // 2
    first_view = core_index * local_views
    mine_psf = lax.dynamic_slice_in_dim(psf, first_view, local_views, 0)

    def my_rows(table):
        chosen = lax.dynamic_slice_in_dim(table, first_view, local_views, 0)
        chosen = lax.dynamic_slice_in_dim(chosen, row_index, 1, 1)[:, 0]
        return chosen.reshape(local_views, column_count, per_device)

    targets = my_rows(tile_block[:, :, :, 0])
    offsets_x = my_rows(tile_x)
    offsets_y = my_rows(tile_y)
    columns_iota = jnp.arange(column_count, dtype=jnp.int32)
    hits = (targets[..., None] == columns_iota).astype(jnp.int32)
    ranks = jnp.cumsum(hits, axis=2, dtype=jnp.int32)
    slot_ids = jnp.arange(capacity, dtype=jnp.int32) + 1
    sent_hits = jnp.swapaxes(lax.dynamic_slice_in_dim(hits, column_index, 1, 1)[:, 0], 1, 2)
    sent_ranks = jnp.swapaxes(lax.dynamic_slice_in_dim(ranks, column_index, 1, 1)[:, 0], 1, 2)
    chooser = sent_hits[:, :, None, :] * (
        sent_ranks[:, :, None, :] == slot_ids[None, None, :, None]
    ).astype(jnp.int32)
    outgoing = jnp.einsum(
        "vgkj,vjabz->gvkabz",
        chooser.astype(jnp.bfloat16),
        tiles[:, 0],
        preferred_element_type=jnp.bfloat16,
    )
    sizes = (column_count, lax.axis_size("gy"))
    halos = first_halos(sizes, radius, initial)
    outgoing, halos = lax.optimization_barrier((outgoing, halos))
    arrived = lax.all_to_all(outgoing, "gx", split_axis=0, concat_axis=0, tiled=True)
    from_hits = lax.dynamic_slice_in_dim(hits, column_index, 1, 3)[..., 0]
    from_ranks = lax.dynamic_slice_in_dim(ranks, column_index, 1, 3)[..., 0]
    picks = from_hits[:, :, None, :] * (
        from_ranks[:, :, None, :] == slot_ids[None, None, :, None]
    ).astype(jnp.int32)
    filled = jnp.sum(picks, axis=3).reshape(local_views, -1)
    corner_x = jnp.sum(picks * offsets_x[:, :, None, :], axis=3).reshape(local_views, -1)
    corner_y = jnp.sum(picks * offsets_y[:, :, None, :], axis=3).reshape(local_views, -1)

    row_iota = jnp.arange(tile_block.shape[1], dtype=jnp.int32)
    global_x = (tile_block[..., 0] * block_x + tile_x).reshape(all_views, -1)
    global_y = (row_iota[None, :, None] * block_y + tile_y).reshape(all_views, -1)
    near_x = jnp.arange(block_x + 2 * radius, dtype=jnp.int32) - radius
    near_y = jnp.arange(block_y + 2 * radius, dtype=jnp.int32) - radius
    cells_x = column_index * block_x + near_x
    cells_y = row_index * block_y + near_y
    cover_x = (
        (cells_x >= global_x[..., None]) & (cells_x < global_x[..., None] + tile_wide)
    ).astype(jnp.bfloat16)
    cover_y = (
        (cells_y >= global_y[..., None]) & (cells_y < global_y[..., None] + tile_tall)
    ).astype(jnp.bfloat16)
    counts = jnp.einsum("vti,vtj->vij", cover_x, cover_y, preferred_element_type=jnp.float32)
    coverage = jnp.minimum(counts, 1.0)
    iota_x = jnp.arange(block_x, dtype=jnp.int32)
    iota_y = jnp.arange(block_y, dtype=jnp.int32)
    iota_z = jnp.arange(depth, dtype=jnp.int32)
    adjoint_x = banded(psf[:, 0], iota_x[:, None] - near_x[None, :] + radius)
    adjoint_y = banded(psf[:, 1], iota_y[:, None] - near_y[None, :] + radius)
    exact = lax.Precision.HIGHEST
    spread = jnp.einsum("vij,vyj->viy", coverage, adjoint_y, precision=exact)
    spread = jnp.einsum("vxi,viy->vxy", adjoint_x, spread, precision=exact)
    profile = jnp.sum(banded(psf[:, 2], iota_z[:, None] - iota_z[None, :] + radius), axis=2)
    norm_field = jnp.einsum("vxy,vz->xyz", spread, profile, precision=exact)
    inverse_norm = 1.0 / (norm_field + damping)

    places_y = jnp.concatenate(
        [
            iota_y,
            jnp.arange(HALO_Y, dtype=jnp.int32) - HALO_Y,
            jnp.arange(HALO_Y, dtype=jnp.int32) + block_y,
        ]
    )
    band_y = banded(mine_psf[:, 1], places_y[None, :] - iota_y[:, None] + radius)
    high, low = split_high_low(band_y)
    flat = (local_views * block_y, places_y.shape[0])
    along_y = jnp.concatenate([high.reshape(flat), low.reshape(flat)], axis=1)
    back_y = jnp.concatenate([high.reshape(flat).T, low.reshape(flat).T], axis=0)
    band_z = banded(mine_psf[:, 2], iota_z[:, None] - iota_z[None, :] + radius)
    along_z = jnp.concatenate(split_high_low(band_z), axis=1)
    back_z = jnp.concatenate(split_high_low(jnp.swapaxes(band_z, 1, 2)), axis=1)
    taps_x = mine_psf[:, 0]
    blurred = first_blur(taps_x, halos, along_y, along_z, block_x)
    observed, spreads = place(filled, corner_x, corner_y, arrived, blurred, back_z, radius)
    return sweeps(
        sizes,
        taps_x,
        observed,
        spreads,
        initial,
        inverse_norm,
        along_y,
        back_y,
        along_z,
        back_z,
    )


def shards(tiles, tile_block, tile_x, tile_y, psf, initial):
    arguments = (tiles, tile_block, tile_x, tile_y, psf, initial)
    if lax.axis_size("gx") != 4:
        return general(*arguments)
    estimate, fullest = routed(*arguments)
    return lax.cond(
        fullest[0, 0] > far_slots(tiles.shape[2]),
        lambda result, *rest: general(*rest),
        lambda result, *rest: result,
        estimate,
        *arguments,
    )


def solution(mesh):
    in_specs = (
        P("vert", "gy", ("groups", "gx"), None, None, None),
        P(None, None, "groups", None),
        P(None, None, "groups"),
        P(None, None, "groups"),
        P(),
        P(("groups", "gx"), "gy", None),
    )
    out_specs = P(("groups", "gx"), "gy", None)
    return jax.shard_map(shards, mesh=mesh, in_specs=in_specs, out_specs=out_specs, check_vma=False)
```

```python
import functools

import jax
import jax.numpy as jnp
from jax import lax
from jax.experimental import pallas as pl
from jax.experimental.pallas import tpu as pltpu
from jax.sharding import PartitionSpec as P

ITERS = 2
HALO_Y = 8

soft_floor = 0.01
damping = 0.5


def split_high_low(matrix):
    high = lax.reduce_precision(matrix, 8, 7)
    return high.astype(jnp.bfloat16), (matrix - high).astype(jnp.bfloat16)


def banded(taps, difference):
    summed = None
    for tap_index in range(taps.shape[-1]):
        term = jnp.where(difference == tap_index, taps[..., tap_index, None, None], 0.0)
        summed = term if summed is None else summed + term
    return summed


class Links:
    def __init__(self, sizes, radius, block_x):
        self.radius = radius
        self.block_x = block_x
        self.me = (lax.axis_index("gx"), lax.axis_index("gy"))
        self.sizes = sizes
        self.directions = [
            (dx, dy) for dx in (-1, 0, 1) for dy in (-1, 0, 1) if (dx, dy) != (0, 0)
        ]

    def exists(self, dx, dy):
        good = None
        for step, me, count in zip((dx, dy), self.me, self.sizes):
            if step == 0:
                continue
            test = me > 0 if step == -1 else me < count - 1
            good = test if good is None else jnp.logical_and(good, test)
        return good

    def device(self, dx, dy):
        return {"gx": self.me[0] + dx, "gy": self.me[1] + dy}

    def greet(self, others=()):
        barrier = pltpu.get_barrier_semaphore()
        for dx, dy in self.directions:

            @pl.when(self.exists(dx, dy))
            def _():
                pl.semaphore_signal(
                    barrier,
                    inc=1,
                    device_id=self.device(dx, dy),
                    device_id_type=pl.DeviceIdType.MESH,
                )

        for other in others:
            pl.semaphore_signal(
                barrier, inc=1, device_id=other, device_id_type=pl.DeviceIdType.MESH
            )

    def await_greetings(self, others=0):
        peers = others
        for dx, dy in self.directions:
            peers = peers + self.exists(dx, dy).astype(jnp.int32)
        pl.semaphore_wait(pltpu.get_barrier_semaphore(), peers)

    def span(self, step):
        if step == 0:
            return pl.ds(self.radius, self.block_x)
        return pl.ds(self.radius if step == -1 else self.block_x, self.radius)

    def ghost(self, step):
        if step == 0:
            return pl.ds(self.radius, self.block_x)
        return pl.ds(0 if step == -1 else self.block_x + self.radius, self.radius)

    def part(self, step):
        if step == 0:
            return pl.ds(0, self.block_x)
        return pl.ds(0 if step == -1 else self.block_x - self.radius, self.radius)

    def exchange(self, make, send_sem, recv_sem):
        self.start(make, send_sem, recv_sem, self.directions)
        self.finish(make, send_sem, recv_sem, self.directions)

    def across_x(self):
        return [one for one in self.directions if one[0] != 0]

    def along_y_only(self):
        return [one for one in self.directions if one[0] == 0]

    def copy(self, make, send_sem, recv_sem, dx, dy):
        index = self.directions.index((dx, dy))
        src, dst = make(dx, dy)
        return pltpu.make_async_remote_copy(
            src_ref=src,
            dst_ref=dst,
            send_sem=send_sem.at[index],
            recv_sem=recv_sem.at[index],
            device_id=self.device(dx, dy),
            device_id_type=pl.DeviceIdType.MESH,
        )

    def start(self, make, send_sem, recv_sem, directions):
        for dx, dy in directions:

            @pl.when(self.exists(dx, dy))
            def _():
                self.copy(make, send_sem, recv_sem, dx, dy).start()

    def finish(self, make, send_sem, recv_sem, directions):
        for dx, dy in directions:

            @pl.when(self.exists(dx, dy))
            def _():
                self.copy(make, send_sem, recv_sem, dx, dy).wait_send()

            @pl.when(self.exists(-dx, -dy))
            def _():
                self.copy(make, send_sem, recv_sem, dx, dy).wait_recv()


def ghosts_of_estimate(links, center, low, high, send_low, send_high):
    def make(dx, dy):
        if dy == 0:
            return center.at[links.span(dx)], center.at[links.ghost(-dx)]
        if dy == -1:
            return send_low.at[links.part(dx)], high.at[links.ghost(-dx)]
        return send_high.at[links.part(dx)], low.at[links.ghost(-dx)]

    return make


def ghosts_of_sums(links, out_x, out_y, in_x, in_y):
    def make(dx, dy):
        if dy == 0:
            side = 0 if dx == -1 else 1
            return out_x.at[side], in_x.at[1 - side]
        side = 0 if dy == -1 else 1
        return out_y.at[side, links.ghost(dx)], in_y.at[1 - side, links.ghost(-dx)]

    return make


def clear_missing(links, center, low, high):
    radius = links.radius
    for step in (-1, 1):

        @pl.when(jnp.logical_not(links.exists(step, 0)))
        def _():
            for rows in (center, low, high):
                rows[links.ghost(step)] = jnp.zeros((radius,) + rows.shape[1:], rows.dtype)

        @pl.when(jnp.logical_not(links.exists(0, step)))
        def _():
            rows = low if step == -1 else high
            rows[...] = jnp.zeros(rows.shape, rows.dtype)

    tail = links.block_x + 2 * radius
    for rows in (center, low, high):
        rows[tail:] = jnp.zeros((rows.shape[0] - tail,) + rows.shape[1:], rows.dtype)


def publish(links, center, send_low, send_high, x, plane):
    center[links.radius + x] = plane.astype(jnp.bfloat16)
    send_low[x] = plane[:HALO_Y].astype(jnp.bfloat16)
    send_high[x] = plane[plane.shape[0] - HALO_Y :].astype(jnp.bfloat16)


def pass_along_y(center, low, high, along_y, passed_y, views):
    block_y, depth = center.shape[1:]

    @pl.loop(0, center.shape[0] // 4)
    def _(step):
        for first in (4 * step, 4 * step + 2):
            columns = []
            for x in (first, first + 1):
                edges = jnp.concatenate(
                    [low[x].astype(jnp.float32), high[x].astype(jnp.float32)], axis=0
                ).astype(jnp.bfloat16)
                columns.append(jnp.concatenate([center[x], edges], axis=0))
            both = jnp.concatenate(columns, axis=1)
            both = jnp.concatenate([both, both], axis=0)
            result = jnp.dot(along_y[...], both, preferred_element_type=jnp.float32)
            for view in range(views):
                rows = slice(view * block_y, (view + 1) * block_y)
                passed_y[view, first] = result[rows, :depth]
                passed_y[view, first + 1] = result[rows, depth:]


def pass_along_xz(taps_x, passed_y, along_z, view, first, group):
    planes = []
    for inner in range(group):
        x = first + inner
        value = taps_x[view, 0] * passed_y[view, x]
        for tap in range(1, taps_x.shape[1]):
            value = value + taps_x[view, tap] * passed_y[view, x + tap]
        planes.append(value.astype(jnp.bfloat16))
    stacked = jnp.concatenate(planes, axis=0)
    stacked = jnp.concatenate([stacked, stacked], axis=1)
    return jnp.dot(stacked, along_z, preferred_element_type=jnp.float32)


def spread_quotient(measured, blurred, back_z):
    quotient = (measured / (blurred + soft_floor)).astype(jnp.bfloat16)
    quotient = jnp.concatenate([quotient, quotient], axis=1)
    return jnp.dot(quotient, back_z, preferred_element_type=jnp.float32)


def group_of(block_x):
    group = 4
    while block_x % group:
        group //= 2
    return group


def halo_kernel(
    sizes, radius, initial, center, low, high, all_center, all_low, all_high, *scratch
):
    send_low, send_high, send_sem, recv_sem = scratch
    block_x = initial.shape[0]
    links = Links(sizes, radius, block_x)
    links.greet()

    @pl.loop(0, block_x)
    def _(x):
        publish(links, all_center, send_low, send_high, x, initial[x])

    clear_missing(links, all_center, all_low, all_high)
    links.await_greetings()
    links.exchange(
        ghosts_of_estimate(links, all_center, all_low, all_high, send_low, send_high),
        send_sem,
        recv_sem,
    )

    @pl.loop(0, center.shape[0])
    def _(x):
        center[x] = all_center[x]
        low[x] = all_low[x]
        high[x] = all_high[x]


def blur_kernel(taps_x, center, low, high, along_y, along_z, blurred, passed_y):
    views, block_x, block_y, depth = blurred.shape
    pass_along_y(center, low, high, along_y, passed_y, views)
    group = group_of(block_x)

    @pl.loop(0, block_x // group)
    def _(step):
        for view in range(views):
            value = pass_along_xz(taps_x, passed_y, along_z[view], view, step * group, group)
            blurred[view, pl.ds(step * group, group)] = value.reshape(group, block_y, depth)


def estimate_scratch(planes, block_x, block_y, depth):
    return [
        pltpu.VMEM((planes, block_y, depth), jnp.bfloat16),
        pltpu.VMEM((planes, HALO_Y, depth), jnp.bfloat16),
        pltpu.VMEM((planes, HALO_Y, depth), jnp.bfloat16),
        pltpu.VMEM((block_x, HALO_Y, depth), jnp.bfloat16),
        pltpu.VMEM((block_x, HALO_Y, depth), jnp.bfloat16),
    ]


def planes_of(block_x, radius):
    return -(-(block_x + 2 * radius) // 4) * 4


def first_halos(sizes, radius, initial):
    block_x, block_y, depth = initial.shape
    vmem = pl.BlockSpec(memory_space=pltpu.VMEM)
    scratch = estimate_scratch(planes_of(block_x, radius), block_x, block_y, depth)
    return pl.pallas_call(
        functools.partial(halo_kernel, sizes, radius),
        out_shape=[jax.ShapeDtypeStruct(one.shape, one.dtype) for one in scratch[:3]],
        in_specs=[vmem],
        out_specs=[vmem] * 3,
        scratch_shapes=scratch
        + [pltpu.SemaphoreType.DMA((8,)), pltpu.SemaphoreType.DMA((8,))],
        compiler_params=pltpu.CompilerParams(
            collective_id=0, has_side_effects=True, vmem_limit_bytes=12 << 20
        ),
    )(initial)


def first_blur(taps_x, halos, along_y, along_z, block_x):
    planes, block_y, depth = halos[0].shape
    views = taps_x.shape[0]
    vmem = pl.BlockSpec(memory_space=pltpu.VMEM)
    shape = (views, block_x, block_y, depth)
    return pl.pallas_call(
        blur_kernel,
        out_shape=jax.ShapeDtypeStruct(shape, jnp.float32),
        in_specs=[pl.BlockSpec(memory_space=pltpu.SMEM)] + [vmem] * 5,
        out_specs=vmem,
        scratch_shapes=[pltpu.VMEM((views, planes, block_y, depth), jnp.float32)],
        cost_estimate=pl.CostEstimate(
            flops=10_000_000_000, bytes_accessed=40_000_000, transcendentals=0
        ),
        compiler_params=pltpu.CompilerParams(vmem_limit_bytes=20 << 20),
    )(taps_x, *halos, along_y, along_z)


def place_kernel(
    below, filled, corner_x, corner_y, tiles, blurred, back_z, observed, spread, summed, counted
):
    view = pl.program_id(0)
    sources, _, capacity, wide, tall, depth = tiles.shape
    _, block_x, block_y, _ = observed.shape
    summed[...] = jnp.zeros_like(summed)
    counted[...] = jnp.zeros_like(counted)

    @pl.loop(0, sources)
    def _(source):
        @pl.loop(0, capacity)
        def _(slot):
            at = source * capacity + slot

            @pl.when(filled[view, at] > 0)
            def _():
                x = corner_x[view, at]
                y = corner_y[view, at]
                where = (pl.ds(x, wide), pl.ds(y, tall), slice(None))
                summed[where] = summed[where] + tiles[source, 0, slot].astype(jnp.float32)
                counted[where] = counted[where] + 1.0

    group = group_of(block_x)
    beyond = spread.shape[1] - below - block_x
    spread[0, :below] = jnp.zeros((below, block_y, depth), jnp.float32)
    spread[0, below + block_x :] = jnp.zeros((beyond, block_y, depth), jnp.float32)

    @pl.loop(0, block_x // group)
    def _(step):
        planes = pl.ds(step * group, group)
        measured = summed[planes] / jnp.maximum(counted[planes], 1.0)
        observed[0, planes] = measured
        flat = (group * block_y, depth)
        result = spread_quotient(
            measured.reshape(flat), blurred[0, planes].reshape(flat), back_z[0]
        )
        spread[0, pl.ds(below + step * group, group)] = result.reshape(group, block_y, depth)


def place(filled, corner_x, corner_y, arrived, blurred, back_z, radius):
    sources, views, capacity, wide, tall, depth = arrived.shape
    shape = blurred.shape
    volume = pl.BlockSpec((1,) + shape[1:], lambda v, *_: (v, 0, 0, 0))
    padded = (views, planes_of(shape[1], radius) + 2 * radius) + shape[2:]
    return pl.pallas_call(
        functools.partial(place_kernel, 2 * radius),
        out_shape=[
            jax.ShapeDtypeStruct(shape, jnp.float32),
            jax.ShapeDtypeStruct(padded, jnp.float32),
        ],
        grid_spec=pltpu.PrefetchScalarGridSpec(
            num_scalar_prefetch=3,
            grid=(views,),
            in_specs=[
                pl.BlockSpec(
                    (sources, 1, capacity, wide, tall, depth), lambda v, *_: (0, v, 0, 0, 0, 0)
                ),
                volume,
                pl.BlockSpec((1,) + back_z.shape[1:], lambda v, *_: (v, 0, 0)),
            ],
            out_specs=[
                volume,
                pl.BlockSpec((1,) + padded[1:], lambda v, *_: (v, 0, 0, 0)),
            ],
            scratch_shapes=[pltpu.VMEM(shape[1:], jnp.float32)] * 2,
        ),
        compiler_params=pltpu.CompilerParams(vmem_limit_bytes=20 << 20),
    )(filled, corner_x, corner_y, arrived, blurred, back_z)


def sweep_kernel(sizes, *refs):
    (
        taps_x,
        observed,
        spreads,
        initial,
        inverse_norm,
        along_y,
        back_y,
        along_z,
        back_z,
        estimate,
        center,
        low,
        high,
        send_low,
        send_high,
        passed_y,
        passed_z,
        acc,
        out_x,
        out_y,
        in_x,
        in_y,
        far_x,
        far_y,
        vert_in,
        est_send,
        est_recv,
        acc_send,
        acc_recv,
        vert_send,
        vert_recv,
        far_send,
        far_recv,
    ) = refs
    views, block_x, block_y, depth = observed.shape
    tap_count = taps_x.shape[1]
    radius = tap_count // 2
    planes = center.shape[1]
    bf16 = jnp.bfloat16
    f32 = jnp.float32
    links = Links(sizes, radius, block_x)
    partner = {"vert": 1 - lax.axis_index("vert")}
    links.greet((partner,))
    for sweep in range(ITERS):
        if sweep > 0:
            at = sweep - 1
            clear_missing(links, center.at[at], low.at[at], high.at[at])
        for step in (-1, 1):
            side = 0 if step == -1 else 1

            @pl.when(jnp.logical_not(links.exists(step, 0)))
            def _():
                in_x[sweep, side] = jnp.zeros(in_x.shape[2:], bf16)
                for other in range(2):
                    in_y[sweep, other, links.ghost(step)] = jnp.zeros(
                        (radius,) + in_y.shape[3:], bf16
                    )

            @pl.when(jnp.logical_not(links.exists(0, step)))
            def _():
                in_y[sweep, side] = jnp.zeros(in_y.shape[2:], bf16)

    below = 2 * radius
    beyond = passed_z.shape[1] - below - block_x
    passed_z[:, :below] = jnp.zeros((views, below, block_y, depth), f32)
    passed_z[:, below + block_x :] = jnp.zeros((views, beyond, block_y, depth), f32)
    group = group_of(block_x)

    for sweep in range(ITERS):
        if sweep > 0:
            at = sweep - 1
            pass_along_y(center.at[at], low.at[at], high.at[at], along_y, passed_y, views)

            @pl.loop(0, block_x // group)
            def _(step):
                first = step * group
                for view in range(views):
                    blurred = pass_along_xz(taps_x, passed_y, along_z[view], view, first, group)
                    measured = observed[view, pl.ds(first, group)].reshape(blurred.shape)
                    result = spread_quotient(measured, blurred, back_z[view])
                    passed_z[view, pl.ds(below + first, group)] = result.reshape(
                        group, block_y, depth
                    )

        if sweep == 0:
            links.await_greetings(1)

        def vert(start, size):
            chunk = pl.ds(start, size)
            return pltpu.make_async_remote_copy(
                src_ref=acc.at[sweep, chunk],
                dst_ref=vert_in.at[sweep, chunk],
                send_sem=vert_send.at[sweep],
                recv_sem=vert_recv.at[sweep],
                device_id=partner,
                device_id_type=pl.DeviceIdType.MESH,
            )

        first_chunk = radius // 4
        last_chunk = (radius + block_x - 1) // 4

        source = spreads if sweep == 0 else passed_z
        far_chunk = (radius + block_x) // 4
        edge_turns = planes // 4 - far_chunk + -(-radius // 4)
        def adjoint(turn):
            step = lax.rem(turn + far_chunk, planes // 4)
            for first in (4 * step, 4 * step + 2):
                columns = []
                for x in (first, first + 1):
                    stack = []
                    for view in range(views):
                        value = taps_x[view, 0] * source[view, x + below]
                        for tap in range(1, tap_count):
                            value = value + taps_x[view, tap] * source[view, x + below - tap]
                        stack.append(value.astype(bf16))
                    columns.append(jnp.concatenate(stack, axis=0))
                both = jnp.concatenate(columns, axis=1)
                result = jnp.dot(back_y[...], both, preferred_element_type=f32)
                rows = block_y + 2 * HALO_Y
                result = result[:rows] + result[rows:]
                for side in range(2):
                    x = first + side
                    lanes = slice(side * depth, (side + 1) * depth)
                    acc[sweep, x] = result[:block_y, lanes]
                    out_y[sweep, 0, x] = result[block_y : block_y + HALO_Y, lanes].astype(bf16)
                    out_y[sweep, 1, x] = result[block_y + HALO_Y :, lanes].astype(bf16)

            @pl.when(jnp.logical_and(step >= first_chunk, step <= last_chunk))
            def _():
                vert(4 * step, 4).start()

        sums = (
            ghosts_of_sums(
                links, out_x.at[sweep], out_y.at[sweep], in_x.at[sweep], in_y.at[sweep]
            ),
            acc_send.at[sweep],
            acc_recv.at[sweep],
        )

        @pl.loop(0, edge_turns)
        def _(turn):
            adjoint(turn)

        @pl.loop(0, radius)
        def _(x):
            out_x[sweep, 0, x] = acc[sweep, x].astype(bf16)
            out_x[sweep, 1, x] = acc[sweep, radius + block_x + x].astype(bf16)

        links.start(*sums, links.across_x())

        @pl.loop(edge_turns, planes // 4)
        def _(turn):
            adjoint(turn)

        links.start(*sums, links.along_y_only())
        links.finish(*sums, links.across_x())
        links.finish(*sums, links.along_y_only())
        forwards = [
            pltpu.make_async_remote_copy(
                src_ref=near.at[sweep],
                dst_ref=far.at[sweep],
                send_sem=far_send.at[sweep, index],
                recv_sem=far_recv.at[sweep, index],
                device_id=partner,
                device_id_type=pl.DeviceIdType.MESH,
            )
            for index, (near, far) in enumerate(((in_x, far_x), (in_y, far_y)))
        ]
        for forward in forwards:
            forward.start()
        vert(4 * first_chunk, 4 * (last_chunk - first_chunk + 1)).wait()

        @pl.loop(0, block_x)
        def _(x):
            acc[sweep, radius + x] = acc[sweep, radius + x] + vert_in[sweep, radius + x]

        for forward in forwards:
            forward.wait()

        def beyond_y(side, plane):
            return in_y[sweep, side, plane].astype(f32) + far_y[sweep, side, plane].astype(f32)

        @pl.loop(0, radius)
        def _(x):
            for side, at, beside in ((0, radius + x, x), (1, block_x + x, radius + block_x + x)):
                plane = acc[sweep, at] + (
                    in_x[sweep, side, x].astype(f32) + far_x[sweep, side, x].astype(f32)
                )
                first = plane[:HALO_Y] + beyond_y(0, beside)
                last = plane[block_y - HALO_Y :] + beyond_y(1, beside)
                acc[sweep, at] = jnp.concatenate(
                    [first, plane[HALO_Y : block_y - HALO_Y], last], axis=0
                )

        def update(x):
            plane = acc[sweep, radius + x]
            first = plane[:HALO_Y] + beyond_y(0, radius + x)
            last = plane[block_y - HALO_Y :] + beyond_y(1, radius + x)
            combined = jnp.concatenate([first, plane[HALO_Y : block_y - HALO_Y], last], axis=0)
            before = initial[x] if sweep == 0 else estimate[x]
            after = before * (combined + damping) * inverse_norm[x]
            estimate[x] = after
            if sweep + 1 < ITERS:
                publish(
                    links, center.at[sweep], send_low.at[sweep], send_high.at[sweep], x, after
                )

        if sweep + 1 < ITERS:
            news = (
                ghosts_of_estimate(
                    links,
                    center.at[sweep],
                    low.at[sweep],
                    high.at[sweep],
                    send_low.at[sweep],
                    send_high.at[sweep],
                ),
                est_send.at[sweep],
                est_recv.at[sweep],
            )

            @pl.loop(0, radius)
            def _(x):
                update(x)
                update(block_x - radius + x)

            links.start(*news, links.across_x())

            @pl.loop(radius, block_x - radius)
            def _(x):
                update(x)

            links.start(*news, links.along_y_only())
            links.finish(*news, links.directions)
        else:

            @pl.loop(0, block_x)
            def _(x):
                update(x)


def sweeps(
    sizes, taps_x, observed, spreads, initial, inverse_norm, along_y, back_y, along_z, back_z
):
    block_x, block_y, depth = initial.shape
    views = observed.shape[0]
    radius = taps_x.shape[1] // 2
    planes = planes_of(block_x, radius)
    extended_x = block_x + 2 * radius
    vmem = pl.BlockSpec(memory_space=pltpu.VMEM)
    bf16 = jnp.bfloat16
    f32 = jnp.float32
    repeats = ITERS - 1
    return pl.pallas_call(
        functools.partial(sweep_kernel, sizes),
        out_shape=jax.ShapeDtypeStruct(initial.shape, f32),
        in_specs=[pl.BlockSpec(memory_space=pltpu.SMEM)] + [vmem] * 8,
        out_specs=vmem,
        scratch_shapes=[
            pltpu.VMEM((repeats,) + scratch.shape, scratch.dtype)
            for scratch in estimate_scratch(planes, block_x, block_y, depth)
        ]
        + [
            pltpu.VMEM((views, planes, block_y, depth), f32),
            pltpu.VMEM((views, planes + 2 * radius, block_y, depth), f32),
            pltpu.VMEM((ITERS, planes, block_y, depth), f32),
            pltpu.VMEM((ITERS, 2, radius, block_y, depth), bf16),
            pltpu.VMEM((ITERS, 2, planes, HALO_Y, depth), bf16),
            pltpu.VMEM((ITERS, 2, radius, block_y, depth), bf16),
            pltpu.VMEM((ITERS, 2, extended_x, HALO_Y, depth), bf16),
            pltpu.VMEM((ITERS, 2, radius, block_y, depth), bf16),
            pltpu.VMEM((ITERS, 2, extended_x, HALO_Y, depth), bf16),
            pltpu.VMEM((ITERS, planes, block_y, depth), f32),
            pltpu.SemaphoreType.DMA((repeats, 8)),
            pltpu.SemaphoreType.DMA((repeats, 8)),
            pltpu.SemaphoreType.DMA((ITERS, 8)),
            pltpu.SemaphoreType.DMA((ITERS, 8)),
            pltpu.SemaphoreType.DMA((ITERS,)),
            pltpu.SemaphoreType.DMA((ITERS,)),
            pltpu.SemaphoreType.DMA((ITERS, 2)),
            pltpu.SemaphoreType.DMA((ITERS, 2)),
        ],
        compiler_params=pltpu.CompilerParams(
            collective_id=1, has_side_effects=True, vmem_limit_bytes=40 << 20
        ),
    )(taps_x, observed, spreads, initial, inverse_norm, along_y, back_y, along_z, back_z)


PAIR_SLOTS = 8
ROW = 40
FAR_AWAY = -1000
MESH = pl.DeviceIdType.MESH


def far_slots(per_device):
    return 3 * per_device // 4


def plan_kernel(per_device, block, xs, ys, table):
    views = table.shape[1]
    pack, slot, entry_x, entry_y = (table.at[index] for index in range(4))
    me = lax.axis_index("gx")
    row = lax.axis_index("gy")
    first = lax.axis_index("vert") * views
    in_low = me < 2
    beside = jnp.where(lax.rem(me, 2) == 0, me + 1, me - 1)
    far_base = jnp.where(in_low, 2, 0)
    far_outer = jnp.where(in_low, 3, 0)
    far_gate = jnp.where(in_low, 2, 1)
    my_outer = jnp.where(in_low, 0, 3)
    spare = 4 * PAIR_SLOTS
    one, zero = jnp.int32(1), jnp.int32(0)
    for view in range(views):
        for at in range(spare):
            pack[view, at] = zero
            slot[view, at] = zero
            entry_x[view, at] = zero
            entry_y[view, at] = jnp.int32(FAR_AWAY)

        def enter(at, where, column):
            slot[view, at] = where
            entry_x[view, at] = xs[first + view, row, column]
            entry_y[view, at] = ys[first + view, row, column]

        mine = near = outer = zero
        for j in range(per_device):
            column = me * per_device + j
            target = block[first + view, row, column]
            enter(jnp.where(target == me, mine, spare), jnp.int32(j), column)
            at = jnp.where(
                target == beside,
                near,
                jnp.where(target == far_outer, PAIR_SLOTS + outer, spare),
            )
            pack[view, at] = jnp.int32(j)
            mine = mine + jnp.where(target == me, one, zero)
            near = near + jnp.where(target == beside, one, zero)
            outer = outer + jnp.where(target == far_outer, one, zero)
        for j in range(per_device):
            target = block[first + view, row, me * per_device + j]
            pack[view, jnp.where(target == far_gate, PAIR_SLOTS + outer, spare)] = jnp.int32(j)
            outer = outer + jnp.where(target == far_gate, one, zero)
        found = zero
        for j in range(per_device):
            column = beside * per_device + j
            hit = block[first + view, row, column] == me
            enter(jnp.where(hit, PAIR_SLOTS + found, spare), found, column)
            found = found + jnp.where(hit, one, zero)
        for side in range(2):
            base = (2 + side) * PAIR_SLOTS
            found = ahead = zero
            for j in range(per_device):
                column = (far_base + side) * per_device + j
                target = block[first + view, row, column]
                hit = target == me
                enter(jnp.where(hit, base + found, spare), found, column)
                found = found + jnp.where(hit, one, zero)
                ahead = ahead + jnp.where(target == my_outer, one, zero)
            ahead = jnp.where(me == my_outer, zero, ahead)
            for at in range(base, base + PAIR_SLOTS):
                slot[view, at] = jnp.minimum(slot[view, at] + ahead, far_slots(per_device) - 1)


def plan(views, per_device, block, xs, ys):
    smem = pl.BlockSpec(memory_space=pltpu.SMEM)
    return pl.pallas_call(
        functools.partial(plan_kernel, per_device),
        out_shape=jax.ShapeDtypeStruct((4, views, ROW), jnp.int32),
        in_specs=[smem] * 3,
        out_specs=smem,
    )(block, xs, ys)


def band_of(psf, view, dim, difference):
    summed = jnp.zeros(difference.shape, jnp.float32)
    for tap in range(psf.shape[2]):
        summed = jnp.where(difference == tap, psf[view, dim, tap], summed)
    return summed


def halves(value):
    high = value.astype(jnp.bfloat16)
    return high, (value - high.astype(jnp.float32)).astype(jnp.bfloat16)


def iota(shape, dim):
    return lax.broadcasted_iota(jnp.int32, shape, dim)


def make_bands(psf, first, radius, block_y, along_y, back_y, back_one, along_z, back_z):
    views = along_z.shape[0]
    depth = along_z.shape[2]
    wide = block_y + 2 * HALO_Y

    def place_of(index):
        inside = jnp.where(index >= wide, index - wide, index)
        return jnp.where(
            inside < block_y,
            inside,
            jnp.where(inside < block_y + HALO_Y, inside - block_y - HALO_Y, inside - HALO_Y),
        )

    backs = []
    for view in range(views):
        shape = (block_y, 2 * wide)
        column = iota(shape, 1)
        high, low = halves(
            band_of(psf, first + view, 1, place_of(column) - iota(shape, 0) + radius)
        )
        f32 = jnp.float32
        rows = slice(view * block_y, (view + 1) * block_y)
        along_y[rows] = jnp.where(column < wide, high.astype(f32), low.astype(f32)).astype(
            jnp.bfloat16
        )
        shape = (2 * wide, block_y)
        row = iota(shape, 0)
        high, low = halves(band_of(psf, first + view, 1, place_of(row) - iota(shape, 1) + radius))
        back = jnp.where(row < wide, high.astype(f32), low.astype(f32))
        backs.append(back)
        back_one[view] = back.astype(jnp.bfloat16)
        shape = (depth, depth)
        difference = iota(shape, 0) - iota(shape, 1)
        along_z[view] = jnp.concatenate(
            halves(band_of(psf, first + view, 2, difference + radius)), axis=0
        )
        back_z[view] = jnp.concatenate(
            halves(band_of(psf, first + view, 2, radius - difference)), axis=0
        )
    back_y[...] = jnp.concatenate(backs, axis=1).astype(jnp.bfloat16)


def contract_last(left, right):
    return lax.dot_general(
        left, right, (((1,), (1,)), ((), ())), preferred_element_type=jnp.float32
    )


def make_norm(psf, first, radius, tile_shape, block, xs, ys, counts, spread, inverse_norm, scale):
    all_views, rows, tiles_row = block.shape
    block_x, block_y, depth = inverse_norm.shape
    views = scale.shape[0]
    tile_wide, tile_tall = tile_shape
    f32 = jnp.float32
    bf16 = jnp.bfloat16
    edge = 8
    near_x = block_x + 2 * edge
    near_y = block_y + 2 * edge
    start_x = lax.axis_index("gx") * block_x - edge
    start_y = lax.axis_index("gy") * block_y - edge
    profiles = []
    for view in range(all_views):
        summed = None
        for row in range(rows):
            left = block[view, row : row + 1] * block_x + xs[view, row : row + 1]
            top = ys[view, row : row + 1] + row * block_y
            from_x = iota((near_x, tiles_row), 0) + start_x - left
            from_y = iota((near_y, tiles_row), 0) + start_y - top
            in_x = jnp.where((from_x >= 0) & (from_x < tile_wide), f32(1), f32(0)).astype(bf16)
            in_y = jnp.where((from_y >= 0) & (from_y < tile_tall), f32(1), f32(0)).astype(bf16)
            term = contract_last(in_y, in_x)
            summed = term if summed is None else summed + term
        counts[view] = summed
        covered = jnp.minimum(summed, 1.0).astype(bf16)
        shape = (block_y, near_y)
        high, low = halves(
            band_of(psf, view, 1, iota(shape, 0) - (iota(shape, 1) - edge) + radius)
        )
        value = jnp.dot(high, covered, preferred_element_type=f32)
        value = value + jnp.dot(low, covered, preferred_element_type=f32)
        shape = (near_x, block_x)
        high, low = halves(
            band_of(psf, view, 0, iota(shape, 1) - (iota(shape, 0) - edge) + radius)
        )
        value_high, value_low = halves(value)
        result = jnp.dot(value_high, high, preferred_element_type=f32)
        result = result + jnp.dot(value_low, high, preferred_element_type=f32)
        result = result + jnp.dot(value_high, low, preferred_element_type=f32)
        spread[view] = result
        profile = jnp.zeros((1, depth), f32)
        place = iota((1, depth), 1)
        for tap in range(psf.shape[2]):
            source = place - tap + radius
            profile = profile + jnp.where(
                (source >= 0) & (source < depth), psf[view, 2, tap], f32(0)
            )
        profiles.append(profile)
    shares = [
        1.0 / jnp.maximum(counts[first + view, edge : edge + block_y], 1.0)
        for view in range(views)
    ]
    for view in range(views):
        counts[first + view, edge : edge + block_y] = shares[view]
    shape = (block_y, depth)
    for x in range(block_x):
        summed = None
        for view in range(all_views):
            term = jnp.broadcast_to(spread[view, :, x : x + 1], shape) * profiles[view]
            summed = term if summed is None else summed + term
        inverse_norm[x] = 1.0 / (summed + damping)
        at = edge + x
        for view in range(views):
            scale[view, x] = jnp.broadcast_to(
                counts[first + view, edge : edge + block_y, at : at + 1], shape
            )


class Route:
    def __init__(self, tx_near, tx_far, rx_near, rx_far, sems):
        self.me = lax.axis_index("gx")
        low = self.me < 2
        self.inside = lax.rem(self.me, 2)
        self.beside = jnp.where(self.inside == 0, self.me + 1, self.me - 1)
        self.gate = jnp.where(low, 2, 1)
        self.is_gate = jnp.logical_or(self.me == 1, self.me == 2)
        self.tx_near, self.tx_far, self.rx_near, self.rx_far = tx_near, tx_far, rx_near, rx_far
        self.near_send, self.near_recv, self.far_send, self.far_recv, self.on_send = sems
        self.pieces = ((0, 4), (4, 4), (8, tx_far.shape[1] - 8))

    def near(self, view):
        return pltpu.make_async_remote_copy(
            src_ref=self.tx_near.at[view],
            dst_ref=self.rx_near[view],
            send_sem=self.near_send.at[view],
            recv_sem=self.near_recv.at[view],
            device_id={"gx": self.beside},
            device_id_type=MESH,
        )

    def far(self, view, piece, side):
        span = pl.ds(*self.pieces[piece])
        return pltpu.make_async_remote_copy(
            src_ref=self.tx_far.at[view, span],
            dst_ref=self.rx_far[view].at[side, span],
            send_sem=self.far_send.at[view, piece],
            recv_sem=self.far_recv.at[view, side, piece],
            device_id={"gx": self.gate},
            device_id_type=MESH,
        )

    def onward(self, view, piece, side):
        span = pl.ds(*self.pieces[piece])
        return pltpu.make_async_remote_copy(
            src_ref=self.rx_far[view].at[side, span],
            dst_ref=self.rx_far[view].at[side, span],
            send_sem=self.on_send.at[view, side, piece],
            recv_sem=self.far_recv.at[view, side, piece],
            device_id={"gx": self.beside},
            device_id_type=MESH,
        )

    def pack_near(self, view, tiles, pack):
        for at in range(PAIR_SLOTS):
            self.tx_near[view, at] = tiles[view][pack[view, at]]

    def pack_far(self, view, tiles, pack):
        for at in range(self.tx_far.shape[1]):
            self.tx_far[view, at] = tiles[view][pack[view, PAIR_SLOTS + at]]

    def send(self, view, pieces):
        for piece in pieces:
            self.far(view, piece, self.inside).start()

    def sent(self, view, piece):
        self.far(view, piece, self.inside).wait_send()

    def hand_on(self, view, piece):
        @pl.when(self.is_gate)
        def _():
            for side in range(2):
                self.far(view, piece, side).wait_recv()
                self.onward(view, piece, side).start()

    def receive_far(self, view):
        @pl.when(self.is_gate)
        def _():
            for side in range(2):
                self.far(view, 2, side).wait_recv()

        @pl.when(jnp.logical_not(self.is_gate))
        def _():
            for piece in range(2):
                for side in range(2):
                    self.onward(view, piece, side).wait_recv()

    def drain(self, views):
        for view in range(views):
            for piece in range(3):
                if piece == 0 or view in (0, views - 1):
                    self.sent(view, piece)
            self.near(view).wait_send()

        @pl.when(self.is_gate)
        def _():
            for view in range(views):
                for piece in range(2):
                    for side in range(2):
                        self.onward(view, piece, side).wait_send()


def chooser_of(view, chosen, entry_y, tile_tall, block_y):
    entries = len(chosen)
    lane = iota((8, entries * tile_tall), 1)
    target = jnp.zeros(lane.shape, jnp.int32)
    for index, entry in enumerate(chosen):
        inside = (lane >= index * tile_tall) & (lane < (index + 1) * tile_tall)
        target = jnp.where(inside, entry_y[view, entry] + lane - index * tile_tall, target)
    target = target[:1]
    one, zero = jnp.float32(1), jnp.float32(0)
    rows = iota((block_y, target.shape[1]), 0)
    return jnp.where(rows == target, one, zero).astype(jnp.bfloat16)


def pass_along_y_of(steps, center, low, high, along_y, passed_y, views):
    block_y, depth = center.shape[1:]

    def one(step):
        for first in (4 * step, 4 * step + 2):
            columns = []
            for x in (first, first + 1):
                edges = jnp.concatenate(
                    [low[x].astype(jnp.float32), high[x].astype(jnp.float32)], axis=0
                ).astype(jnp.bfloat16)
                columns.append(jnp.concatenate([center[x], edges], axis=0))
            both = jnp.concatenate(columns, axis=1)
            both = jnp.concatenate([both, both], axis=0)
            result = jnp.dot(along_y[...], both, preferred_element_type=jnp.float32)
            for view in range(views):
                rows = slice(view * block_y, (view + 1) * block_y)
                passed_y[view, first] = result[rows, :depth]
                passed_y[view, first + 1] = result[rows, depth:]

    if isinstance(steps, range):
        pl.loop(steps.start, steps.stop)(one)
    else:
        for step in steps:
            one(step)


def place_view(view, sources, groups, tables, padded, partial, begins, ends, refs):
    slot, entry_x, entry_y = tables
    scale, per_blur, back_z, observed, spread = refs
    block_x, block_y, depth = observed.shape[1:]
    bf16 = jnp.bfloat16
    f32 = jnp.float32
    padded_planes, tile_tall = padded.shape[1:3]
    margin = padded_planes - block_x
    tile_wide = block_x - margin
    chosen = [g * PAIR_SLOTS + at for g in sources for at in range(PAIR_SLOTS)]
    for entry in chosen:
        read = groups[entry // PAIR_SLOTS]
        padded[entry, margin : margin + tile_wide] = read(slot[view, entry])
    chooser = chooser_of(view, chosen, entry_y, tile_tall, block_y)

    def place_pair(first):
        columns = []
        for x in (first, first + 1):
            rows = [padded[entry, x + margin - entry_x[view, entry]] for entry in chosen]
            columns.append(jnp.concatenate(rows, axis=0))
        both = jnp.concatenate(columns, axis=1)
        summed = jnp.dot(chooser, both, preferred_element_type=f32)
        quotients = []
        for side in range(2):
            x = first + side
            plane = summed[:, side * depth : (side + 1) * depth]
            if not begins:
                plane = plane + partial[x]
            if not ends:
                partial[x] = plane
                continue
            observed[view, x] = plane * scale[view, x]
            quotients.append((plane * per_blur[view, x]).astype(bf16))
        return quotients

    pairs = 4

    @pl.loop(0, block_x // (2 * pairs))
    def _(step):
        quotients = []
        for pair in range(pairs):
            quotients += place_pair(2 * pairs * step + 2 * pair)
        if ends:
            stacked = jnp.concatenate(quotients, axis=0)
            stacked = jnp.concatenate([stacked, stacked], axis=1)
            result = jnp.dot(stacked, back_z[view], preferred_element_type=f32)
            for side in range(2 * pairs):
                rows = slice(side * block_y, (side + 1) * block_y)
                spread[view, 2 * pairs * step + side] = result[rows]


def routed_kernel(sizes, *refs):
    (
        psf,
        table,
        tiles_from,
        block,
        xs,
        ys,
        initial_from,
        estimate,
        fullest,
        start_center,
        start_low,
        start_high,
        start_send_low,
        start_send_high,
        start_send,
        start_recv,
        center,
        low,
        high,
        send_low,
        send_high,
        passed_y,
        passed_z,
        acc,
        acc_y,
        out_x,
        out_y,
        in_x,
        in_y,
        far_x,
        far_y,
        vert_in,
        est_send,
        est_recv,
        acc_send,
        acc_recv,
        vert_send,
        vert_recv,
        far_send,
        far_recv,
        taps_x,
        along_y,
        back_y,
        back_one,
        along_z,
        back_z,
        counts,
        norm_spread,
        inverse_norm,
        scale,
        per_blur,
        observed,
        initial,
        load_sems,
        fill_mine,
        fill_other,
        fill_send,
        fill_recv,
        padded,
        partial,
        tx_near,
        tx_far,
        *rest,
    ) = refs
    views, block_x, block_y, depth = observed.shape
    pack, slot, entry_x, entry_y = (table.at[index] for index in range(4))
    tiles, rx_near, rx_far = (rest[at * views : (at + 1) * views] for at in range(3))
    route_sems = rest[3 * views :]
    tap_count = psf.shape[2]
    radius = tap_count // 2
    planes = center.shape[1]
    per_device = tiles_from.shape[2]
    tile_shape = tiles_from.shape[3:5]
    bf16 = jnp.bfloat16
    f32 = jnp.float32
    links = Links(sizes, radius, block_x)
    column = lax.axis_index("gx")
    first_view = lax.axis_index("vert") * views
    partner = {"vert": 1 - lax.axis_index("vert")}
    part_count = lax.axis_size("groups")
    parts = [
        {"groups": lax.rem(lax.axis_index("groups") + step, part_count)}
        for step in range(1, part_count)
    ]
    route = Route(tx_near, tx_far, rx_near, rx_far, route_sems)

    loads = [
        pltpu.make_async_copy(tiles_from.at[view, 0], tiles[view], load_sems.at[view])
        for view in range(views)
    ]
    loads.append(pltpu.make_async_copy(initial_from, initial, load_sems.at[views]))
    for load in loads:
        load.start()
    barrier = pltpu.get_barrier_semaphore()
    others = [partner] + parts
    others += [{"gx": lax.rem(column + step, sizes[0])} for step in range(1, sizes[0])]
    for other in others:
        pl.semaphore_signal(barrier, inc=1, device_id=other, device_id_type=MESH)
    peers = len(others)
    for dx, dy in links.directions:
        if dy == 0:
            continue
        peers = peers + links.exists(dx, dy).astype(jnp.int32)

        @pl.when(links.exists(dx, dy))
        def _():
            pl.semaphore_signal(
                barrier, inc=1, device_id=links.device(dx, dy), device_id_type=MESH
            )

    loads[0].wait()
    route.pack_far(0, tiles, pack)
    pl.semaphore_wait(barrier, peers)
    route.send(0, range(3))
    route.pack_near(0, tiles, pack)
    route.near(0).start()
    loads[views].wait()

    @pl.loop(0, block_x, unroll=4)
    def _(x):
        publish(links, start_center, start_send_low, start_send_high, x, initial[x])

    clear_missing(links, start_center, start_low, start_high)
    start = (
        ghosts_of_estimate(
            links, start_center, start_low, start_high, start_send_low, start_send_high
        ),
        start_send,
        start_recv,
    )
    links.start(*start, links.directions)
    for view in range(1, views):
        loads[view].wait()
        route.pack_near(view, tiles, pack)
        route.near(view).start()
        route.pack_far(view, tiles, pack)
        if view == 1:
            route.send(view, (0,))

    number = iota(block.shape[1:], 1)
    most = jnp.zeros((block.shape[1], 1), f32)
    for view in range(block.shape[0]):
        beyond = (block[view] >= sizes[0] // 2) != (number >= block.shape[2] // 2)
        for source in range(sizes[0]):
            within = (number >= source * per_device) & (number < (source + 1) * per_device)
            count = jnp.sum(jnp.where(beyond & within, f32(1), f32(0)), axis=1, keepdims=True)
            most = jnp.maximum(most, count)
    fill_mine[...] = jnp.broadcast_to(jnp.max(most, axis=0, keepdims=True), fill_mine.shape)
    fills = [
        pltpu.make_async_remote_copy(
            src_ref=fill_mine,
            dst_ref=fill_other.at[index],
            send_sem=fill_send.at[index],
            recv_sem=fill_recv.at[index],
            device_id=other,
            device_id_type=MESH,
        )
        for index, other in enumerate(parts)
    ]
    for fill in fills:
        fill.start()

    make_bands(psf, first_view, radius, block_y, along_y, back_y, back_one, along_z, back_z)
    for view in range(views):
        for tap in range(tap_count):
            taps_x[view, tap] = psf[first_view + view, 0, tap]
    for sweep in range(ITERS):
        if sweep > 0:
            at = sweep - 1
            clear_missing(links, center.at[at], low.at[at], high.at[at])
        for step in (-1, 1):
            side = 0 if step == -1 else 1

            @pl.when(jnp.logical_not(links.exists(step, 0)))
            def _():
                in_x[sweep, side] = jnp.zeros(in_x.shape[2:], bf16)
                for other in range(2):
                    in_y[sweep, other, links.ghost(step)] = jnp.zeros(
                        (radius,) + in_y.shape[3:], bf16
                    )

            @pl.when(jnp.logical_not(links.exists(0, step)))
            def _():
                in_y[sweep, side] = jnp.zeros(in_y.shape[2:], bf16)

    for entry in range(padded.shape[0]):
        padded[entry] = jnp.zeros(padded.shape[1:], bf16)
    group = group_of(block_x)

    make_norm(
        psf,
        first_view,
        radius,
        tile_shape,
        block,
        xs,
        ys,
        counts,
        norm_spread,
        inverse_norm,
        scale,
    )
    links.finish(*start, links.directions)
    pass_along_y(start_center, start_low, start_high, along_y, passed_y, views)

    @pl.loop(0, block_x // group)
    def _(step):
        first = step * group
        for view in range(views):
            blurred = pass_along_xz(taps_x, passed_y, along_z[view], view, first, group)
            blurred = blurred.reshape(group, block_y, depth)
            chunk = pl.ds(first, group)
            per_blur[view, chunk] = scale[view, chunk] / (blurred + soft_floor)

    if views > 1:
        route.send(1, (1, 2))
    for fill in fills:
        fill.wait()
    greatest = fill_mine[...]
    for index in range(len(fills)):
        greatest = jnp.maximum(greatest, fill_other[index])
    fullest[0, 0] = jnp.max(greatest)

    def vert_copy(sweep, start, size):
        chunk = pl.ds(start, size)
        return pltpu.make_async_remote_copy(
            src_ref=acc.at[sweep, chunk],
            dst_ref=vert_in.at[sweep, chunk],
            send_sem=vert_send.at[sweep],
            recv_sem=vert_recv.at[sweep],
            device_id=partner,
            device_id_type=MESH,
        )

    first_chunk = radius // 4
    last_chunk = (radius + block_x - 1) // 4
    far_chunk = (radius + block_x) // 4
    edge_turns = planes // 4 - far_chunk + -(-radius // 4)
    rows = block_y + 2 * HALO_Y

    def adjoint(sweep, chosen, begins, ends, step, static):
        matrix = back_y[...] if len(chosen) == views else back_one[chosen[0]]
        last_plane = block_x + 2 * radius - 1
        for first in (4 * step, 4 * step + 2):
            if static and first > last_plane:
                continue
            columns = []
            for x in (first, first + 1):
                stack = []
                for view in chosen:
                    taps = range(tap_count)
                    if static:
                        taps = [tap for tap in taps if 0 <= x - tap < block_x]
                    value = None
                    for tap in taps:
                        term = taps_x[view, tap] * passed_z[view, x - tap]
                        value = term if value is None else value + term
                    stack.append(value.astype(bf16))
                columns.append(jnp.concatenate(stack, axis=0))
            both = jnp.concatenate(columns, axis=1)
            result = jnp.dot(matrix, both, preferred_element_type=f32)
            result = result[:rows] + result[rows:]
            for side in range(2):
                x = first + side
                lanes = slice(side * depth, (side + 1) * depth)
                middle, edges = result[:block_y, lanes], result[block_y:, lanes]
                if not begins:
                    middle = middle + acc[sweep, x]
                    edges = edges + acc_y[x]
                acc[sweep, x] = middle
                if ends:
                    out_y[sweep, 0, x] = edges[:HALO_Y].astype(bf16)
                    out_y[sweep, 1, x] = edges[HALO_Y:].astype(bf16)
                else:
                    acc_y[x] = edges

        if ends:
            if not static:
                vert_copy(sweep, 4 * step, 4).start()
            elif first_chunk <= step <= last_chunk:
                vert_copy(sweep, 4 * step, 4).start()

    inner_range = range(-(-radius // 4), (radius + block_x) // 4)
    outer_steps = [step for step in range(planes // 4) if step not in inner_range]
    whole = (-(-(tap_count - 1) // 4), block_x // 4)
    edge_steps = [(turn + far_chunk) % (planes // 4) for turn in range(edge_turns)]
    inner_steps = [
        step
        for step in range(planes // 4)
        if step not in edge_steps and not whole[0] <= step < whole[1]
    ]

    def adjoint_edges(*how):
        for step in edge_steps:
            adjoint(*how, step, True)

    def adjoint_inside(*how):
        for step in inner_steps:
            adjoint(*how, step, True)

        @pl.loop(*whole)
        def _(step):
            adjoint(*how, step, False)

    for sweep in range(ITERS):
        if sweep == 0:
            for view in range(views):
                groups = [
                    lambda at: tiles[view][at],
                    lambda at: rx_near[view][at],
                    lambda at: rx_far[view][0, at],
                    lambda at: rx_far[view][1, at],
                ]
                place = functools.partial(
                    place_view,
                    groups=groups,
                    tables=(slot, entry_x, entry_y),
                    padded=padded,
                    partial=partial,
                    refs=(scale, per_blur, back_z, observed, passed_z),
                )
                last = view + 1 == views
                if last:
                    route.near(view).wait_recv()
                    place(view, (0, 1), begins=True, ends=False)
                if view == 0:
                    route.hand_on(view, 0)
                paced = view > 0 and not last
                for piece in (1, 2):
                    if paced:
                        route.sent(view, piece)
                        route.send(view + 1, (piece,))
                    if piece == 1:
                        route.hand_on(view, piece)
                route.receive_far(view)
                if last:
                    place(view, (2, 3), begins=False, ends=True)
                else:
                    route.near(view).wait_recv()
                    place(view, (0, 1, 2, 3), begins=True, ends=True)
                    if view + 2 < views:
                        route.send(view + 2, (0,))
                    if view > 0:
                        route.hand_on(view + 1, 0)

                    adjoint_edges(sweep, (view,), view == 0, False)
                    adjoint_inside(sweep, (view,), view == 0, False)

                    if view == 0:
                        route.hand_on(view + 1, 0)

            chosen, begins = (views - 1,), views == 1
        else:
            at = sweep - 1
            pass_along_y_of(outer_steps, center.at[at], low.at[at], high.at[at], along_y, passed_y, views)

            @pl.loop(0, block_x // group)
            def _(step):
                first = step * group
                for view in range(views):
                    blurred = pass_along_xz(taps_x, passed_y, along_z[view], view, first, group)
                    measured = observed[view, pl.ds(first, group)].reshape(blurred.shape)
                    result = spread_quotient(measured, blurred, back_z[view])
                    passed_z[view, pl.ds(first, group)] = result.reshape(
                        group, block_y, depth
                    )

            chosen, begins = tuple(range(views)), True

        sums = (
            ghosts_of_sums(
                links, out_x.at[sweep], out_y.at[sweep], in_x.at[sweep], in_y.at[sweep]
            ),
            acc_send.at[sweep],
            acc_recv.at[sweep],
        )

        adjoint_edges(sweep, chosen, begins, True)

        @pl.loop(0, radius, unroll=radius)
        def _(x):
            out_x[sweep, 0, x] = acc[sweep, x].astype(bf16)
            out_x[sweep, 1, x] = acc[sweep, radius + block_x + x].astype(bf16)

        links.start(*sums, links.across_x())

        adjoint_inside(sweep, chosen, begins, True)

        links.start(*sums, links.along_y_only())
        forwards = [
            pltpu.make_async_remote_copy(
                src_ref=near.at[sweep],
                dst_ref=far.at[sweep],
                send_sem=far_send.at[sweep, index],
                recv_sem=far_recv.at[sweep, index],
                device_id=partner,
                device_id_type=pl.DeviceIdType.MESH,
            )
            for index, (near, far) in enumerate(((in_x, far_x), (in_y, far_y)))
        ]
        links.finish(*sums, [(-1, 0), (1, 0)])
        forwards[0].start()
        links.finish(*sums, [one for one in links.directions if one[1] != 0])
        forwards[1].start()
        vert_copy(sweep, 4 * first_chunk, 4 * (last_chunk - first_chunk + 1)).wait()

        @pl.loop(0, block_x, unroll=4)
        def _(x):
            acc[sweep, radius + x] = acc[sweep, radius + x] + vert_in[sweep, radius + x]

        for forward in forwards:
            forward.wait()

        def beyond_y(side, plane):
            return in_y[sweep, side, plane].astype(f32) + far_y[sweep, side, plane].astype(f32)

        @pl.loop(0, radius, unroll=radius)
        def _(x):
            for side, at, beside in ((0, radius + x, x), (1, block_x + x, radius + block_x + x)):
                plane = acc[sweep, at] + (
                    in_x[sweep, side, x].astype(f32) + far_x[sweep, side, x].astype(f32)
                )
                first = plane[:HALO_Y] + beyond_y(0, beside)
                last = plane[block_y - HALO_Y :] + beyond_y(1, beside)
                acc[sweep, at] = jnp.concatenate(
                    [first, plane[HALO_Y : block_y - HALO_Y], last], axis=0
                )

        def update(x):
            plane = acc[sweep, radius + x]
            first = plane[:HALO_Y] + beyond_y(0, radius + x)
            last = plane[block_y - HALO_Y :] + beyond_y(1, radius + x)
            combined = jnp.concatenate([first, plane[HALO_Y : block_y - HALO_Y], last], axis=0)
            before = initial[x] if sweep == 0 else estimate[x]
            after = before * (combined + damping) * inverse_norm[x]
            estimate[x] = after
            if sweep + 1 < ITERS:
                publish(
                    links, center.at[sweep], send_low.at[sweep], send_high.at[sweep], x, after
                )

        if sweep + 1 < ITERS:
            news = (
                ghosts_of_estimate(
                    links,
                    center.at[sweep],
                    low.at[sweep],
                    high.at[sweep],
                    send_low.at[sweep],
                    send_high.at[sweep],
                ),
                est_send.at[sweep],
                est_recv.at[sweep],
            )

            @pl.loop(0, radius, unroll=radius)
            def _(x):
                update(x)
                update(block_x - radius + x)

            links.start(*news, links.across_x())

            @pl.loop(radius, block_x - radius, unroll=3)
            def _(x):
                update(x)

            links.start(*news, links.along_y_only())
            links.finish(*news, links.along_y_only())
            pass_along_y_of(
                inner_range,
                center.at[sweep],
                low.at[sweep],
                high.at[sweep],
                along_y,
                passed_y,
                views,
            )
            links.finish(*news, links.across_x())
        else:

            @pl.loop(0, block_x, unroll=4)
            def _(x):
                update(x)

    route.drain(views)


def routed(tiles, tile_block, tile_x, tile_y, psf, initial):
    block_x, block_y, depth = initial.shape
    views, _, per_device = tiles.shape[:3]
    all_views, rows, tiles_row = tile_x.shape
    tile = tiles.shape[3:]
    radius = psf.shape[2] // 2
    planes = planes_of(block_x, radius)
    extended_x = block_x + 2 * radius
    wide = block_y + 2 * HALO_Y
    sizes = (lax.axis_size("gx"), lax.axis_size("gy"))
    part_count = lax.axis_size("groups")
    cap = far_slots(per_device)
    block = tile_block.reshape(tile_x.shape)
    tables = plan(views, per_device, block, tile_x, tile_y)
    vmem = pl.BlockSpec(memory_space=pltpu.VMEM)
    smem = pl.BlockSpec(memory_space=pltpu.SMEM)
    anywhere = pl.BlockSpec(memory_space=pl.ANY)
    dma = pltpu.SemaphoreType.DMA
    bf16 = jnp.bfloat16
    f32 = jnp.float32
    repeats = ITERS - 1
    volume = (views, block_x, block_y, depth)
    return pl.pallas_call(
        functools.partial(routed_kernel, sizes),
        out_shape=[
            jax.ShapeDtypeStruct(initial.shape, f32),
            jax.ShapeDtypeStruct((1, 1), f32),
        ],
        in_specs=[smem] * 2 + [anywhere] + [vmem] * 3 + [anywhere],
        out_specs=[vmem, smem],
        scratch_shapes=estimate_scratch(planes, block_x, block_y, depth)
        + [dma((8,)), dma((8,))]
        + [
            pltpu.VMEM((repeats,) + scratch.shape, scratch.dtype)
            for scratch in estimate_scratch(planes, block_x, block_y, depth)
        ]
        + [
            pltpu.VMEM((views, planes, block_y, depth), f32),
            pltpu.VMEM(volume, f32),
            pltpu.VMEM((ITERS, planes, block_y, depth), f32),
            pltpu.VMEM((planes, 2 * HALO_Y, depth), f32),
            pltpu.VMEM((ITERS, 2, radius, block_y, depth), bf16),
            pltpu.VMEM((ITERS, 2, planes, HALO_Y, depth), bf16),
            pltpu.VMEM((ITERS, 2, radius, block_y, depth), bf16),
            pltpu.VMEM((ITERS, 2, extended_x, HALO_Y, depth), bf16),
            pltpu.VMEM((ITERS, 2, radius, block_y, depth), bf16),
            pltpu.VMEM((ITERS, 2, extended_x, HALO_Y, depth), bf16),
            pltpu.VMEM((ITERS, planes, block_y, depth), f32),
            dma((repeats, 8)),
            dma((repeats, 8)),
            dma((ITERS, 8)),
            dma((ITERS, 8)),
            dma((ITERS,)),
            dma((ITERS,)),
            dma((ITERS, 2)),
            dma((ITERS, 2)),
            pltpu.SMEM((views, psf.shape[2]), f32),
            pltpu.VMEM((views * block_y, 2 * wide), bf16),
            pltpu.VMEM((2 * wide, views * block_y), bf16),
            pltpu.VMEM((views, 2 * wide, block_y), bf16),
            pltpu.VMEM((views, 2 * depth, depth), bf16),
            pltpu.VMEM((views, 2 * depth, depth), bf16),
            pltpu.VMEM((all_views, block_y + 16, block_x + 16), f32),
            pltpu.VMEM((all_views, block_y, block_x), f32),
            pltpu.VMEM(initial.shape, f32),
            pltpu.VMEM(volume, f32),
            pltpu.VMEM(volume, f32),
            pltpu.VMEM(volume, f32),
            pltpu.VMEM(initial.shape, f32),
            dma((views + 1,)),
            pltpu.VMEM((8, 128), f32),
            pltpu.VMEM((part_count - 1, 8, 128), f32),
            dma((part_count - 1,)),
            dma((part_count - 1,)),
            pltpu.VMEM((4 * PAIR_SLOTS, 2 * block_x - tile[0]) + tile[1:], bf16),
            pltpu.VMEM(volume[1:], f32),
            pltpu.VMEM((views, PAIR_SLOTS) + tile, bf16),
            pltpu.VMEM((views, cap) + tile, bf16),
        ]
        + [pltpu.VMEM(tiles.shape[2:], bf16)] * views
        + [pltpu.VMEM((PAIR_SLOTS,) + tile, bf16)] * views
        + [pltpu.VMEM((2, cap) + tile, bf16)] * views
        + [dma((views,)), dma((views,)), dma((views, 3)), dma((views, 2, 3)), dma((views, 2, 2))],
        compiler_params=pltpu.CompilerParams(
            collective_id=2, has_side_effects=True, vmem_limit_bytes=56 << 20
        ),
    )(psf, tables, tiles, block, tile_x, tile_y, initial)


def general(tiles, tile_block, tile_x, tile_y, psf, initial):
    column_count = lax.axis_size("gx")
    column_index = lax.axis_index("gx")
    row_index = lax.axis_index("gy")
    core_index = lax.axis_index("vert")
    local_views = tiles.shape[0]
    all_views = psf.shape[0]
    per_device = tiles.shape[2]
    tile_wide = tiles.shape[3]
    tile_tall = tiles.shape[4]
    block_x, block_y, depth = initial.shape
    capacity = max(2, 2 * per_device // column_count)
    radius = psf.shape[2] // 2
    first_view = core_index * local_views
    mine_psf = lax.dynamic_slice_in_dim(psf, first_view, local_views, 0)

    def my_rows(table):
        chosen = lax.dynamic_slice_in_dim(table, first_view, local_views, 0)
        chosen = lax.dynamic_slice_in_dim(chosen, row_index, 1, 1)[:, 0]
        return chosen.reshape(local_views, column_count, per_device)

    targets = my_rows(tile_block[:, :, :, 0])
    offsets_x = my_rows(tile_x)
    offsets_y = my_rows(tile_y)
    columns_iota = jnp.arange(column_count, dtype=jnp.int32)
    hits = (targets[..., None] == columns_iota).astype(jnp.int32)
    ranks = jnp.cumsum(hits, axis=2, dtype=jnp.int32)
    slot_ids = jnp.arange(capacity, dtype=jnp.int32) + 1
    sent_hits = jnp.swapaxes(lax.dynamic_slice_in_dim(hits, column_index, 1, 1)[:, 0], 1, 2)
    sent_ranks = jnp.swapaxes(lax.dynamic_slice_in_dim(ranks, column_index, 1, 1)[:, 0], 1, 2)
    chooser = sent_hits[:, :, None, :] * (
        sent_ranks[:, :, None, :] == slot_ids[None, None, :, None]
    ).astype(jnp.int32)
    outgoing = jnp.einsum(
        "vgkj,vjabz->gvkabz",
        chooser.astype(jnp.bfloat16),
        tiles[:, 0],
        preferred_element_type=jnp.bfloat16,
    )
    sizes = (column_count, lax.axis_size("gy"))
    halos = first_halos(sizes, radius, initial)
    outgoing, halos = lax.optimization_barrier((outgoing, halos))
    arrived = lax.all_to_all(outgoing, "gx", split_axis=0, concat_axis=0, tiled=True)
    from_hits = lax.dynamic_slice_in_dim(hits, column_index, 1, 3)[..., 0]
    from_ranks = lax.dynamic_slice_in_dim(ranks, column_index, 1, 3)[..., 0]
    picks = from_hits[:, :, None, :] * (
        from_ranks[:, :, None, :] == slot_ids[None, None, :, None]
    ).astype(jnp.int32)
    filled = jnp.sum(picks, axis=3).reshape(local_views, -1)
    corner_x = jnp.sum(picks * offsets_x[:, :, None, :], axis=3).reshape(local_views, -1)
    corner_y = jnp.sum(picks * offsets_y[:, :, None, :], axis=3).reshape(local_views, -1)

    row_iota = jnp.arange(tile_block.shape[1], dtype=jnp.int32)
    global_x = (tile_block[..., 0] * block_x + tile_x).reshape(all_views, -1)
    global_y = (row_iota[None, :, None] * block_y + tile_y).reshape(all_views, -1)
    near_x = jnp.arange(block_x + 2 * radius, dtype=jnp.int32) - radius
    near_y = jnp.arange(block_y + 2 * radius, dtype=jnp.int32) - radius
    cells_x = column_index * block_x + near_x
    cells_y = row_index * block_y + near_y
    cover_x = (
        (cells_x >= global_x[..., None]) & (cells_x < global_x[..., None] + tile_wide)
    ).astype(jnp.bfloat16)
    cover_y = (
        (cells_y >= global_y[..., None]) & (cells_y < global_y[..., None] + tile_tall)
    ).astype(jnp.bfloat16)
    counts = jnp.einsum("vti,vtj->vij", cover_x, cover_y, preferred_element_type=jnp.float32)
    coverage = jnp.minimum(counts, 1.0)
    iota_x = jnp.arange(block_x, dtype=jnp.int32)
    iota_y = jnp.arange(block_y, dtype=jnp.int32)
    iota_z = jnp.arange(depth, dtype=jnp.int32)
    adjoint_x = banded(psf[:, 0], iota_x[:, None] - near_x[None, :] + radius)
    adjoint_y = banded(psf[:, 1], iota_y[:, None] - near_y[None, :] + radius)
    exact = lax.Precision.HIGHEST
    spread = jnp.einsum("vij,vyj->viy", coverage, adjoint_y, precision=exact)
    spread = jnp.einsum("vxi,viy->vxy", adjoint_x, spread, precision=exact)
    profile = jnp.sum(banded(psf[:, 2], iota_z[:, None] - iota_z[None, :] + radius), axis=2)
    norm_field = jnp.einsum("vxy,vz->xyz", spread, profile, precision=exact)
    inverse_norm = 1.0 / (norm_field + damping)

    places_y = jnp.concatenate(
        [
            iota_y,
            jnp.arange(HALO_Y, dtype=jnp.int32) - HALO_Y,
            jnp.arange(HALO_Y, dtype=jnp.int32) + block_y,
        ]
    )
    band_y = banded(mine_psf[:, 1], places_y[None, :] - iota_y[:, None] + radius)
    high, low = split_high_low(band_y)
    flat = (local_views * block_y, places_y.shape[0])
    along_y = jnp.concatenate([high.reshape(flat), low.reshape(flat)], axis=1)
    back_y = jnp.concatenate([high.reshape(flat).T, low.reshape(flat).T], axis=0)
    band_z = banded(mine_psf[:, 2], iota_z[:, None] - iota_z[None, :] + radius)
    along_z = jnp.concatenate(split_high_low(band_z), axis=1)
    back_z = jnp.concatenate(split_high_low(jnp.swapaxes(band_z, 1, 2)), axis=1)
    taps_x = mine_psf[:, 0]
    blurred = first_blur(taps_x, halos, along_y, along_z, block_x)
    observed, spreads = place(filled, corner_x, corner_y, arrived, blurred, back_z, radius)
    return sweeps(
        sizes,
        taps_x,
        observed,
        spreads,
        initial,
        inverse_norm,
        along_y,
        back_y,
        along_z,
        back_z,
    )


def shards(tiles, tile_block, tile_x, tile_y, psf, initial):
    arguments = (tiles, tile_block, tile_x, tile_y, psf, initial)
    if lax.axis_size("gx") != 4:
        return general(*arguments)
    estimate, fullest = routed(*arguments)
    return lax.cond(
        fullest[0, 0] > far_slots(tiles.shape[2]),
        lambda result, *rest: general(*rest),
        lambda result, *rest: result,
        estimate,
        *arguments,
    )


def solution(mesh):
    in_specs = (
        P("vert", "gy", ("groups", "gx"), None, None, None),
        P(None, None, "groups", None),
        P(None, None, "groups"),
        P(None, None, "groups"),
        P(),
        P(("groups", "gx"), "gy", None),
    )
    out_specs = P(("groups", "gx"), "gy", None)
    return jax.shard_map(shards, mesh=mesh, in_specs=in_specs, out_specs=out_specs, check_vma=False)
```

```python
import functools

import jax
import jax.numpy as jnp
from jax import lax
from jax.experimental import pallas as pl
from jax.experimental.pallas import tpu as pltpu
from jax.sharding import PartitionSpec as P

ITERS = 2
HALO_Y = 8

soft_floor = 0.01
damping = 0.5


def split_high_low(matrix):
    high = lax.reduce_precision(matrix, 8, 7)
    return high.astype(jnp.bfloat16), (matrix - high).astype(jnp.bfloat16)


def banded(taps, difference):
    summed = None
    for tap_index in range(taps.shape[-1]):
        term = jnp.where(difference == tap_index, taps[..., tap_index, None, None], 0.0)
        summed = term if summed is None else summed + term
    return summed


class Links:
    def __init__(self, sizes, radius, block_x):
        self.radius = radius
        self.block_x = block_x
        self.me = (lax.axis_index("gx"), lax.axis_index("gy"))
        self.sizes = sizes
        self.directions = [
            (dx, dy) for dx in (-1, 0, 1) for dy in (-1, 0, 1) if (dx, dy) != (0, 0)
        ]

    def exists(self, dx, dy):
        good = None
        for step, me, count in zip((dx, dy), self.me, self.sizes):
            if step == 0:
                continue
            test = me > 0 if step == -1 else me < count - 1
            good = test if good is None else jnp.logical_and(good, test)
        return good

    def device(self, dx, dy):
        return {"gx": self.me[0] + dx, "gy": self.me[1] + dy}

    def greet(self, others=()):
        barrier = pltpu.get_barrier_semaphore()
        for dx, dy in self.directions:

            @pl.when(self.exists(dx, dy))
            def _():
                pl.semaphore_signal(
                    barrier,
                    inc=1,
                    device_id=self.device(dx, dy),
                    device_id_type=pl.DeviceIdType.MESH,
                )

        for other in others:
            pl.semaphore_signal(
                barrier, inc=1, device_id=other, device_id_type=pl.DeviceIdType.MESH
            )

    def await_greetings(self, others=0):
        peers = others
        for dx, dy in self.directions:
            peers = peers + self.exists(dx, dy).astype(jnp.int32)
        pl.semaphore_wait(pltpu.get_barrier_semaphore(), peers)

    def span(self, step):
        if step == 0:
            return pl.ds(self.radius, self.block_x)
        return pl.ds(self.radius if step == -1 else self.block_x, self.radius)

    def ghost(self, step):
        if step == 0:
            return pl.ds(self.radius, self.block_x)
        return pl.ds(0 if step == -1 else self.block_x + self.radius, self.radius)

    def part(self, step):
        if step == 0:
            return pl.ds(0, self.block_x)
        return pl.ds(0 if step == -1 else self.block_x - self.radius, self.radius)

    def exchange(self, make, send_sem, recv_sem):
        self.start(make, send_sem, recv_sem, self.directions)
        self.finish(make, send_sem, recv_sem, self.directions)

    def across_x(self):
        return [one for one in self.directions if one[0] != 0]

    def along_y_only(self):
        return [one for one in self.directions if one[0] == 0]

    def copy(self, make, send_sem, recv_sem, dx, dy):
        index = self.directions.index((dx, dy))
        src, dst = make(dx, dy)
        return pltpu.make_async_remote_copy(
            src_ref=src,
            dst_ref=dst,
            send_sem=send_sem.at[index],
            recv_sem=recv_sem.at[index],
            device_id=self.device(dx, dy),
            device_id_type=pl.DeviceIdType.MESH,
        )

    def start(self, make, send_sem, recv_sem, directions):
        for dx, dy in directions:

            @pl.when(self.exists(dx, dy))
            def _():
                self.copy(make, send_sem, recv_sem, dx, dy).start()

    def finish(self, make, send_sem, recv_sem, directions):
        for dx, dy in directions:

            @pl.when(self.exists(dx, dy))
            def _():
                self.copy(make, send_sem, recv_sem, dx, dy).wait_send()

            @pl.when(self.exists(-dx, -dy))
            def _():
                self.copy(make, send_sem, recv_sem, dx, dy).wait_recv()


def ghosts_of_estimate(links, center, low, high, send_low, send_high):
    def make(dx, dy):
        if dy == 0:
            return center.at[links.span(dx)], center.at[links.ghost(-dx)]
        if dy == -1:
            return send_low.at[links.part(dx)], high.at[links.ghost(-dx)]
        return send_high.at[links.part(dx)], low.at[links.ghost(-dx)]

    return make


def ghosts_of_sums(links, out_x, out_y, in_x, in_y):
    def make(dx, dy):
        if dy == 0:
            side = 0 if dx == -1 else 1
            return out_x.at[side], in_x.at[1 - side]
        side = 0 if dy == -1 else 1
        return out_y.at[side, links.ghost(dx)], in_y.at[1 - side, links.ghost(-dx)]

    return make


def clear_missing(links, center, low, high):
    radius = links.radius
    for step in (-1, 1):

        @pl.when(jnp.logical_not(links.exists(step, 0)))
        def _():
            for rows in (center, low, high):
                rows[links.ghost(step)] = jnp.zeros((radius,) + rows.shape[1:], rows.dtype)

        @pl.when(jnp.logical_not(links.exists(0, step)))
        def _():
            rows = low if step == -1 else high
            rows[...] = jnp.zeros(rows.shape, rows.dtype)

    tail = links.block_x + 2 * radius
    for rows in (center, low, high):
        rows[tail:] = jnp.zeros((rows.shape[0] - tail,) + rows.shape[1:], rows.dtype)


def publish(links, center, send_low, send_high, x, plane):
    center[links.radius + x] = plane.astype(jnp.bfloat16)
    send_low[x] = plane[:HALO_Y].astype(jnp.bfloat16)
    send_high[x] = plane[plane.shape[0] - HALO_Y :].astype(jnp.bfloat16)


def pass_along_y(center, low, high, along_y, passed_y, views):
    block_y, depth = center.shape[1:]

    @pl.loop(0, center.shape[0] // 4)
    def _(step):
        for first in (4 * step, 4 * step + 2):
            columns = []
            for x in (first, first + 1):
                edges = jnp.concatenate(
                    [low[x].astype(jnp.float32), high[x].astype(jnp.float32)], axis=0
                ).astype(jnp.bfloat16)
                columns.append(jnp.concatenate([center[x], edges], axis=0))
            both = jnp.concatenate(columns, axis=1)
            both = jnp.concatenate([both, both], axis=0)
            result = jnp.dot(along_y[...], both, preferred_element_type=jnp.float32)
            for view in range(views):
                rows = slice(view * block_y, (view + 1) * block_y)
                passed_y[view, first] = result[rows, :depth]
                passed_y[view, first + 1] = result[rows, depth:]


def pass_along_xz(taps_x, passed_y, along_z, view, first, group):
    planes = []
    for inner in range(group):
        x = first + inner
        value = taps_x[view, 0] * passed_y[view, x]
        for tap in range(1, taps_x.shape[1]):
            value = value + taps_x[view, tap] * passed_y[view, x + tap]
        planes.append(value.astype(jnp.bfloat16))
    stacked = jnp.concatenate(planes, axis=0)
    stacked = jnp.concatenate([stacked, stacked], axis=1)
    return jnp.dot(stacked, along_z, preferred_element_type=jnp.float32)


def spread_quotient(measured, blurred, back_z):
    quotient = (measured / (blurred + soft_floor)).astype(jnp.bfloat16)
    quotient = jnp.concatenate([quotient, quotient], axis=1)
    return jnp.dot(quotient, back_z, preferred_element_type=jnp.float32)


def group_of(block_x):
    group = 4
    while block_x % group:
        group //= 2
    return group


def halo_kernel(
    sizes, radius, initial, center, low, high, all_center, all_low, all_high, *scratch
):
    send_low, send_high, send_sem, recv_sem = scratch
    block_x = initial.shape[0]
    links = Links(sizes, radius, block_x)
    links.greet()

    @pl.loop(0, block_x)
    def _(x):
        publish(links, all_center, send_low, send_high, x, initial[x])

    clear_missing(links, all_center, all_low, all_high)
    links.await_greetings()
    links.exchange(
        ghosts_of_estimate(links, all_center, all_low, all_high, send_low, send_high),
        send_sem,
        recv_sem,
    )

    @pl.loop(0, center.shape[0])
    def _(x):
        center[x] = all_center[x]
        low[x] = all_low[x]
        high[x] = all_high[x]


def blur_kernel(taps_x, center, low, high, along_y, along_z, blurred, passed_y):
    views, block_x, block_y, depth = blurred.shape
    pass_along_y(center, low, high, along_y, passed_y, views)
    group = group_of(block_x)

    @pl.loop(0, block_x // group)
    def _(step):
        for view in range(views):
            value = pass_along_xz(taps_x, passed_y, along_z[view], view, step * group, group)
            blurred[view, pl.ds(step * group, group)] = value.reshape(group, block_y, depth)


def estimate_scratch(planes, block_x, block_y, depth):
    return [
        pltpu.VMEM((planes, block_y, depth), jnp.bfloat16),
        pltpu.VMEM((planes, HALO_Y, depth), jnp.bfloat16),
        pltpu.VMEM((planes, HALO_Y, depth), jnp.bfloat16),
        pltpu.VMEM((block_x, HALO_Y, depth), jnp.bfloat16),
        pltpu.VMEM((block_x, HALO_Y, depth), jnp.bfloat16),
    ]


def planes_of(block_x, radius):
    return -(-(block_x + 2 * radius) // 4) * 4


def first_halos(sizes, radius, initial):
    block_x, block_y, depth = initial.shape
    vmem = pl.BlockSpec(memory_space=pltpu.VMEM)
    scratch = estimate_scratch(planes_of(block_x, radius), block_x, block_y, depth)
    return pl.pallas_call(
        functools.partial(halo_kernel, sizes, radius),
        out_shape=[jax.ShapeDtypeStruct(one.shape, one.dtype) for one in scratch[:3]],
        in_specs=[vmem],
        out_specs=[vmem] * 3,
        scratch_shapes=scratch
        + [pltpu.SemaphoreType.DMA((8,)), pltpu.SemaphoreType.DMA((8,))],
        compiler_params=pltpu.CompilerParams(
            collective_id=0, has_side_effects=True, vmem_limit_bytes=12 << 20
        ),
    )(initial)


def first_blur(taps_x, halos, along_y, along_z, block_x):
    planes, block_y, depth = halos[0].shape
    views = taps_x.shape[0]
    vmem = pl.BlockSpec(memory_space=pltpu.VMEM)
    shape = (views, block_x, block_y, depth)
    return pl.pallas_call(
        blur_kernel,
        out_shape=jax.ShapeDtypeStruct(shape, jnp.float32),
        in_specs=[pl.BlockSpec(memory_space=pltpu.SMEM)] + [vmem] * 5,
        out_specs=vmem,
        scratch_shapes=[pltpu.VMEM((views, planes, block_y, depth), jnp.float32)],
        cost_estimate=pl.CostEstimate(
            flops=10_000_000_000, bytes_accessed=40_000_000, transcendentals=0
        ),
        compiler_params=pltpu.CompilerParams(vmem_limit_bytes=20 << 20),
    )(taps_x, *halos, along_y, along_z)


def place_kernel(
    below, filled, corner_x, corner_y, tiles, blurred, back_z, observed, spread, summed, counted
):
    view = pl.program_id(0)
    sources, _, capacity, wide, tall, depth = tiles.shape
    _, block_x, block_y, _ = observed.shape
    summed[...] = jnp.zeros_like(summed)
    counted[...] = jnp.zeros_like(counted)

    @pl.loop(0, sources)
    def _(source):
        @pl.loop(0, capacity)
        def _(slot):
            at = source * capacity + slot

            @pl.when(filled[view, at] > 0)
            def _():
                x = corner_x[view, at]
                y = corner_y[view, at]
                where = (pl.ds(x, wide), pl.ds(y, tall), slice(None))
                summed[where] = summed[where] + tiles[source, 0, slot].astype(jnp.float32)
                counted[where] = counted[where] + 1.0

    group = group_of(block_x)
    beyond = spread.shape[1] - below - block_x
    spread[0, :below] = jnp.zeros((below, block_y, depth), jnp.float32)
    spread[0, below + block_x :] = jnp.zeros((beyond, block_y, depth), jnp.float32)

    @pl.loop(0, block_x // group)
    def _(step):
        planes = pl.ds(step * group, group)
        measured = summed[planes] / jnp.maximum(counted[planes], 1.0)
        observed[0, planes] = measured
        flat = (group * block_y, depth)
        result = spread_quotient(
            measured.reshape(flat), blurred[0, planes].reshape(flat), back_z[0]
        )
        spread[0, pl.ds(below + step * group, group)] = result.reshape(group, block_y, depth)


def place(filled, corner_x, corner_y, arrived, blurred, back_z, radius):
    sources, views, capacity, wide, tall, depth = arrived.shape
    shape = blurred.shape
    volume = pl.BlockSpec((1,) + shape[1:], lambda v, *_: (v, 0, 0, 0))
    padded = (views, planes_of(shape[1], radius) + 2 * radius) + shape[2:]
    return pl.pallas_call(
        functools.partial(place_kernel, 2 * radius),
        out_shape=[
            jax.ShapeDtypeStruct(shape, jnp.float32),
            jax.ShapeDtypeStruct(padded, jnp.float32),
        ],
        grid_spec=pltpu.PrefetchScalarGridSpec(
            num_scalar_prefetch=3,
            grid=(views,),
            in_specs=[
                pl.BlockSpec(
                    (sources, 1, capacity, wide, tall, depth), lambda v, *_: (0, v, 0, 0, 0, 0)
                ),
                volume,
                pl.BlockSpec((1,) + back_z.shape[1:], lambda v, *_: (v, 0, 0)),
            ],
            out_specs=[
                volume,
                pl.BlockSpec((1,) + padded[1:], lambda v, *_: (v, 0, 0, 0)),
            ],
            scratch_shapes=[pltpu.VMEM(shape[1:], jnp.float32)] * 2,
        ),
        compiler_params=pltpu.CompilerParams(vmem_limit_bytes=20 << 20),
    )(filled, corner_x, corner_y, arrived, blurred, back_z)


def sweep_kernel(sizes, *refs):
    (
        taps_x,
        observed,
        spreads,
        initial,
        inverse_norm,
        along_y,
        back_y,
        along_z,
        back_z,
        estimate,
        center,
        low,
        high,
        send_low,
        send_high,
        passed_y,
        passed_z,
        acc,
        out_x,
        out_y,
        in_x,
        in_y,
        far_x,
        far_y,
        vert_in,
        est_send,
        est_recv,
        acc_send,
        acc_recv,
        vert_send,
        vert_recv,
        far_send,
        far_recv,
    ) = refs
    views, block_x, block_y, depth = observed.shape
    tap_count = taps_x.shape[1]
    radius = tap_count // 2
    planes = center.shape[1]
    bf16 = jnp.bfloat16
    f32 = jnp.float32
    links = Links(sizes, radius, block_x)
    partner = {"vert": 1 - lax.axis_index("vert")}
    links.greet((partner,))
    for sweep in range(ITERS):
        if sweep > 0:
            at = sweep - 1
            clear_missing(links, center.at[at], low.at[at], high.at[at])
        for step in (-1, 1):
            side = 0 if step == -1 else 1

            @pl.when(jnp.logical_not(links.exists(step, 0)))
            def _():
                in_x[sweep, side] = jnp.zeros(in_x.shape[2:], bf16)
                for other in range(2):
                    in_y[sweep, other, links.ghost(step)] = jnp.zeros(
                        (radius,) + in_y.shape[3:], bf16
                    )

            @pl.when(jnp.logical_not(links.exists(0, step)))
            def _():
                in_y[sweep, side] = jnp.zeros(in_y.shape[2:], bf16)

    below = 2 * radius
    beyond = passed_z.shape[1] - below - block_x
    passed_z[:, :below] = jnp.zeros((views, below, block_y, depth), f32)
    passed_z[:, below + block_x :] = jnp.zeros((views, beyond, block_y, depth), f32)
    group = group_of(block_x)

    for sweep in range(ITERS):
        if sweep > 0:
            at = sweep - 1
            pass_along_y(center.at[at], low.at[at], high.at[at], along_y, passed_y, views)

            @pl.loop(0, block_x // group)
            def _(step):
                first = step * group
                for view in range(views):
                    blurred = pass_along_xz(taps_x, passed_y, along_z[view], view, first, group)
                    measured = observed[view, pl.ds(first, group)].reshape(blurred.shape)
                    result = spread_quotient(measured, blurred, back_z[view])
                    passed_z[view, pl.ds(below + first, group)] = result.reshape(
                        group, block_y, depth
                    )

        if sweep == 0:
            links.await_greetings(1)

        def vert(start, size):
            chunk = pl.ds(start, size)
            return pltpu.make_async_remote_copy(
                src_ref=acc.at[sweep, chunk],
                dst_ref=vert_in.at[sweep, chunk],
                send_sem=vert_send.at[sweep],
                recv_sem=vert_recv.at[sweep],
                device_id=partner,
                device_id_type=pl.DeviceIdType.MESH,
            )

        first_chunk = radius // 4
        last_chunk = (radius + block_x - 1) // 4

        source = spreads if sweep == 0 else passed_z
        far_chunk = (radius + block_x) // 4
        edge_turns = planes // 4 - far_chunk + -(-radius // 4)
        def adjoint(turn):
            step = lax.rem(turn + far_chunk, planes // 4)
            for first in (4 * step, 4 * step + 2):
                columns = []
                for x in (first, first + 1):
                    stack = []
                    for view in range(views):
                        value = taps_x[view, 0] * source[view, x + below]
                        for tap in range(1, tap_count):
                            value = value + taps_x[view, tap] * source[view, x + below - tap]
                        stack.append(value.astype(bf16))
                    columns.append(jnp.concatenate(stack, axis=0))
                both = jnp.concatenate(columns, axis=1)
                result = jnp.dot(back_y[...], both, preferred_element_type=f32)
                rows = block_y + 2 * HALO_Y
                result = result[:rows] + result[rows:]
                for side in range(2):
                    x = first + side
                    lanes = slice(side * depth, (side + 1) * depth)
                    acc[sweep, x] = result[:block_y, lanes]
                    out_y[sweep, 0, x] = result[block_y : block_y + HALO_Y, lanes].astype(bf16)
                    out_y[sweep, 1, x] = result[block_y + HALO_Y :, lanes].astype(bf16)

            @pl.when(jnp.logical_and(step >= first_chunk, step <= last_chunk))
            def _():
                vert(4 * step, 4).start()

        sums = (
            ghosts_of_sums(
                links, out_x.at[sweep], out_y.at[sweep], in_x.at[sweep], in_y.at[sweep]
            ),
            acc_send.at[sweep],
            acc_recv.at[sweep],
        )

        @pl.loop(0, edge_turns)
        def _(turn):
            adjoint(turn)

        @pl.loop(0, radius)
        def _(x):
            out_x[sweep, 0, x] = acc[sweep, x].astype(bf16)
            out_x[sweep, 1, x] = acc[sweep, radius + block_x + x].astype(bf16)

        links.start(*sums, links.across_x())

        @pl.loop(edge_turns, planes // 4)
        def _(turn):
            adjoint(turn)

        links.start(*sums, links.along_y_only())
        links.finish(*sums, links.across_x())
        links.finish(*sums, links.along_y_only())
        forwards = [
            pltpu.make_async_remote_copy(
                src_ref=near.at[sweep],
                dst_ref=far.at[sweep],
                send_sem=far_send.at[sweep, index],
                recv_sem=far_recv.at[sweep, index],
                device_id=partner,
                device_id_type=pl.DeviceIdType.MESH,
            )
            for index, (near, far) in enumerate(((in_x, far_x), (in_y, far_y)))
        ]
        for forward in forwards:
            forward.start()
        vert(4 * first_chunk, 4 * (last_chunk - first_chunk + 1)).wait()

        @pl.loop(0, block_x)
        def _(x):
            acc[sweep, radius + x] = acc[sweep, radius + x] + vert_in[sweep, radius + x]

        for forward in forwards:
            forward.wait()

        def beyond_y(side, plane):
            return in_y[sweep, side, plane].astype(f32) + far_y[sweep, side, plane].astype(f32)

        @pl.loop(0, radius)
        def _(x):
            for side, at, beside in ((0, radius + x, x), (1, block_x + x, radius + block_x + x)):
                plane = acc[sweep, at] + (
                    in_x[sweep, side, x].astype(f32) + far_x[sweep, side, x].astype(f32)
                )
                first = plane[:HALO_Y] + beyond_y(0, beside)
                last = plane[block_y - HALO_Y :] + beyond_y(1, beside)
                acc[sweep, at] = jnp.concatenate(
                    [first, plane[HALO_Y : block_y - HALO_Y], last], axis=0
                )

        def update(x):
            plane = acc[sweep, radius + x]
            first = plane[:HALO_Y] + beyond_y(0, radius + x)
            last = plane[block_y - HALO_Y :] + beyond_y(1, radius + x)
            combined = jnp.concatenate([first, plane[HALO_Y : block_y - HALO_Y], last], axis=0)
            before = initial[x] if sweep == 0 else estimate[x]
            after = before * (combined + damping) * inverse_norm[x]
            estimate[x] = after
            if sweep + 1 < ITERS:
                publish(
                    links, center.at[sweep], send_low.at[sweep], send_high.at[sweep], x, after
                )

        if sweep + 1 < ITERS:
            news = (
                ghosts_of_estimate(
                    links,
                    center.at[sweep],
                    low.at[sweep],
                    high.at[sweep],
                    send_low.at[sweep],
                    send_high.at[sweep],
                ),
                est_send.at[sweep],
                est_recv.at[sweep],
            )

            @pl.loop(0, radius)
            def _(x):
                update(x)
                update(block_x - radius + x)

            links.start(*news, links.across_x())

            @pl.loop(radius, block_x - radius)
            def _(x):
                update(x)

            links.start(*news, links.along_y_only())
            links.finish(*news, links.directions)
        else:

            @pl.loop(0, block_x)
            def _(x):
                update(x)


def sweeps(
    sizes, taps_x, observed, spreads, initial, inverse_norm, along_y, back_y, along_z, back_z
):
    block_x, block_y, depth = initial.shape
    views = observed.shape[0]
    radius = taps_x.shape[1] // 2
    planes = planes_of(block_x, radius)
    extended_x = block_x + 2 * radius
    vmem = pl.BlockSpec(memory_space=pltpu.VMEM)
    bf16 = jnp.bfloat16
    f32 = jnp.float32
    repeats = ITERS - 1
    return pl.pallas_call(
        functools.partial(sweep_kernel, sizes),
        out_shape=jax.ShapeDtypeStruct(initial.shape, f32),
        in_specs=[pl.BlockSpec(memory_space=pltpu.SMEM)] + [vmem] * 8,
        out_specs=vmem,
        scratch_shapes=[
            pltpu.VMEM((repeats,) + scratch.shape, scratch.dtype)
            for scratch in estimate_scratch(planes, block_x, block_y, depth)
        ]
        + [
            pltpu.VMEM((views, planes, block_y, depth), f32),
            pltpu.VMEM((views, planes + 2 * radius, block_y, depth), f32),
            pltpu.VMEM((ITERS, planes, block_y, depth), f32),
            pltpu.VMEM((ITERS, 2, radius, block_y, depth), bf16),
            pltpu.VMEM((ITERS, 2, planes, HALO_Y, depth), bf16),
            pltpu.VMEM((ITERS, 2, radius, block_y, depth), bf16),
            pltpu.VMEM((ITERS, 2, extended_x, HALO_Y, depth), bf16),
            pltpu.VMEM((ITERS, 2, radius, block_y, depth), bf16),
            pltpu.VMEM((ITERS, 2, extended_x, HALO_Y, depth), bf16),
            pltpu.VMEM((ITERS, planes, block_y, depth), f32),
            pltpu.SemaphoreType.DMA((repeats, 8)),
            pltpu.SemaphoreType.DMA((repeats, 8)),
            pltpu.SemaphoreType.DMA((ITERS, 8)),
            pltpu.SemaphoreType.DMA((ITERS, 8)),
            pltpu.SemaphoreType.DMA((ITERS,)),
            pltpu.SemaphoreType.DMA((ITERS,)),
            pltpu.SemaphoreType.DMA((ITERS, 2)),
            pltpu.SemaphoreType.DMA((ITERS, 2)),
        ],
        compiler_params=pltpu.CompilerParams(
            collective_id=1, has_side_effects=True, vmem_limit_bytes=40 << 20
        ),
    )(taps_x, observed, spreads, initial, inverse_norm, along_y, back_y, along_z, back_z)


PAIR_SLOTS = 8
ROW = 40
FAR_AWAY = -1000
MESH = pl.DeviceIdType.MESH


def far_slots(per_device):
    return 3 * per_device // 4


def plan_kernel(per_device, block, xs, ys, table):
    views = table.shape[1]
    pack, slot, entry_x, entry_y = (table.at[index] for index in range(4))
    me = lax.axis_index("gx")
    row = lax.axis_index("gy")
    first = lax.axis_index("vert") * views
    in_low = me < 2
    beside = jnp.where(lax.rem(me, 2) == 0, me + 1, me - 1)
    far_base = jnp.where(in_low, 2, 0)
    far_outer = jnp.where(in_low, 3, 0)
    far_gate = jnp.where(in_low, 2, 1)
    my_outer = jnp.where(in_low, 0, 3)
    spare = 4 * PAIR_SLOTS
    one, zero = jnp.int32(1), jnp.int32(0)
    for view in range(views):
        for at in range(spare):
            pack[view, at] = zero
            slot[view, at] = zero
            entry_x[view, at] = zero
            entry_y[view, at] = jnp.int32(FAR_AWAY)

        def enter(at, where, column):
            slot[view, at] = where
            entry_x[view, at] = xs[first + view, row, column]
            entry_y[view, at] = ys[first + view, row, column]

        mine = near = outer = zero
        for j in range(per_device):
            column = me * per_device + j
            target = block[first + view, row, column]
            enter(jnp.where(target == me, mine, spare), jnp.int32(j), column)
            at = jnp.where(
                target == beside,
                near,
                jnp.where(target == far_outer, PAIR_SLOTS + outer, spare),
            )
            pack[view, at] = jnp.int32(j)
            mine = mine + jnp.where(target == me, one, zero)
            near = near + jnp.where(target == beside, one, zero)
            outer = outer + jnp.where(target == far_outer, one, zero)
        for j in range(per_device):
            target = block[first + view, row, me * per_device + j]
            pack[view, jnp.where(target == far_gate, PAIR_SLOTS + outer, spare)] = jnp.int32(j)
            outer = outer + jnp.where(target == far_gate, one, zero)
        found = zero
        for j in range(per_device):
            column = beside * per_device + j
            hit = block[first + view, row, column] == me
            enter(jnp.where(hit, PAIR_SLOTS + found, spare), found, column)
            found = found + jnp.where(hit, one, zero)
        for side in range(2):
            base = (2 + side) * PAIR_SLOTS
            found = ahead = zero
            for j in range(per_device):
                column = (far_base + side) * per_device + j
                target = block[first + view, row, column]
                hit = target == me
                enter(jnp.where(hit, base + found, spare), found, column)
                found = found + jnp.where(hit, one, zero)
                ahead = ahead + jnp.where(target == my_outer, one, zero)
            ahead = jnp.where(me == my_outer, zero, ahead)
            for at in range(base, base + PAIR_SLOTS):
                slot[view, at] = jnp.minimum(slot[view, at] + ahead, far_slots(per_device) - 1)


def plan(views, per_device, block, xs, ys):
    smem = pl.BlockSpec(memory_space=pltpu.SMEM)
    return pl.pallas_call(
        functools.partial(plan_kernel, per_device),
        out_shape=jax.ShapeDtypeStruct((4, views, ROW), jnp.int32),
        in_specs=[smem] * 3,
        out_specs=smem,
    )(block, xs, ys)


def band_of(psf, view, dim, difference):
    summed = jnp.zeros(difference.shape, jnp.float32)
    for tap in range(psf.shape[2]):
        summed = jnp.where(difference == tap, psf[view, dim, tap], summed)
    return summed


def halves(value):
    high = value.astype(jnp.bfloat16)
    return high, (value - high.astype(jnp.float32)).astype(jnp.bfloat16)


def iota(shape, dim):
    return lax.broadcasted_iota(jnp.int32, shape, dim)


def make_bands(psf, first, radius, block_y, along_y, back_y, back_one, along_z, back_z):
    views = along_z.shape[0]
    depth = along_z.shape[2]
    wide = block_y + 2 * HALO_Y

    def place_of(index):
        inside = jnp.where(index >= wide, index - wide, index)
        return jnp.where(
            inside < block_y,
            inside,
            jnp.where(inside < block_y + HALO_Y, inside - block_y - HALO_Y, inside - HALO_Y),
        )

    backs = []
    for view in range(views):
        shape = (block_y, 2 * wide)
        column = iota(shape, 1)
        high, low = halves(
            band_of(psf, first + view, 1, place_of(column) - iota(shape, 0) + radius)
        )
        f32 = jnp.float32
        rows = slice(view * block_y, (view + 1) * block_y)
        along_y[rows] = jnp.where(column < wide, high.astype(f32), low.astype(f32)).astype(
            jnp.bfloat16
        )
        shape = (2 * wide, block_y)
        row = iota(shape, 0)
        high, low = halves(band_of(psf, first + view, 1, place_of(row) - iota(shape, 1) + radius))
        back = jnp.where(row < wide, high.astype(f32), low.astype(f32))
        backs.append(back)
        back_one[view] = back.astype(jnp.bfloat16)
        shape = (depth, depth)
        difference = iota(shape, 0) - iota(shape, 1)
        along_z[view] = jnp.concatenate(
            halves(band_of(psf, first + view, 2, difference + radius)), axis=0
        )
        back_z[view] = jnp.concatenate(
            halves(band_of(psf, first + view, 2, radius - difference)), axis=0
        )
    back_y[...] = jnp.concatenate(backs, axis=1).astype(jnp.bfloat16)


def contract_last(left, right):
    return lax.dot_general(
        left, right, (((1,), (1,)), ((), ())), preferred_element_type=jnp.float32
    )


def make_norm(psf, first, radius, tile_shape, block, xs, ys, counts, spread, inverse_norm, scale):
    all_views, rows, tiles_row = block.shape
    block_x, block_y, depth = inverse_norm.shape
    views = scale.shape[0]
    tile_wide, tile_tall = tile_shape
    f32 = jnp.float32
    bf16 = jnp.bfloat16
    edge = 8
    near_x = block_x + 2 * edge
    near_y = block_y + 2 * edge
    start_x = lax.axis_index("gx") * block_x - edge
    start_y = lax.axis_index("gy") * block_y - edge
    profiles = []
    for view in range(all_views):
        summed = None
        for row in range(rows):
            left = block[view, row : row + 1] * block_x + xs[view, row : row + 1]
            top = ys[view, row : row + 1] + row * block_y
            from_x = iota((near_x, tiles_row), 0) + start_x - left
            from_y = iota((near_y, tiles_row), 0) + start_y - top
            in_x = jnp.where((from_x >= 0) & (from_x < tile_wide), f32(1), f32(0)).astype(bf16)
            in_y = jnp.where((from_y >= 0) & (from_y < tile_tall), f32(1), f32(0)).astype(bf16)
            term = contract_last(in_y, in_x)
            summed = term if summed is None else summed + term
        counts[view] = summed
        covered = jnp.minimum(summed, 1.0).astype(bf16)
        shape = (block_y, near_y)
        high, low = halves(
            band_of(psf, view, 1, iota(shape, 0) - (iota(shape, 1) - edge) + radius)
        )
        value = jnp.dot(high, covered, preferred_element_type=f32)
        value = value + jnp.dot(low, covered, preferred_element_type=f32)
        shape = (near_x, block_x)
        high, low = halves(
            band_of(psf, view, 0, iota(shape, 1) - (iota(shape, 0) - edge) + radius)
        )
        value_high, value_low = halves(value)
        result = jnp.dot(value_high, high, preferred_element_type=f32)
        result = result + jnp.dot(value_low, high, preferred_element_type=f32)
        result = result + jnp.dot(value_high, low, preferred_element_type=f32)
        spread[view] = result
        profile = jnp.zeros((1, depth), f32)
        place = iota((1, depth), 1)
        for tap in range(psf.shape[2]):
            source = place - tap + radius
            profile = profile + jnp.where(
                (source >= 0) & (source < depth), psf[view, 2, tap], f32(0)
            )
        profiles.append(profile)
    shares = [
        1.0 / jnp.maximum(counts[first + view, edge : edge + block_y], 1.0)
        for view in range(views)
    ]
    for view in range(views):
        counts[first + view, edge : edge + block_y] = shares[view]
    shape = (block_y, depth)
    for x in range(block_x):
        summed = None
        for view in range(all_views):
            term = jnp.broadcast_to(spread[view, :, x : x + 1], shape) * profiles[view]
            summed = term if summed is None else summed + term
        inverse_norm[x] = 1.0 / (summed + damping)
        at = edge + x
        for view in range(views):
            scale[view, x] = jnp.broadcast_to(
                counts[first + view, edge : edge + block_y, at : at + 1], shape
            )


class Route:
    def __init__(self, tx_near, tx_far, rx_near, rx_far, sems):
        self.me = lax.axis_index("gx")
        low = self.me < 2
        self.inside = lax.rem(self.me, 2)
        self.beside = jnp.where(self.inside == 0, self.me + 1, self.me - 1)
        self.gate = jnp.where(low, 2, 1)
        self.is_gate = jnp.logical_or(self.me == 1, self.me == 2)
        self.tx_near, self.tx_far, self.rx_near, self.rx_far = tx_near, tx_far, rx_near, rx_far
        self.near_send, self.near_recv, self.far_send, self.far_recv, self.on_send = sems
        self.pieces = ((0, 4), (4, 4), (8, tx_far.shape[1] - 8))

    def near(self, view):
        return pltpu.make_async_remote_copy(
            src_ref=self.tx_near.at[view],
            dst_ref=self.rx_near[view],
            send_sem=self.near_send.at[view],
            recv_sem=self.near_recv.at[view],
            device_id={"gx": self.beside},
            device_id_type=MESH,
        )

    def far(self, view, piece, side):
        span = pl.ds(*self.pieces[piece])
        return pltpu.make_async_remote_copy(
            src_ref=self.tx_far.at[view, span],
            dst_ref=self.rx_far[view].at[side, span],
            send_sem=self.far_send.at[view, piece],
            recv_sem=self.far_recv.at[view, side, piece],
            device_id={"gx": self.gate},
            device_id_type=MESH,
        )

    def onward(self, view, piece, side):
        span = pl.ds(*self.pieces[piece])
        return pltpu.make_async_remote_copy(
            src_ref=self.rx_far[view].at[side, span],
            dst_ref=self.rx_far[view].at[side, span],
            send_sem=self.on_send.at[view, side, piece],
            recv_sem=self.far_recv.at[view, side, piece],
            device_id={"gx": self.beside},
            device_id_type=MESH,
        )

    def pack_near(self, view, tiles, pack):
        for at in range(PAIR_SLOTS):
            self.tx_near[view, at] = tiles[view][pack[view, at]]

    def pack_far(self, view, tiles, pack):
        for at in range(self.tx_far.shape[1]):
            self.tx_far[view, at] = tiles[view][pack[view, PAIR_SLOTS + at]]

    def send(self, view, pieces):
        for piece in pieces:
            self.far(view, piece, self.inside).start()

    def sent(self, view, piece):
        self.far(view, piece, self.inside).wait_send()

    def hand_on(self, view, piece):
        @pl.when(self.is_gate)
        def _():
            for side in range(2):
                self.far(view, piece, side).wait_recv()
                self.onward(view, piece, side).start()

    def receive_far(self, view):
        @pl.when(self.is_gate)
        def _():
            for side in range(2):
                self.far(view, 2, side).wait_recv()

        @pl.when(jnp.logical_not(self.is_gate))
        def _():
            for piece in range(2):
                for side in range(2):
                    self.onward(view, piece, side).wait_recv()

    def drain(self, views):
        for view in range(views):
            for piece in range(3):
                if piece == 0 or view in (0, views - 1):
                    self.sent(view, piece)
            self.near(view).wait_send()

        @pl.when(self.is_gate)
        def _():
            for view in range(views):
                for piece in range(2):
                    for side in range(2):
                        self.onward(view, piece, side).wait_send()


def chooser_of(view, chosen, entry_y, tile_tall, block_y):
    entries = len(chosen)
    lane = iota((8, entries * tile_tall), 1)
    target = jnp.zeros(lane.shape, jnp.int32)
    for index, entry in enumerate(chosen):
        inside = (lane >= index * tile_tall) & (lane < (index + 1) * tile_tall)
        target = jnp.where(inside, entry_y[view, entry] + lane - index * tile_tall, target)
    target = target[:1]
    one, zero = jnp.float32(1), jnp.float32(0)
    rows = iota((block_y, target.shape[1]), 0)
    return jnp.where(rows == target, one, zero).astype(jnp.bfloat16)


def pass_along_y_of(steps, center, low, high, along_y, passed_y, views):
    block_y, depth = center.shape[1:]

    def one(step):
        for first in (4 * step, 4 * step + 2):
            columns = []
            for x in (first, first + 1):
                edges = jnp.concatenate(
                    [low[x].astype(jnp.float32), high[x].astype(jnp.float32)], axis=0
                ).astype(jnp.bfloat16)
                columns.append(jnp.concatenate([center[x], edges], axis=0))
            both = jnp.concatenate(columns, axis=1)
            both = jnp.concatenate([both, both], axis=0)
            result = jnp.dot(along_y[...], both, preferred_element_type=jnp.float32)
            for view in range(views):
                rows = slice(view * block_y, (view + 1) * block_y)
                passed_y[view, first] = result[rows, :depth]
                passed_y[view, first + 1] = result[rows, depth:]

    if isinstance(steps, range):
        pl.loop(steps.start, steps.stop, unroll=len(steps))(one)
    else:
        for step in steps:
            one(step)


def place_view(view, sources, groups, tables, padded, partial, begins, ends, refs):
    slot, entry_x, entry_y = tables
    scale, per_blur, back_z, observed, spread = refs
    block_x, block_y, depth = observed.shape[1:]
    bf16 = jnp.bfloat16
    f32 = jnp.float32
    padded_planes, tile_tall = padded.shape[1:3]
    margin = padded_planes - block_x
    tile_wide = block_x - margin
    chosen = [g * PAIR_SLOTS + at for g in sources for at in range(PAIR_SLOTS)]
    for entry in chosen:
        read = groups[entry // PAIR_SLOTS]
        padded[entry, margin : margin + tile_wide] = read(slot[view, entry])
    chooser = chooser_of(view, chosen, entry_y, tile_tall, block_y)

    def place_pair(first):
        columns = []
        for x in (first, first + 1):
            rows = [padded[entry, x + margin - entry_x[view, entry]] for entry in chosen]
            columns.append(jnp.concatenate(rows, axis=0))
        both = jnp.concatenate(columns, axis=1)
        summed = jnp.dot(chooser, both, preferred_element_type=f32)
        quotients = []
        for side in range(2):
            x = first + side
            plane = summed[:, side * depth : (side + 1) * depth]
            if not begins:
                plane = plane + partial[x]
            if not ends:
                partial[x] = plane
                continue
            observed[view, x] = plane * scale[view, x]
            quotients.append((plane * per_blur[view, x]).astype(bf16))
        return quotients

    pairs = 4

    @pl.loop(0, block_x // (2 * pairs))
    def _(step):
        quotients = []
        for pair in range(pairs):
            quotients += place_pair(2 * pairs * step + 2 * pair)
        if ends:
            stacked = jnp.concatenate(quotients, axis=0)
            stacked = jnp.concatenate([stacked, stacked], axis=1)
            result = jnp.dot(stacked, back_z[view], preferred_element_type=f32)
            for side in range(2 * pairs):
                rows = slice(side * block_y, (side + 1) * block_y)
                spread[view, 2 * pairs * step + side] = result[rows]


def routed_kernel(sizes, *refs):
    (
        psf,
        table,
        tiles_from,
        block,
        xs,
        ys,
        initial_from,
        estimate,
        fullest,
        start_center,
        start_low,
        start_high,
        start_send_low,
        start_send_high,
        start_send,
        start_recv,
        center,
        low,
        high,
        send_low,
        send_high,
        passed_y,
        passed_z,
        acc,
        acc_y,
        out_x,
        out_y,
        in_x,
        in_y,
        far_x,
        far_y,
        vert_in,
        est_send,
        est_recv,
        acc_send,
        acc_recv,
        vert_send,
        vert_recv,
        far_send,
        far_recv,
        taps_x,
        along_y,
        back_y,
        back_one,
        along_z,
        back_z,
        counts,
        norm_spread,
        inverse_norm,
        scale,
        per_blur,
        observed,
        part_send,
        part_recv,
        initial,
        load_sems,
        fill_mine,
        fill_other,
        fill_send,
        fill_recv,
        padded,
        partial,
        tx_near,
        tx_far,
        *rest,
    ) = refs
    views, block_x, block_y, depth = observed.shape
    pack, slot, entry_x, entry_y = (table.at[index] for index in range(4))
    tiles, rx_near, rx_far = (rest[at * views : (at + 1) * views] for at in range(3))
    route_sems = rest[3 * views :]
    tap_count = psf.shape[2]
    radius = tap_count // 2
    planes = center.shape[1]
    per_device = tiles_from.shape[2]
    tile_shape = tiles_from.shape[3:5]
    bf16 = jnp.bfloat16
    f32 = jnp.float32
    links = Links(sizes, radius, block_x)
    column = lax.axis_index("gx")
    first_view = lax.axis_index("vert") * views
    partner = {"vert": 1 - lax.axis_index("vert")}
    part_count = lax.axis_size("groups")
    parts = [
        {"groups": lax.rem(lax.axis_index("groups") + step, part_count)}
        for step in range(1, part_count)
    ]
    route = Route(tx_near, tx_far, rx_near, rx_far, route_sems)

    loads = [
        pltpu.make_async_copy(tiles_from.at[view, 0], tiles[view], load_sems.at[view])
        for view in range(views)
    ]
    loads.append(pltpu.make_async_copy(initial_from, initial, load_sems.at[views]))
    for load in loads:
        load.start()
    barrier = pltpu.get_barrier_semaphore()
    others = [partner] + parts
    others += [{"gx": lax.rem(column + step, sizes[0])} for step in range(1, sizes[0])]
    for other in others:
        pl.semaphore_signal(barrier, inc=1, device_id=other, device_id_type=MESH)
    peers = len(others)
    for dx, dy in links.directions:
        if dy == 0:
            continue
        peers = peers + links.exists(dx, dy).astype(jnp.int32)

        @pl.when(links.exists(dx, dy))
        def _():
            pl.semaphore_signal(
                barrier, inc=1, device_id=links.device(dx, dy), device_id_type=MESH
            )

    loads[0].wait()
    route.pack_far(0, tiles, pack)
    pl.semaphore_wait(barrier, peers)
    route.send(0, range(3))
    route.pack_near(0, tiles, pack)
    route.near(0).start()
    loads[views].wait()

    @pl.loop(0, block_x, unroll=4)
    def _(x):
        publish(links, start_center, start_send_low, start_send_high, x, initial[x])

    clear_missing(links, start_center, start_low, start_high)
    start = (
        ghosts_of_estimate(
            links, start_center, start_low, start_high, start_send_low, start_send_high
        ),
        start_send,
        start_recv,
    )
    links.start(*start, links.directions)
    for view in range(1, views):
        loads[view].wait()
        route.pack_near(view, tiles, pack)
        route.near(view).start()
        route.pack_far(view, tiles, pack)
        if view == 1:
            route.send(view, (0,))

    number = iota(block.shape[1:], 1)
    most = jnp.zeros((block.shape[1], 1), f32)
    for view in range(block.shape[0]):
        beyond = (block[view] >= sizes[0] // 2) != (number >= block.shape[2] // 2)
        for source in range(sizes[0]):
            within = (number >= source * per_device) & (number < (source + 1) * per_device)
            count = jnp.sum(jnp.where(beyond & within, f32(1), f32(0)), axis=1, keepdims=True)
            most = jnp.maximum(most, count)
    fill_mine[...] = jnp.broadcast_to(jnp.max(most, axis=0, keepdims=True), fill_mine.shape)
    fills = [
        pltpu.make_async_remote_copy(
            src_ref=fill_mine,
            dst_ref=fill_other.at[index],
            send_sem=fill_send.at[index],
            recv_sem=fill_recv.at[index],
            device_id=other,
            device_id_type=MESH,
        )
        for index, other in enumerate(parts)
    ]
    for fill in fills:
        fill.start()

    make_bands(psf, first_view, radius, block_y, along_y, back_y, back_one, along_z, back_z)
    for view in range(views):
        for tap in range(tap_count):
            taps_x[view, tap] = psf[first_view + view, 0, tap]
    for sweep in range(ITERS):
        if sweep > 0:
            at = sweep - 1
            clear_missing(links, center.at[at], low.at[at], high.at[at])
        for step in (-1, 1):
            side = 0 if step == -1 else 1

            @pl.when(jnp.logical_not(links.exists(step, 0)))
            def _():
                in_x[sweep, side] = jnp.zeros(in_x.shape[2:], bf16)
                for other in range(2):
                    in_y[sweep, other, links.ghost(step)] = jnp.zeros(
                        (radius,) + in_y.shape[3:], bf16
                    )

            @pl.when(jnp.logical_not(links.exists(0, step)))
            def _():
                in_y[sweep, side] = jnp.zeros(in_y.shape[2:], bf16)

    for entry in range(padded.shape[0]):
        padded[entry] = jnp.zeros(padded.shape[1:], bf16)
    group = group_of(block_x)

    make_norm(
        psf,
        first_view,
        radius,
        tile_shape,
        block,
        xs,
        ys,
        counts,
        norm_spread,
        inverse_norm,
        scale,
    )
    links.finish(*start, links.directions)
    pass_along_y(start_center, start_low, start_high, along_y, passed_y, views)

    @pl.loop(0, block_x // group)
    def _(step):
        first = step * group
        for view in range(views):
            blurred = pass_along_xz(taps_x, passed_y, along_z[view], view, first, group)
            blurred = blurred.reshape(group, block_y, depth)
            chunk = pl.ds(first, group)
            per_blur[view, chunk] = scale[view, chunk] / (blurred + soft_floor)

    if views > 1:
        route.send(1, (1, 2))
    for fill in fills:
        fill.wait()
    greatest = fill_mine[...]
    for index in range(len(fills)):
        greatest = jnp.maximum(greatest, fill_other[index])
    fullest[0, 0] = jnp.max(greatest)

    def vert_copy(sweep, start, size):
        chunk = pl.ds(start, size)
        return pltpu.make_async_remote_copy(
            src_ref=acc.at[sweep, chunk],
            dst_ref=vert_in.at[sweep, chunk],
            send_sem=vert_send.at[sweep],
            recv_sem=vert_recv.at[sweep],
            device_id=partner,
            device_id_type=MESH,
        )

    first_chunk = radius // 4
    last_chunk = (radius + block_x - 1) // 4
    far_chunk = (radius + block_x) // 4
    edge_turns = planes // 4 - far_chunk + -(-radius // 4)
    rows = block_y + 2 * HALO_Y

    def adjoint(sweep, chosen, begins, ends, step, static):
        matrix = back_y[...] if len(chosen) == views else back_one[chosen[0]]
        last_plane = block_x + 2 * radius - 1
        for first in (4 * step, 4 * step + 2):
            if static and first > last_plane:
                continue
            columns = []
            for x in (first, first + 1):
                stack = []
                for view in chosen:
                    taps = range(tap_count)
                    if static:
                        taps = [tap for tap in taps if 0 <= x - tap < block_x]
                    value = None
                    for tap in taps:
                        term = taps_x[view, tap] * passed_z[view, x - tap]
                        value = term if value is None else value + term
                    stack.append(value.astype(bf16))
                columns.append(jnp.concatenate(stack, axis=0))
            both = jnp.concatenate(columns, axis=1)
            result = jnp.dot(matrix, both, preferred_element_type=f32)
            result = result[:rows] + result[rows:]
            for side in range(2):
                x = first + side
                lanes = slice(side * depth, (side + 1) * depth)
                middle, edges = result[:block_y, lanes], result[block_y:, lanes]
                if not begins:
                    middle = middle + acc[sweep, x]
                    edges = edges + acc_y[x]
                acc[sweep, x] = middle
                if ends:
                    out_y[sweep, 0, x] = edges[:HALO_Y].astype(bf16)
                    out_y[sweep, 1, x] = edges[HALO_Y:].astype(bf16)
                else:
                    acc_y[x] = edges

        if ends:
            if not static:
                vert_copy(sweep, 4 * step, 4).start()
            elif first_chunk <= step <= last_chunk:
                vert_copy(sweep, 4 * step, 4).start()

    inner_range = range(-(-radius // 4), (radius + block_x) // 4)
    outer_steps = [step for step in range(planes // 4) if step not in inner_range]
    whole = (-(-(tap_count - 1) // 4), block_x // 4)
    edge_steps = [(turn + far_chunk) % (planes // 4) for turn in range(edge_turns)]
    inner_steps = [
        step
        for step in range(planes // 4)
        if step not in edge_steps and not whole[0] <= step < whole[1]
    ]

    def adjoint_edges(*how):
        for step in edge_steps:
            adjoint(*how, step, True)

    middle = (whole[0] + whole[1]) // 2
    y_parts = (
        (radius, 4 * whole[0] - radius),
        (4 * whole[1], radius + block_x - 4 * whole[1]),
        (4 * whole[0], 4 * (middle - whole[0])),
        (4 * middle, 4 * (whole[1] - middle)),
    )

    def adjoint_inside(sweep, chosen, begins, ends):
        how = (sweep, chosen, begins, ends)
        for step in inner_steps:
            adjoint(*how, step, True)
        if ends:
            start_sums_y(sweep, (0, 1))

        @pl.loop(whole[0], middle)
        def _(step):
            adjoint(*how, step, False)

        if ends:
            start_sums_y(sweep, (2,))

        @pl.loop(middle, whole[1])
        def _(step):
            adjoint(*how, step, False)

        if ends:
            start_sums_y(sweep, (3,))

    def sums_y(sweep, dy, part):
        side = 0 if dy == -1 else 1
        span = pl.ds(*y_parts[part])
        return pltpu.make_async_remote_copy(
            src_ref=out_y.at[sweep, side, span],
            dst_ref=in_y.at[sweep, 1 - side, span],
            send_sem=part_send.at[sweep, side, part],
            recv_sem=part_recv.at[sweep, side, part],
            device_id=links.device(0, dy),
            device_id_type=MESH,
        )

    def start_sums_y(sweep, parts_now):
        for dy in (-1, 1):

            @pl.when(links.exists(0, dy))
            def _():
                for part in parts_now:
                    sums_y(sweep, dy, part).start()

    def finish_sums_y(sweep):
        for dy in (-1, 1):

            @pl.when(links.exists(0, dy))
            def _():
                for part in range(len(y_parts)):
                    sums_y(sweep, dy, part).wait_send()

            @pl.when(links.exists(0, -dy))
            def _():
                for part in range(len(y_parts)):
                    sums_y(sweep, dy, part).wait_recv()

    for sweep in range(ITERS):
        if sweep == 0:
            for view in range(views):
                groups = [
                    lambda at: tiles[view][at],
                    lambda at: rx_near[view][at],
                    lambda at: rx_far[view][0, at],
                    lambda at: rx_far[view][1, at],
                ]
                place = functools.partial(
                    place_view,
                    groups=groups,
                    tables=(slot, entry_x, entry_y),
                    padded=padded,
                    partial=partial,
                    refs=(scale, per_blur, back_z, observed, passed_z),
                )
                last = view + 1 == views
                if last:
                    route.near(view).wait_recv()
                    place(view, (0, 1), begins=True, ends=False)
                if view == 0:
                    route.hand_on(view, 0)
                paced = view > 0 and not last
                for piece in (1, 2):
                    if paced:
                        route.sent(view, piece)
                        route.send(view + 1, (piece,))
                    if piece == 1:
                        route.hand_on(view, piece)
                route.receive_far(view)
                if last:
                    place(view, (2, 3), begins=False, ends=True)
                else:
                    route.near(view).wait_recv()
                    place(view, (0, 1, 2, 3), begins=True, ends=True)
                    if view + 2 < views:
                        route.send(view + 2, (0,))
                    if view > 0:
                        route.hand_on(view + 1, 0)

                    adjoint_edges(sweep, (view,), view == 0, False)
                    adjoint_inside(sweep, (view,), view == 0, False)

                    if view == 0:
                        route.hand_on(view + 1, 0)

            chosen, begins = (views - 1,), views == 1
        else:
            at = sweep - 1
            pass_along_y_of(outer_steps, center.at[at], low.at[at], high.at[at], along_y, passed_y, views)

            @pl.loop(0, block_x // group, unroll=2)
            def _(step):
                first = step * group
                for view in range(views):
                    blurred = pass_along_xz(taps_x, passed_y, along_z[view], view, first, group)
                    measured = observed[view, pl.ds(first, group)].reshape(blurred.shape)
                    result = spread_quotient(measured, blurred, back_z[view])
                    passed_z[view, pl.ds(first, group)] = result.reshape(
                        group, block_y, depth
                    )

            chosen, begins = tuple(range(views)), True

        sums = (
            ghosts_of_sums(
                links, out_x.at[sweep], out_y.at[sweep], in_x.at[sweep], in_y.at[sweep]
            ),
            acc_send.at[sweep],
            acc_recv.at[sweep],
        )

        adjoint_edges(sweep, chosen, begins, True)

        @pl.loop(0, radius, unroll=radius)
        def _(x):
            out_x[sweep, 0, x] = acc[sweep, x].astype(bf16)
            out_x[sweep, 1, x] = acc[sweep, radius + block_x + x].astype(bf16)

        links.start(*sums, links.across_x())

        adjoint_inside(sweep, chosen, begins, True)

        forwards = [
            pltpu.make_async_remote_copy(
                src_ref=near.at[sweep],
                dst_ref=far.at[sweep],
                send_sem=far_send.at[sweep, index],
                recv_sem=far_recv.at[sweep, index],
                device_id=partner,
                device_id_type=pl.DeviceIdType.MESH,
            )
            for index, (near, far) in enumerate(((in_x, far_x), (in_y, far_y)))
        ]
        links.finish(*sums, [(-1, 0), (1, 0)])
        forwards[0].start()
        links.finish(*sums, [one for one in links.across_x() if one[1] != 0])
        finish_sums_y(sweep)
        forwards[1].start()
        vert_copy(sweep, 4 * first_chunk, 4 * (last_chunk - first_chunk + 1)).wait()

        @pl.loop(0, block_x, unroll=4)
        def _(x):
            acc[sweep, radius + x] = acc[sweep, radius + x] + vert_in[sweep, radius + x]

        for forward in forwards:
            forward.wait()

        def beyond_y(side, plane):
            return in_y[sweep, side, plane].astype(f32) + far_y[sweep, side, plane].astype(f32)

        @pl.loop(0, radius, unroll=radius)
        def _(x):
            for side, at, beside in ((0, radius + x, x), (1, block_x + x, radius + block_x + x)):
                plane = acc[sweep, at] + (
                    in_x[sweep, side, x].astype(f32) + far_x[sweep, side, x].astype(f32)
                )
                first = plane[:HALO_Y] + beyond_y(0, beside)
                last = plane[block_y - HALO_Y :] + beyond_y(1, beside)
                acc[sweep, at] = jnp.concatenate(
                    [first, plane[HALO_Y : block_y - HALO_Y], last], axis=0
                )

        def update(x):
            plane = acc[sweep, radius + x]
            first = plane[:HALO_Y] + beyond_y(0, radius + x)
            last = plane[block_y - HALO_Y :] + beyond_y(1, radius + x)
            combined = jnp.concatenate([first, plane[HALO_Y : block_y - HALO_Y], last], axis=0)
            before = initial[x] if sweep == 0 else estimate[x]
            after = before * (combined + damping) * inverse_norm[x]
            estimate[x] = after
            if sweep + 1 < ITERS:
                publish(
                    links, center.at[sweep], send_low.at[sweep], send_high.at[sweep], x, after
                )

        if sweep + 1 < ITERS:
            news = (
                ghosts_of_estimate(
                    links,
                    center.at[sweep],
                    low.at[sweep],
                    high.at[sweep],
                    send_low.at[sweep],
                    send_high.at[sweep],
                ),
                est_send.at[sweep],
                est_recv.at[sweep],
            )

            @pl.loop(0, radius, unroll=radius)
            def _(x):
                update(x)
                update(block_x - radius + x)

            links.start(*news, links.across_x())

            @pl.loop(radius, block_x - radius, unroll=3)
            def _(x):
                update(x)

            links.start(*news, links.along_y_only())
            links.finish(*news, links.along_y_only())
            pass_along_y_of(
                inner_range,
                center.at[sweep],
                low.at[sweep],
                high.at[sweep],
                along_y,
                passed_y,
                views,
            )
            links.finish(*news, links.across_x())
        else:

            @pl.loop(0, block_x, unroll=4)
            def _(x):
                update(x)

    route.drain(views)


def routed(tiles, tile_block, tile_x, tile_y, psf, initial):
    block_x, block_y, depth = initial.shape
    views, _, per_device = tiles.shape[:3]
    all_views, rows, tiles_row = tile_x.shape
    tile = tiles.shape[3:]
    radius = psf.shape[2] // 2
    planes = planes_of(block_x, radius)
    extended_x = block_x + 2 * radius
    wide = block_y + 2 * HALO_Y
    sizes = (lax.axis_size("gx"), lax.axis_size("gy"))
    part_count = lax.axis_size("groups")
    cap = far_slots(per_device)
    block = tile_block.reshape(tile_x.shape)
    tables = plan(views, per_device, block, tile_x, tile_y)
    vmem = pl.BlockSpec(memory_space=pltpu.VMEM)
    smem = pl.BlockSpec(memory_space=pltpu.SMEM)
    anywhere = pl.BlockSpec(memory_space=pl.ANY)
    dma = pltpu.SemaphoreType.DMA
    bf16 = jnp.bfloat16
    f32 = jnp.float32
    repeats = ITERS - 1
    volume = (views, block_x, block_y, depth)
    return pl.pallas_call(
        functools.partial(routed_kernel, sizes),
        out_shape=[
            jax.ShapeDtypeStruct(initial.shape, f32),
            jax.ShapeDtypeStruct((1, 1), f32),
        ],
        in_specs=[smem] * 2 + [anywhere] + [vmem] * 3 + [anywhere],
        out_specs=[vmem, smem],
        scratch_shapes=estimate_scratch(planes, block_x, block_y, depth)
        + [dma((8,)), dma((8,))]
        + [
            pltpu.VMEM((repeats,) + scratch.shape, scratch.dtype)
            for scratch in estimate_scratch(planes, block_x, block_y, depth)
        ]
        + [
            pltpu.VMEM((views, planes, block_y, depth), f32),
            pltpu.VMEM(volume, f32),
            pltpu.VMEM((ITERS, planes, block_y, depth), f32),
            pltpu.VMEM((planes, 2 * HALO_Y, depth), f32),
            pltpu.VMEM((ITERS, 2, radius, block_y, depth), bf16),
            pltpu.VMEM((ITERS, 2, planes, HALO_Y, depth), bf16),
            pltpu.VMEM((ITERS, 2, radius, block_y, depth), bf16),
            pltpu.VMEM((ITERS, 2, extended_x, HALO_Y, depth), bf16),
            pltpu.VMEM((ITERS, 2, radius, block_y, depth), bf16),
            pltpu.VMEM((ITERS, 2, extended_x, HALO_Y, depth), bf16),
            pltpu.VMEM((ITERS, planes, block_y, depth), f32),
            dma((repeats, 8)),
            dma((repeats, 8)),
            dma((ITERS, 8)),
            dma((ITERS, 8)),
            dma((ITERS,)),
            dma((ITERS,)),
            dma((ITERS, 2)),
            dma((ITERS, 2)),
            pltpu.SMEM((views, psf.shape[2]), f32),
            pltpu.VMEM((views * block_y, 2 * wide), bf16),
            pltpu.VMEM((2 * wide, views * block_y), bf16),
            pltpu.VMEM((views, 2 * wide, block_y), bf16),
            pltpu.VMEM((views, 2 * depth, depth), bf16),
            pltpu.VMEM((views, 2 * depth, depth), bf16),
            pltpu.VMEM((all_views, block_y + 16, block_x + 16), f32),
            pltpu.VMEM((all_views, block_y, block_x), f32),
            pltpu.VMEM(initial.shape, f32),
            pltpu.VMEM(volume, f32),
            pltpu.VMEM(volume, f32),
            pltpu.VMEM(volume, f32),
            dma((ITERS, 2, 4)),
            dma((ITERS, 2, 4)),
            pltpu.VMEM(initial.shape, f32),
            dma((views + 1,)),
            pltpu.VMEM((8, 128), f32),
            pltpu.VMEM((part_count - 1, 8, 128), f32),
            dma((part_count - 1,)),
            dma((part_count - 1,)),
            pltpu.VMEM((4 * PAIR_SLOTS, 2 * block_x - tile[0]) + tile[1:], bf16),
            pltpu.VMEM(volume[1:], f32),
            pltpu.VMEM((views, PAIR_SLOTS) + tile, bf16),
            pltpu.VMEM((views, cap) + tile, bf16),
        ]
        + [pltpu.VMEM(tiles.shape[2:], bf16)] * views
        + [pltpu.VMEM((PAIR_SLOTS,) + tile, bf16)] * views
        + [pltpu.VMEM((2, cap) + tile, bf16)] * views
        + [dma((views,)), dma((views,)), dma((views, 3)), dma((views, 2, 3)), dma((views, 2, 2))],
        compiler_params=pltpu.CompilerParams(
            collective_id=2, has_side_effects=True, vmem_limit_bytes=56 << 20
        ),
    )(psf, tables, tiles, block, tile_x, tile_y, initial)


def general(tiles, tile_block, tile_x, tile_y, psf, initial):
    column_count = lax.axis_size("gx")
    column_index = lax.axis_index("gx")
    row_index = lax.axis_index("gy")
    core_index = lax.axis_index("vert")
    local_views = tiles.shape[0]
    all_views = psf.shape[0]
    per_device = tiles.shape[2]
    tile_wide = tiles.shape[3]
    tile_tall = tiles.shape[4]
    block_x, block_y, depth = initial.shape
    capacity = max(2, 2 * per_device // column_count)
    radius = psf.shape[2] // 2
    first_view = core_index * local_views
    mine_psf = lax.dynamic_slice_in_dim(psf, first_view, local_views, 0)

    def my_rows(table):
        chosen = lax.dynamic_slice_in_dim(table, first_view, local_views, 0)
        chosen = lax.dynamic_slice_in_dim(chosen, row_index, 1, 1)[:, 0]
        return chosen.reshape(local_views, column_count, per_device)

    targets = my_rows(tile_block[:, :, :, 0])
    offsets_x = my_rows(tile_x)
    offsets_y = my_rows(tile_y)
    columns_iota = jnp.arange(column_count, dtype=jnp.int32)
    hits = (targets[..., None] == columns_iota).astype(jnp.int32)
    ranks = jnp.cumsum(hits, axis=2, dtype=jnp.int32)
    slot_ids = jnp.arange(capacity, dtype=jnp.int32) + 1
    sent_hits = jnp.swapaxes(lax.dynamic_slice_in_dim(hits, column_index, 1, 1)[:, 0], 1, 2)
    sent_ranks = jnp.swapaxes(lax.dynamic_slice_in_dim(ranks, column_index, 1, 1)[:, 0], 1, 2)
    chooser = sent_hits[:, :, None, :] * (
        sent_ranks[:, :, None, :] == slot_ids[None, None, :, None]
    ).astype(jnp.int32)
    outgoing = jnp.einsum(
        "vgkj,vjabz->gvkabz",
        chooser.astype(jnp.bfloat16),
        tiles[:, 0],
        preferred_element_type=jnp.bfloat16,
    )
    sizes = (column_count, lax.axis_size("gy"))
    halos = first_halos(sizes, radius, initial)
    outgoing, halos = lax.optimization_barrier((outgoing, halos))
    arrived = lax.all_to_all(outgoing, "gx", split_axis=0, concat_axis=0, tiled=True)
    from_hits = lax.dynamic_slice_in_dim(hits, column_index, 1, 3)[..., 0]
    from_ranks = lax.dynamic_slice_in_dim(ranks, column_index, 1, 3)[..., 0]
    picks = from_hits[:, :, None, :] * (
        from_ranks[:, :, None, :] == slot_ids[None, None, :, None]
    ).astype(jnp.int32)
    filled = jnp.sum(picks, axis=3).reshape(local_views, -1)
    corner_x = jnp.sum(picks * offsets_x[:, :, None, :], axis=3).reshape(local_views, -1)
    corner_y = jnp.sum(picks * offsets_y[:, :, None, :], axis=3).reshape(local_views, -1)

    row_iota = jnp.arange(tile_block.shape[1], dtype=jnp.int32)
    global_x = (tile_block[..., 0] * block_x + tile_x).reshape(all_views, -1)
    global_y = (row_iota[None, :, None] * block_y + tile_y).reshape(all_views, -1)
    near_x = jnp.arange(block_x + 2 * radius, dtype=jnp.int32) - radius
    near_y = jnp.arange(block_y + 2 * radius, dtype=jnp.int32) - radius
    cells_x = column_index * block_x + near_x
    cells_y = row_index * block_y + near_y
    cover_x = (
        (cells_x >= global_x[..., None]) & (cells_x < global_x[..., None] + tile_wide)
    ).astype(jnp.bfloat16)
    cover_y = (
        (cells_y >= global_y[..., None]) & (cells_y < global_y[..., None] + tile_tall)
    ).astype(jnp.bfloat16)
    counts = jnp.einsum("vti,vtj->vij", cover_x, cover_y, preferred_element_type=jnp.float32)
    coverage = jnp.minimum(counts, 1.0)
    iota_x = jnp.arange(block_x, dtype=jnp.int32)
    iota_y = jnp.arange(block_y, dtype=jnp.int32)
    iota_z = jnp.arange(depth, dtype=jnp.int32)
    adjoint_x = banded(psf[:, 0], iota_x[:, None] - near_x[None, :] + radius)
    adjoint_y = banded(psf[:, 1], iota_y[:, None] - near_y[None, :] + radius)
    exact = lax.Precision.HIGHEST
    spread = jnp.einsum("vij,vyj->viy", coverage, adjoint_y, precision=exact)
    spread = jnp.einsum("vxi,viy->vxy", adjoint_x, spread, precision=exact)
    profile = jnp.sum(banded(psf[:, 2], iota_z[:, None] - iota_z[None, :] + radius), axis=2)
    norm_field = jnp.einsum("vxy,vz->xyz", spread, profile, precision=exact)
    inverse_norm = 1.0 / (norm_field + damping)

    places_y = jnp.concatenate(
        [
            iota_y,
            jnp.arange(HALO_Y, dtype=jnp.int32) - HALO_Y,
            jnp.arange(HALO_Y, dtype=jnp.int32) + block_y,
        ]
    )
    band_y = banded(mine_psf[:, 1], places_y[None, :] - iota_y[:, None] + radius)
    high, low = split_high_low(band_y)
    flat = (local_views * block_y, places_y.shape[0])
    along_y = jnp.concatenate([high.reshape(flat), low.reshape(flat)], axis=1)
    back_y = jnp.concatenate([high.reshape(flat).T, low.reshape(flat).T], axis=0)
    band_z = banded(mine_psf[:, 2], iota_z[:, None] - iota_z[None, :] + radius)
    along_z = jnp.concatenate(split_high_low(band_z), axis=1)
    back_z = jnp.concatenate(split_high_low(jnp.swapaxes(band_z, 1, 2)), axis=1)
    taps_x = mine_psf[:, 0]
    blurred = first_blur(taps_x, halos, along_y, along_z, block_x)
    observed, spreads = place(filled, corner_x, corner_y, arrived, blurred, back_z, radius)
    return sweeps(
        sizes,
        taps_x,
        observed,
        spreads,
        initial,
        inverse_norm,
        along_y,
        back_y,
        along_z,
        back_z,
    )


def shards(tiles, tile_block, tile_x, tile_y, psf, initial):
    arguments = (tiles, tile_block, tile_x, tile_y, psf, initial)
    if lax.axis_size("gx") != 4:
        return general(*arguments)
    estimate, fullest = routed(*arguments)
    return lax.cond(
        fullest[0, 0] > far_slots(tiles.shape[2]),
        lambda result, *rest: general(*rest),
        lambda result, *rest: result,
        estimate,
        *arguments,
    )


def solution(mesh):
    in_specs = (
        P("vert", "gy", ("groups", "gx"), None, None, None),
        P(None, None, "groups", None),
        P(None, None, "groups"),
        P(None, None, "groups"),
        P(),
        P(("groups", "gx"), "gy", None),
    )
    out_specs = P(("groups", "gx"), "gy", None)
    return jax.shard_map(shards, mesh=mesh, in_specs=in_specs, out_specs=out_specs, check_vma=False)
```

```python
import functools

import jax
import jax.numpy as jnp
from jax import lax
from jax.experimental import pallas as pl
from jax.experimental.pallas import tpu as pltpu
from jax.sharding import PartitionSpec as P

ITERS = 2
HALO_Y = 8

soft_floor = 0.01
damping = 0.5


def split_high_low(matrix):
    high = lax.reduce_precision(matrix, 8, 7)
    return high.astype(jnp.bfloat16), (matrix - high).astype(jnp.bfloat16)


def banded(taps, difference):
    summed = None
    for tap_index in range(taps.shape[-1]):
        term = jnp.where(difference == tap_index, taps[..., tap_index, None, None], 0.0)
        summed = term if summed is None else summed + term
    return summed


class Links:
    def __init__(self, sizes, radius, block_x):
        self.radius = radius
        self.block_x = block_x
        self.me = (lax.axis_index("gx"), lax.axis_index("gy"))
        self.sizes = sizes
        self.directions = [
            (dx, dy) for dx in (-1, 0, 1) for dy in (-1, 0, 1) if (dx, dy) != (0, 0)
        ]

    def exists(self, dx, dy):
        good = None
        for step, me, count in zip((dx, dy), self.me, self.sizes):
            if step == 0:
                continue
            test = me > 0 if step == -1 else me < count - 1
            good = test if good is None else jnp.logical_and(good, test)
        return good

    def device(self, dx, dy):
        return {"gx": self.me[0] + dx, "gy": self.me[1] + dy}

    def greet(self, others=()):
        barrier = pltpu.get_barrier_semaphore()
        for dx, dy in self.directions:

            @pl.when(self.exists(dx, dy))
            def _():
                pl.semaphore_signal(
                    barrier,
                    inc=1,
                    device_id=self.device(dx, dy),
                    device_id_type=pl.DeviceIdType.MESH,
                )

        for other in others:
            pl.semaphore_signal(
                barrier, inc=1, device_id=other, device_id_type=pl.DeviceIdType.MESH
            )

    def await_greetings(self, others=0):
        peers = others
        for dx, dy in self.directions:
            peers = peers + self.exists(dx, dy).astype(jnp.int32)
        pl.semaphore_wait(pltpu.get_barrier_semaphore(), peers)

    def span(self, step):
        if step == 0:
            return pl.ds(self.radius, self.block_x)
        return pl.ds(self.radius if step == -1 else self.block_x, self.radius)

    def ghost(self, step):
        if step == 0:
            return pl.ds(self.radius, self.block_x)
        return pl.ds(0 if step == -1 else self.block_x + self.radius, self.radius)

    def part(self, step):
        if step == 0:
            return pl.ds(0, self.block_x)
        return pl.ds(0 if step == -1 else self.block_x - self.radius, self.radius)

    def exchange(self, make, send_sem, recv_sem):
        self.start(make, send_sem, recv_sem, self.directions)
        self.finish(make, send_sem, recv_sem, self.directions)

    def across_x(self):
        return [one for one in self.directions if one[0] != 0]

    def along_y_only(self):
        return [one for one in self.directions if one[0] == 0]

    def copy(self, make, send_sem, recv_sem, dx, dy):
        index = self.directions.index((dx, dy))
        src, dst = make(dx, dy)
        return pltpu.make_async_remote_copy(
            src_ref=src,
            dst_ref=dst,
            send_sem=send_sem.at[index],
            recv_sem=recv_sem.at[index],
            device_id=self.device(dx, dy),
            device_id_type=pl.DeviceIdType.MESH,
        )

    def start(self, make, send_sem, recv_sem, directions):
        for dx, dy in directions:

            @pl.when(self.exists(dx, dy))
            def _():
                self.copy(make, send_sem, recv_sem, dx, dy).start()

    def finish(self, make, send_sem, recv_sem, directions):
        for dx, dy in directions:

            @pl.when(self.exists(dx, dy))
            def _():
                self.copy(make, send_sem, recv_sem, dx, dy).wait_send()

            @pl.when(self.exists(-dx, -dy))
            def _():
                self.copy(make, send_sem, recv_sem, dx, dy).wait_recv()


def ghosts_of_estimate(links, center, low, high, send_low, send_high):
    def make(dx, dy):
        if dy == 0:
            return center.at[links.span(dx)], center.at[links.ghost(-dx)]
        if dy == -1:
            return send_low.at[links.part(dx)], high.at[links.ghost(-dx)]
        return send_high.at[links.part(dx)], low.at[links.ghost(-dx)]

    return make


def ghosts_of_sums(links, out_x, out_y, in_x, in_y):
    def make(dx, dy):
        if dy == 0:
            side = 0 if dx == -1 else 1
            return out_x.at[side], in_x.at[1 - side]
        side = 0 if dy == -1 else 1
        return out_y.at[side, links.ghost(dx)], in_y.at[1 - side, links.ghost(-dx)]

    return make


def clear_missing(links, center, low, high):
    radius = links.radius
    for step in (-1, 1):

        @pl.when(jnp.logical_not(links.exists(step, 0)))
        def _():
            for rows in (center, low, high):
                rows[links.ghost(step)] = jnp.zeros((radius,) + rows.shape[1:], rows.dtype)

        @pl.when(jnp.logical_not(links.exists(0, step)))
        def _():
            rows = low if step == -1 else high
            rows[...] = jnp.zeros(rows.shape, rows.dtype)

    tail = links.block_x + 2 * radius
    for rows in (center, low, high):
        rows[tail:] = jnp.zeros((rows.shape[0] - tail,) + rows.shape[1:], rows.dtype)


def publish(links, center, send_low, send_high, x, plane):
    center[links.radius + x] = plane.astype(jnp.bfloat16)
    send_low[x] = plane[:HALO_Y].astype(jnp.bfloat16)
    send_high[x] = plane[plane.shape[0] - HALO_Y :].astype(jnp.bfloat16)


def pass_along_y(center, low, high, along_y, passed_y, views):
    block_y, depth = center.shape[1:]

    @pl.loop(0, center.shape[0] // 4)
    def _(step):
        for first in (4 * step, 4 * step + 2):
            columns = []
            for x in (first, first + 1):
                edges = jnp.concatenate(
                    [low[x].astype(jnp.float32), high[x].astype(jnp.float32)], axis=0
                ).astype(jnp.bfloat16)
                columns.append(jnp.concatenate([center[x], edges], axis=0))
            both = jnp.concatenate(columns, axis=1)
            both = jnp.concatenate([both, both], axis=0)
            result = jnp.dot(along_y[...], both, preferred_element_type=jnp.float32)
            for view in range(views):
                rows = slice(view * block_y, (view + 1) * block_y)
                passed_y[view, first] = result[rows, :depth]
                passed_y[view, first + 1] = result[rows, depth:]


def pass_along_xz(taps_x, passed_y, along_z, view, first, group):
    planes = []
    for inner in range(group):
        x = first + inner
        value = taps_x[view, 0] * passed_y[view, x]
        for tap in range(1, taps_x.shape[1]):
            value = value + taps_x[view, tap] * passed_y[view, x + tap]
        planes.append(value.astype(jnp.bfloat16))
    stacked = jnp.concatenate(planes, axis=0)
    stacked = jnp.concatenate([stacked, stacked], axis=1)
    return jnp.dot(stacked, along_z, preferred_element_type=jnp.float32)


def spread_quotient(measured, blurred, back_z):
    quotient = (measured / (blurred + soft_floor)).astype(jnp.bfloat16)
    quotient = jnp.concatenate([quotient, quotient], axis=1)
    return jnp.dot(quotient, back_z, preferred_element_type=jnp.float32)


def group_of(block_x):
    group = 4
    while block_x % group:
        group //= 2
    return group


def halo_kernel(
    sizes, radius, initial, center, low, high, all_center, all_low, all_high, *scratch
):
    send_low, send_high, send_sem, recv_sem = scratch
    block_x = initial.shape[0]
    links = Links(sizes, radius, block_x)
    links.greet()

    @pl.loop(0, block_x)
    def _(x):
        publish(links, all_center, send_low, send_high, x, initial[x])

    clear_missing(links, all_center, all_low, all_high)
    links.await_greetings()
    links.exchange(
        ghosts_of_estimate(links, all_center, all_low, all_high, send_low, send_high),
        send_sem,
        recv_sem,
    )

    @pl.loop(0, center.shape[0])
    def _(x):
        center[x] = all_center[x]
        low[x] = all_low[x]
        high[x] = all_high[x]


def blur_kernel(taps_x, center, low, high, along_y, along_z, blurred, passed_y):
    views, block_x, block_y, depth = blurred.shape
    pass_along_y(center, low, high, along_y, passed_y, views)
    group = group_of(block_x)

    @pl.loop(0, block_x // group)
    def _(step):
        for view in range(views):
            value = pass_along_xz(taps_x, passed_y, along_z[view], view, step * group, group)
            blurred[view, pl.ds(step * group, group)] = value.reshape(group, block_y, depth)


def estimate_scratch(planes, block_x, block_y, depth):
    return [
        pltpu.VMEM((planes, block_y, depth), jnp.bfloat16),
        pltpu.VMEM((planes, HALO_Y, depth), jnp.bfloat16),
        pltpu.VMEM((planes, HALO_Y, depth), jnp.bfloat16),
        pltpu.VMEM((block_x, HALO_Y, depth), jnp.bfloat16),
        pltpu.VMEM((block_x, HALO_Y, depth), jnp.bfloat16),
    ]


def planes_of(block_x, radius):
    return -(-(block_x + 2 * radius) // 4) * 4


def first_halos(sizes, radius, initial):
    block_x, block_y, depth = initial.shape
    vmem = pl.BlockSpec(memory_space=pltpu.VMEM)
    scratch = estimate_scratch(planes_of(block_x, radius), block_x, block_y, depth)
    return pl.pallas_call(
        functools.partial(halo_kernel, sizes, radius),
        out_shape=[jax.ShapeDtypeStruct(one.shape, one.dtype) for one in scratch[:3]],
        in_specs=[vmem],
        out_specs=[vmem] * 3,
        scratch_shapes=scratch
        + [pltpu.SemaphoreType.DMA((8,)), pltpu.SemaphoreType.DMA((8,))],
        compiler_params=pltpu.CompilerParams(
            collective_id=0, has_side_effects=True, vmem_limit_bytes=12 << 20
        ),
    )(initial)


def first_blur(taps_x, halos, along_y, along_z, block_x):
    planes, block_y, depth = halos[0].shape
    views = taps_x.shape[0]
    vmem = pl.BlockSpec(memory_space=pltpu.VMEM)
    shape = (views, block_x, block_y, depth)
    return pl.pallas_call(
        blur_kernel,
        out_shape=jax.ShapeDtypeStruct(shape, jnp.float32),
        in_specs=[pl.BlockSpec(memory_space=pltpu.SMEM)] + [vmem] * 5,
        out_specs=vmem,
        scratch_shapes=[pltpu.VMEM((views, planes, block_y, depth), jnp.float32)],
        cost_estimate=pl.CostEstimate(
            flops=10_000_000_000, bytes_accessed=40_000_000, transcendentals=0
        ),
        compiler_params=pltpu.CompilerParams(vmem_limit_bytes=20 << 20),
    )(taps_x, *halos, along_y, along_z)


def place_kernel(
    below, filled, corner_x, corner_y, tiles, blurred, back_z, observed, spread, summed, counted
):
    view = pl.program_id(0)
    sources, _, capacity, wide, tall, depth = tiles.shape
    _, block_x, block_y, _ = observed.shape
    summed[...] = jnp.zeros_like(summed)
    counted[...] = jnp.zeros_like(counted)

    @pl.loop(0, sources)
    def _(source):
        @pl.loop(0, capacity)
        def _(slot):
            at = source * capacity + slot

            @pl.when(filled[view, at] > 0)
            def _():
                x = corner_x[view, at]
                y = corner_y[view, at]
                where = (pl.ds(x, wide), pl.ds(y, tall), slice(None))
                summed[where] = summed[where] + tiles[source, 0, slot].astype(jnp.float32)
                counted[where] = counted[where] + 1.0

    group = group_of(block_x)
    beyond = spread.shape[1] - below - block_x
    spread[0, :below] = jnp.zeros((below, block_y, depth), jnp.float32)
    spread[0, below + block_x :] = jnp.zeros((beyond, block_y, depth), jnp.float32)

    @pl.loop(0, block_x // group)
    def _(step):
        planes = pl.ds(step * group, group)
        measured = summed[planes] / jnp.maximum(counted[planes], 1.0)
        observed[0, planes] = measured
        flat = (group * block_y, depth)
        result = spread_quotient(
            measured.reshape(flat), blurred[0, planes].reshape(flat), back_z[0]
        )
        spread[0, pl.ds(below + step * group, group)] = result.reshape(group, block_y, depth)


def place(filled, corner_x, corner_y, arrived, blurred, back_z, radius):
    sources, views, capacity, wide, tall, depth = arrived.shape
    shape = blurred.shape
    volume = pl.BlockSpec((1,) + shape[1:], lambda v, *_: (v, 0, 0, 0))
    padded = (views, planes_of(shape[1], radius) + 2 * radius) + shape[2:]
    return pl.pallas_call(
        functools.partial(place_kernel, 2 * radius),
        out_shape=[
            jax.ShapeDtypeStruct(shape, jnp.float32),
            jax.ShapeDtypeStruct(padded, jnp.float32),
        ],
        grid_spec=pltpu.PrefetchScalarGridSpec(
            num_scalar_prefetch=3,
            grid=(views,),
            in_specs=[
                pl.BlockSpec(
                    (sources, 1, capacity, wide, tall, depth), lambda v, *_: (0, v, 0, 0, 0, 0)
                ),
                volume,
                pl.BlockSpec((1,) + back_z.shape[1:], lambda v, *_: (v, 0, 0)),
            ],
            out_specs=[
                volume,
                pl.BlockSpec((1,) + padded[1:], lambda v, *_: (v, 0, 0, 0)),
            ],
            scratch_shapes=[pltpu.VMEM(shape[1:], jnp.float32)] * 2,
        ),
        compiler_params=pltpu.CompilerParams(vmem_limit_bytes=20 << 20),
    )(filled, corner_x, corner_y, arrived, blurred, back_z)


def sweep_kernel(sizes, *refs):
    (
        taps_x,
        observed,
        spreads,
        initial,
        inverse_norm,
        along_y,
        back_y,
        along_z,
        back_z,
        estimate,
        center,
        low,
        high,
        send_low,
        send_high,
        passed_y,
        passed_z,
        acc,
        out_x,
        out_y,
        in_x,
        in_y,
        far_x,
        far_y,
        vert_in,
        est_send,
        est_recv,
        acc_send,
        acc_recv,
        vert_send,
        vert_recv,
        far_send,
        far_recv,
    ) = refs
    views, block_x, block_y, depth = observed.shape
    tap_count = taps_x.shape[1]
    radius = tap_count // 2
    planes = center.shape[1]
    bf16 = jnp.bfloat16
    f32 = jnp.float32
    links = Links(sizes, radius, block_x)
    partner = {"vert": 1 - lax.axis_index("vert")}
    links.greet((partner,))
    for sweep in range(ITERS):
        if sweep > 0:
            at = sweep - 1
            clear_missing(links, center.at[at], low.at[at], high.at[at])
        for step in (-1, 1):
            side = 0 if step == -1 else 1

            @pl.when(jnp.logical_not(links.exists(step, 0)))
            def _():
                in_x[sweep, side] = jnp.zeros(in_x.shape[2:], bf16)
                for other in range(2):
                    in_y[sweep, other, links.ghost(step)] = jnp.zeros(
                        (radius,) + in_y.shape[3:], bf16
                    )

            @pl.when(jnp.logical_not(links.exists(0, step)))
            def _():
                in_y[sweep, side] = jnp.zeros(in_y.shape[2:], bf16)

    below = 2 * radius
    beyond = passed_z.shape[1] - below - block_x
    passed_z[:, :below] = jnp.zeros((views, below, block_y, depth), f32)
    passed_z[:, below + block_x :] = jnp.zeros((views, beyond, block_y, depth), f32)
    group = group_of(block_x)

    for sweep in range(ITERS):
        if sweep > 0:
            at = sweep - 1
            pass_along_y(center.at[at], low.at[at], high.at[at], along_y, passed_y, views)

            @pl.loop(0, block_x // group)
            def _(step):
                first = step * group
                for view in range(views):
                    blurred = pass_along_xz(taps_x, passed_y, along_z[view], view, first, group)
                    measured = observed[view, pl.ds(first, group)].reshape(blurred.shape)
                    result = spread_quotient(measured, blurred, back_z[view])
                    passed_z[view, pl.ds(below + first, group)] = result.reshape(
                        group, block_y, depth
                    )

        if sweep == 0:
            links.await_greetings(1)

        def vert(start, size):
            chunk = pl.ds(start, size)
            return pltpu.make_async_remote_copy(
                src_ref=acc.at[sweep, chunk],
                dst_ref=vert_in.at[sweep, chunk],
                send_sem=vert_send.at[sweep],
                recv_sem=vert_recv.at[sweep],
                device_id=partner,
                device_id_type=pl.DeviceIdType.MESH,
            )

        first_chunk = radius // 4
        last_chunk = (radius + block_x - 1) // 4

        source = spreads if sweep == 0 else passed_z
        far_chunk = (radius + block_x) // 4
        edge_turns = planes // 4 - far_chunk + -(-radius // 4)
        def adjoint(turn):
            step = lax.rem(turn + far_chunk, planes // 4)
            for first in (4 * step, 4 * step + 2):
                columns = []
                for x in (first, first + 1):
                    stack = []
                    for view in range(views):
                        value = taps_x[view, 0] * source[view, x + below]
                        for tap in range(1, tap_count):
                            value = value + taps_x[view, tap] * source[view, x + below - tap]
                        stack.append(value.astype(bf16))
                    columns.append(jnp.concatenate(stack, axis=0))
                both = jnp.concatenate(columns, axis=1)
                result = jnp.dot(back_y[...], both, preferred_element_type=f32)
                rows = block_y + 2 * HALO_Y
                result = result[:rows] + result[rows:]
                for side in range(2):
                    x = first + side
                    lanes = slice(side * depth, (side + 1) * depth)
                    acc[sweep, x] = result[:block_y, lanes]
                    out_y[sweep, 0, x] = result[block_y : block_y + HALO_Y, lanes].astype(bf16)
                    out_y[sweep, 1, x] = result[block_y + HALO_Y :, lanes].astype(bf16)

            @pl.when(jnp.logical_and(step >= first_chunk, step <= last_chunk))
            def _():
                vert(4 * step, 4).start()

        sums = (
            ghosts_of_sums(
                links, out_x.at[sweep], out_y.at[sweep], in_x.at[sweep], in_y.at[sweep]
            ),
            acc_send.at[sweep],
            acc_recv.at[sweep],
        )

        @pl.loop(0, edge_turns)
        def _(turn):
            adjoint(turn)

        @pl.loop(0, radius)
        def _(x):
            out_x[sweep, 0, x] = acc[sweep, x].astype(bf16)
            out_x[sweep, 1, x] = acc[sweep, radius + block_x + x].astype(bf16)

        links.start(*sums, links.across_x())

        @pl.loop(edge_turns, planes // 4)
        def _(turn):
            adjoint(turn)

        links.start(*sums, links.along_y_only())
        links.finish(*sums, links.across_x())
        links.finish(*sums, links.along_y_only())
        forwards = [
            pltpu.make_async_remote_copy(
                src_ref=near.at[sweep],
                dst_ref=far.at[sweep],
                send_sem=far_send.at[sweep, index],
                recv_sem=far_recv.at[sweep, index],
                device_id=partner,
                device_id_type=pl.DeviceIdType.MESH,
            )
            for index, (near, far) in enumerate(((in_x, far_x), (in_y, far_y)))
        ]
        for forward in forwards:
            forward.start()
        vert(4 * first_chunk, 4 * (last_chunk - first_chunk + 1)).wait()

        @pl.loop(0, block_x)
        def _(x):
            acc[sweep, radius + x] = acc[sweep, radius + x] + vert_in[sweep, radius + x]

        for forward in forwards:
            forward.wait()

        def beyond_y(side, plane):
            return in_y[sweep, side, plane].astype(f32) + far_y[sweep, side, plane].astype(f32)

        @pl.loop(0, radius)
        def _(x):
            for side, at, beside in ((0, radius + x, x), (1, block_x + x, radius + block_x + x)):
                plane = acc[sweep, at] + (
                    in_x[sweep, side, x].astype(f32) + far_x[sweep, side, x].astype(f32)
                )
                first = plane[:HALO_Y] + beyond_y(0, beside)
                last = plane[block_y - HALO_Y :] + beyond_y(1, beside)
                acc[sweep, at] = jnp.concatenate(
                    [first, plane[HALO_Y : block_y - HALO_Y], last], axis=0
                )

        def update(x):
            plane = acc[sweep, radius + x]
            first = plane[:HALO_Y] + beyond_y(0, radius + x)
            last = plane[block_y - HALO_Y :] + beyond_y(1, radius + x)
            combined = jnp.concatenate([first, plane[HALO_Y : block_y - HALO_Y], last], axis=0)
            before = initial[x] if sweep == 0 else estimate[x]
            after = before * (combined + damping) * inverse_norm[x]
            estimate[x] = after
            if sweep + 1 < ITERS:
                publish(
                    links, center.at[sweep], send_low.at[sweep], send_high.at[sweep], x, after
                )

        if sweep + 1 < ITERS:
            news = (
                ghosts_of_estimate(
                    links,
                    center.at[sweep],
                    low.at[sweep],
                    high.at[sweep],
                    send_low.at[sweep],
                    send_high.at[sweep],
                ),
                est_send.at[sweep],
                est_recv.at[sweep],
            )

            @pl.loop(0, radius)
            def _(x):
                update(x)
                update(block_x - radius + x)

            links.start(*news, links.across_x())

            @pl.loop(radius, block_x - radius)
            def _(x):
                update(x)

            links.start(*news, links.along_y_only())
            links.finish(*news, links.directions)
        else:

            @pl.loop(0, block_x)
            def _(x):
                update(x)


def sweeps(
    sizes, taps_x, observed, spreads, initial, inverse_norm, along_y, back_y, along_z, back_z
):
    block_x, block_y, depth = initial.shape
    views = observed.shape[0]
    radius = taps_x.shape[1] // 2
    planes = planes_of(block_x, radius)
    extended_x = block_x + 2 * radius
    vmem = pl.BlockSpec(memory_space=pltpu.VMEM)
    bf16 = jnp.bfloat16
    f32 = jnp.float32
    repeats = ITERS - 1
    return pl.pallas_call(
        functools.partial(sweep_kernel, sizes),
        out_shape=jax.ShapeDtypeStruct(initial.shape, f32),
        in_specs=[pl.BlockSpec(memory_space=pltpu.SMEM)] + [vmem] * 8,
        out_specs=vmem,
        scratch_shapes=[
            pltpu.VMEM((repeats,) + scratch.shape, scratch.dtype)
            for scratch in estimate_scratch(planes, block_x, block_y, depth)
        ]
        + [
            pltpu.VMEM((views, planes, block_y, depth), f32),
            pltpu.VMEM((views, planes + 2 * radius, block_y, depth), f32),
            pltpu.VMEM((ITERS, planes, block_y, depth), f32),
            pltpu.VMEM((ITERS, 2, radius, block_y, depth), bf16),
            pltpu.VMEM((ITERS, 2, planes, HALO_Y, depth), bf16),
            pltpu.VMEM((ITERS, 2, radius, block_y, depth), bf16),
            pltpu.VMEM((ITERS, 2, extended_x, HALO_Y, depth), bf16),
            pltpu.VMEM((ITERS, 2, radius, block_y, depth), bf16),
            pltpu.VMEM((ITERS, 2, extended_x, HALO_Y, depth), bf16),
            pltpu.VMEM((ITERS, planes, block_y, depth), f32),
            pltpu.SemaphoreType.DMA((repeats, 8)),
            pltpu.SemaphoreType.DMA((repeats, 8)),
            pltpu.SemaphoreType.DMA((ITERS, 8)),
            pltpu.SemaphoreType.DMA((ITERS, 8)),
            pltpu.SemaphoreType.DMA((ITERS,)),
            pltpu.SemaphoreType.DMA((ITERS,)),
            pltpu.SemaphoreType.DMA((ITERS, 2)),
            pltpu.SemaphoreType.DMA((ITERS, 2)),
        ],
        compiler_params=pltpu.CompilerParams(
            collective_id=1, has_side_effects=True, vmem_limit_bytes=40 << 20
        ),
    )(taps_x, observed, spreads, initial, inverse_norm, along_y, back_y, along_z, back_z)


PAIR_SLOTS = 8
ROW = 40
FAR_AWAY = -1000
MESH = pl.DeviceIdType.MESH


def far_slots(per_device):
    return 3 * per_device // 4


def plan_kernel(per_device, block, xs, ys, table):
    views = table.shape[1]
    pack, slot, entry_x, entry_y = (table.at[index] for index in range(4))
    me = lax.axis_index("gx")
    row = lax.axis_index("gy")
    first = lax.axis_index("vert") * views
    in_low = me < 2
    beside = jnp.where(lax.rem(me, 2) == 0, me + 1, me - 1)
    far_base = jnp.where(in_low, 2, 0)
    far_outer = jnp.where(in_low, 3, 0)
    far_gate = jnp.where(in_low, 2, 1)
    my_outer = jnp.where(in_low, 0, 3)
    spare = 4 * PAIR_SLOTS
    one, zero = jnp.int32(1), jnp.int32(0)
    for view in range(views):
        for at in range(spare):
            pack[view, at] = zero
            slot[view, at] = zero
            entry_x[view, at] = zero
            entry_y[view, at] = jnp.int32(FAR_AWAY)

        def read(source):
            places = [source * per_device + j for j in range(per_device)]
            return [[ref[first + view, row, at] for at in places] for ref in (block, xs, ys)]

        def enter(at, where, x, y):
            slot[view, at] = where
            entry_x[view, at] = x
            entry_y[view, at] = y

        own_targets, own_x, own_y = read(me)
        mine = near = outer = zero
        for j in range(per_device):
            target = own_targets[j]
            enter(jnp.where(target == me, mine, spare), jnp.int32(j), own_x[j], own_y[j])
            at = jnp.where(
                target == beside,
                near,
                jnp.where(target == far_outer, PAIR_SLOTS + outer, spare),
            )
            pack[view, at] = jnp.int32(j)
            mine = mine + jnp.where(target == me, one, zero)
            near = near + jnp.where(target == beside, one, zero)
            outer = outer + jnp.where(target == far_outer, one, zero)
        for j in range(per_device):
            target = own_targets[j]
            pack[view, jnp.where(target == far_gate, PAIR_SLOTS + outer, spare)] = jnp.int32(j)
            outer = outer + jnp.where(target == far_gate, one, zero)
        found = zero
        targets, from_x, from_y = read(beside)
        for j in range(per_device):
            hit = targets[j] == me
            enter(jnp.where(hit, PAIR_SLOTS + found, spare), found, from_x[j], from_y[j])
            found = found + jnp.where(hit, one, zero)
        for side in range(2):
            base = (2 + side) * PAIR_SLOTS
            found = ahead = zero
            targets, from_x, from_y = read(far_base + side)
            for j in range(per_device):
                target = targets[j]
                hit = target == me
                enter(jnp.where(hit, base + found, spare), found, from_x[j], from_y[j])
                found = found + jnp.where(hit, one, zero)
                ahead = ahead + jnp.where(target == my_outer, one, zero)
            ahead = jnp.where(me == my_outer, zero, ahead)
            for at in range(base, base + PAIR_SLOTS):
                slot[view, at] = jnp.minimum(slot[view, at] + ahead, far_slots(per_device) - 1)


def plan(views, per_device, block, xs, ys):
    smem = pl.BlockSpec(memory_space=pltpu.SMEM)
    return pl.pallas_call(
        functools.partial(plan_kernel, per_device),
        out_shape=jax.ShapeDtypeStruct((4, views, ROW), jnp.int32),
        in_specs=[smem] * 3,
        out_specs=smem,
    )(block, xs, ys)


def band_of(psf, view, dim, difference):
    summed = jnp.zeros(difference.shape, jnp.float32)
    for tap in range(psf.shape[2]):
        summed = jnp.where(difference == tap, psf[view, dim, tap], summed)
    return summed


def halves(value):
    high = value.astype(jnp.bfloat16)
    return high, (value - high.astype(jnp.float32)).astype(jnp.bfloat16)


def iota(shape, dim):
    return lax.broadcasted_iota(jnp.int32, shape, dim)


def make_bands(psf, first, radius, block_y, along_y, back_y, back_one, along_z, back_z):
    views = along_z.shape[0]
    depth = along_z.shape[2]
    wide = block_y + 2 * HALO_Y

    def place_of(index):
        inside = jnp.where(index >= wide, index - wide, index)
        return jnp.where(
            inside < block_y,
            inside,
            jnp.where(inside < block_y + HALO_Y, inside - block_y - HALO_Y, inside - HALO_Y),
        )

    backs = []
    for view in range(views):
        shape = (block_y, 2 * wide)
        column = iota(shape, 1)
        high, low = halves(
            band_of(psf, first + view, 1, place_of(column) - iota(shape, 0) + radius)
        )
        f32 = jnp.float32
        rows = slice(view * block_y, (view + 1) * block_y)
        along_y[rows] = jnp.where(column < wide, high.astype(f32), low.astype(f32)).astype(
            jnp.bfloat16
        )
        shape = (2 * wide, block_y)
        row = iota(shape, 0)
        high, low = halves(band_of(psf, first + view, 1, place_of(row) - iota(shape, 1) + radius))
        back = jnp.where(row < wide, high.astype(f32), low.astype(f32))
        backs.append(back)
        back_one[view] = back.astype(jnp.bfloat16)
        shape = (depth, depth)
        difference = iota(shape, 0) - iota(shape, 1)
        along_z[view] = jnp.concatenate(
            halves(band_of(psf, first + view, 2, difference + radius)), axis=0
        )
        back_z[view] = jnp.concatenate(
            halves(band_of(psf, first + view, 2, radius - difference)), axis=0
        )
    back_y[...] = jnp.concatenate(backs, axis=1).astype(jnp.bfloat16)


def contract_last(left, right):
    return lax.dot_general(
        left, right, (((1,), (1,)), ((), ())), preferred_element_type=jnp.float32
    )


def make_norm(psf, first, radius, tile_shape, block, xs, ys, counts, spread, inverse_norm, scale):
    all_views, rows, tiles_row = block.shape
    block_x, block_y, depth = inverse_norm.shape
    views = scale.shape[0]
    tile_wide, tile_tall = tile_shape
    f32 = jnp.float32
    bf16 = jnp.bfloat16
    edge = 8
    near_x = block_x + 2 * edge
    near_y = block_y + 2 * edge
    start_x = lax.axis_index("gx") * block_x - edge
    start_y = lax.axis_index("gy") * block_y - edge
    profiles = []
    for view in range(all_views):
        summed = None
        for row in range(rows):
            left = block[view, row : row + 1] * block_x + xs[view, row : row + 1]
            top = ys[view, row : row + 1] + row * block_y
            from_x = iota((near_x, tiles_row), 0) + start_x - left
            from_y = iota((near_y, tiles_row), 0) + start_y - top
            in_x = jnp.where((from_x >= 0) & (from_x < tile_wide), f32(1), f32(0)).astype(bf16)
            in_y = jnp.where((from_y >= 0) & (from_y < tile_tall), f32(1), f32(0)).astype(bf16)
            term = contract_last(in_y, in_x)
            summed = term if summed is None else summed + term
        counts[view] = summed
        covered = jnp.minimum(summed, 1.0).astype(bf16)
        shape = (block_y, near_y)
        high, low = halves(
            band_of(psf, view, 1, iota(shape, 0) - (iota(shape, 1) - edge) + radius)
        )
        value = jnp.dot(high, covered, preferred_element_type=f32)
        value = value + jnp.dot(low, covered, preferred_element_type=f32)
        shape = (near_x, block_x)
        high, low = halves(
            band_of(psf, view, 0, iota(shape, 1) - (iota(shape, 0) - edge) + radius)
        )
        value_high, value_low = halves(value)
        result = jnp.dot(value_high, high, preferred_element_type=f32)
        result = result + jnp.dot(value_low, high, preferred_element_type=f32)
        result = result + jnp.dot(value_high, low, preferred_element_type=f32)
        spread[view] = result
        profile = jnp.zeros((1, depth), f32)
        place = iota((1, depth), 1)
        for tap in range(psf.shape[2]):
            source = place - tap + radius
            profile = profile + jnp.where(
                (source >= 0) & (source < depth), psf[view, 2, tap], f32(0)
            )
        profiles.append(profile)
    shares = [
        1.0 / jnp.maximum(counts[first + view, edge : edge + block_y], 1.0)
        for view in range(views)
    ]
    for view in range(views):
        counts[first + view, edge : edge + block_y] = shares[view]
    shape = (block_y, depth)
    for x in range(block_x):
        summed = None
        for view in range(all_views):
            term = jnp.broadcast_to(spread[view, :, x : x + 1], shape) * profiles[view]
            summed = term if summed is None else summed + term
        inverse_norm[x] = 1.0 / (summed + damping)
        at = edge + x
        for view in range(views):
            scale[view, x] = jnp.broadcast_to(
                counts[first + view, edge : edge + block_y, at : at + 1], shape
            )


class Route:
    def __init__(self, tx_near, tx_far, rx_near, rx_far, sems):
        self.me = lax.axis_index("gx")
        low = self.me < 2
        self.inside = lax.rem(self.me, 2)
        self.beside = jnp.where(self.inside == 0, self.me + 1, self.me - 1)
        self.gate = jnp.where(low, 2, 1)
        self.is_gate = jnp.logical_or(self.me == 1, self.me == 2)
        self.tx_near, self.tx_far, self.rx_near, self.rx_far = tx_near, tx_far, rx_near, rx_far
        self.near_send, self.near_recv, self.far_send, self.far_recv, self.on_send = sems
        self.pieces = ((0, 4), (4, 4), (8, tx_far.shape[1] - 8))

    def near(self, view):
        return pltpu.make_async_remote_copy(
            src_ref=self.tx_near.at[view],
            dst_ref=self.rx_near[view],
            send_sem=self.near_send.at[view],
            recv_sem=self.near_recv.at[view],
            device_id={"gx": self.beside},
            device_id_type=MESH,
        )

    def far(self, view, piece, side):
        span = pl.ds(*self.pieces[piece])
        return pltpu.make_async_remote_copy(
            src_ref=self.tx_far.at[view, span],
            dst_ref=self.rx_far[view].at[side, span],
            send_sem=self.far_send.at[view, piece],
            recv_sem=self.far_recv.at[view, side, piece],
            device_id={"gx": self.gate},
            device_id_type=MESH,
        )

    def onward(self, view, piece, side):
        span = pl.ds(*self.pieces[piece])
        return pltpu.make_async_remote_copy(
            src_ref=self.rx_far[view].at[side, span],
            dst_ref=self.rx_far[view].at[side, span],
            send_sem=self.on_send.at[view, side, piece],
            recv_sem=self.far_recv.at[view, side, piece],
            device_id={"gx": self.beside},
            device_id_type=MESH,
        )

    def pack_near(self, view, tiles, pack):
        for at in range(PAIR_SLOTS):
            self.tx_near[view, at] = tiles[view][pack[view, at]]

    def pack_far(self, view, tiles, pack):
        for at in range(self.tx_far.shape[1]):
            self.tx_far[view, at] = tiles[view][pack[view, PAIR_SLOTS + at]]

    def send(self, view, pieces):
        for piece in pieces:
            self.far(view, piece, self.inside).start()

    def sent(self, view, piece):
        self.far(view, piece, self.inside).wait_send()

    def hand_on(self, view, piece):
        @pl.when(self.is_gate)
        def _():
            for side in range(2):
                self.far(view, piece, side).wait_recv()
                self.onward(view, piece, side).start()

    def receive_far(self, view):
        @pl.when(self.is_gate)
        def _():
            for side in range(2):
                self.far(view, 2, side).wait_recv()

        @pl.when(jnp.logical_not(self.is_gate))
        def _():
            for piece in range(2):
                for side in range(2):
                    self.onward(view, piece, side).wait_recv()

    def drain(self, views):
        for view in range(views):
            for piece in range(3):
                if piece == 0 or view in (0, views - 1):
                    self.sent(view, piece)
            self.near(view).wait_send()

        @pl.when(self.is_gate)
        def _():
            for view in range(views):
                for piece in range(2):
                    for side in range(2):
                        self.onward(view, piece, side).wait_send()


def chooser_of(view, chosen, entry_y, tile_tall, block_y):
    entries = len(chosen)
    lane = iota((8, entries * tile_tall), 1)
    target = jnp.zeros(lane.shape, jnp.int32)
    for index, entry in enumerate(chosen):
        inside = (lane >= index * tile_tall) & (lane < (index + 1) * tile_tall)
        target = jnp.where(inside, entry_y[view, entry] + lane - index * tile_tall, target)
    target = target[:1]
    one, zero = jnp.float32(1), jnp.float32(0)
    rows = iota((block_y, target.shape[1]), 0)
    return jnp.where(rows == target, one, zero).astype(jnp.bfloat16)


def pass_along_y_of(steps, center, low, high, along_y, passed_y, views):
    block_y, depth = center.shape[1:]

    def one(step):
        for first in (4 * step, 4 * step + 2):
            columns = []
            for x in (first, first + 1):
                edges = jnp.concatenate(
                    [low[x].astype(jnp.float32), high[x].astype(jnp.float32)], axis=0
                ).astype(jnp.bfloat16)
                columns.append(jnp.concatenate([center[x], edges], axis=0))
            both = jnp.concatenate(columns, axis=1)
            both = jnp.concatenate([both, both], axis=0)
            result = jnp.dot(along_y[...], both, preferred_element_type=jnp.float32)
            for view in range(views):
                rows = slice(view * block_y, (view + 1) * block_y)
                passed_y[view, first] = result[rows, :depth]
                passed_y[view, first + 1] = result[rows, depth:]

    if isinstance(steps, range):
        pl.loop(steps.start, steps.stop, unroll=len(steps))(one)
    else:
        for step in steps:
            one(step)


def place_view(view, sources, groups, tables, padded, partial, begins, ends, refs):
    slot, entry_x, entry_y = tables
    scale, per_blur, back_z, observed, spread = refs
    block_x, block_y, depth = observed.shape[1:]
    bf16 = jnp.bfloat16
    f32 = jnp.float32
    padded_planes, tile_tall = padded.shape[1:3]
    margin = padded_planes - block_x
    tile_wide = block_x - margin
    chosen = [g * PAIR_SLOTS + at for g in sources for at in range(PAIR_SLOTS)]
    for entry in chosen:
        read = groups[entry // PAIR_SLOTS]
        padded[entry, margin : margin + tile_wide] = read(slot[view, entry])
    chooser = chooser_of(view, chosen, entry_y, tile_tall, block_y)

    def place_pair(first):
        columns = []
        for x in (first, first + 1):
            rows = [padded[entry, x + margin - entry_x[view, entry]] for entry in chosen]
            columns.append(jnp.concatenate(rows, axis=0))
        both = jnp.concatenate(columns, axis=1)
        summed = jnp.dot(chooser, both, preferred_element_type=f32)
        quotients = []
        for side in range(2):
            x = first + side
            plane = summed[:, side * depth : (side + 1) * depth]
            if not begins:
                plane = plane + partial[x]
            if not ends:
                partial[x] = plane
                continue
            observed[view, x] = plane * scale[view, x]
            quotients.append((plane * per_blur[view, x]).astype(bf16))
        return quotients

    pairs = 4

    @pl.loop(0, block_x // (2 * pairs))
    def _(step):
        quotients = []
        for pair in range(pairs):
            quotients += place_pair(2 * pairs * step + 2 * pair)
        if ends:
            stacked = jnp.concatenate(quotients, axis=0)
            stacked = jnp.concatenate([stacked, stacked], axis=1)
            result = jnp.dot(stacked, back_z[view], preferred_element_type=f32)
            for side in range(2 * pairs):
                rows = slice(side * block_y, (side + 1) * block_y)
                spread[view, 2 * pairs * step + side] = result[rows]


def routed_kernel(sizes, *refs):
    (
        psf,
        table,
        tiles_from,
        block,
        xs,
        ys,
        initial_from,
        estimate,
        fullest,
        start_center,
        start_low,
        start_high,
        start_send_low,
        start_send_high,
        start_send,
        start_recv,
        center,
        low,
        high,
        send_low,
        send_high,
        passed_y,
        passed_z,
        acc,
        acc_y,
        out_x,
        out_y,
        in_x,
        in_y,
        far_x,
        far_y,
        vert_in,
        est_send,
        est_recv,
        acc_send,
        acc_recv,
        vert_send,
        vert_recv,
        far_send,
        far_recv,
        taps_x,
        along_y,
        back_y,
        back_one,
        along_z,
        back_z,
        counts,
        norm_spread,
        inverse_norm,
        scale,
        per_blur,
        observed,
        part_send,
        part_recv,
        initial,
        load_sems,
        fill_mine,
        fill_other,
        fill_send,
        fill_recv,
        padded,
        partial,
        tx_near,
        tx_far,
        *rest,
    ) = refs
    views, block_x, block_y, depth = observed.shape
    pack, slot, entry_x, entry_y = (table.at[index] for index in range(4))
    tiles, rx_near, rx_far = (rest[at * views : (at + 1) * views] for at in range(3))
    route_sems = rest[3 * views :]
    tap_count = psf.shape[2]
    radius = tap_count // 2
    planes = center.shape[1]
    per_device = tiles_from.shape[2]
    tile_shape = tiles_from.shape[3:5]
    bf16 = jnp.bfloat16
    f32 = jnp.float32
    links = Links(sizes, radius, block_x)
    column = lax.axis_index("gx")
    first_view = lax.axis_index("vert") * views
    partner = {"vert": 1 - lax.axis_index("vert")}
    part_count = lax.axis_size("groups")
    parts = [
        {"groups": lax.rem(lax.axis_index("groups") + step, part_count)}
        for step in range(1, part_count)
    ]
    route = Route(tx_near, tx_far, rx_near, rx_far, route_sems)

    loads = [
        pltpu.make_async_copy(tiles_from.at[view, 0], tiles[view], load_sems.at[view])
        for view in range(views)
    ]
    loads.append(pltpu.make_async_copy(initial_from, initial, load_sems.at[views]))
    for load in loads:
        load.start()
    barrier = pltpu.get_barrier_semaphore()
    others = [partner] + parts
    others += [{"gx": lax.rem(column + step, sizes[0])} for step in range(1, sizes[0])]
    for other in others:
        pl.semaphore_signal(barrier, inc=1, device_id=other, device_id_type=MESH)
    peers = len(others)
    for dx, dy in links.directions:
        if dy == 0:
            continue
        peers = peers + links.exists(dx, dy).astype(jnp.int32)

        @pl.when(links.exists(dx, dy))
        def _():
            pl.semaphore_signal(
                barrier, inc=1, device_id=links.device(dx, dy), device_id_type=MESH
            )

    loads[0].wait()
    route.pack_far(0, tiles, pack)
    pl.semaphore_wait(barrier, peers)
    route.send(0, range(3))
    route.pack_near(0, tiles, pack)
    route.near(0).start()
    loads[views].wait()

    @pl.loop(0, block_x, unroll=4)
    def _(x):
        publish(links, start_center, start_send_low, start_send_high, x, initial[x])

    clear_missing(links, start_center, start_low, start_high)
    start = (
        ghosts_of_estimate(
            links, start_center, start_low, start_high, start_send_low, start_send_high
        ),
        start_send,
        start_recv,
    )
    links.start(*start, links.directions)
    for view in range(1, views):
        loads[view].wait()
        route.pack_near(view, tiles, pack)
        route.near(view).start()
        route.pack_far(view, tiles, pack)
        if view == 1:
            route.send(view, (0,))

    number = iota(block.shape[1:], 1)
    most = jnp.zeros((block.shape[1], 1), f32)
    for view in range(block.shape[0]):
        beyond = (block[view] >= sizes[0] // 2) != (number >= block.shape[2] // 2)
        for source in range(sizes[0]):
            within = (number >= source * per_device) & (number < (source + 1) * per_device)
            count = jnp.sum(jnp.where(beyond & within, f32(1), f32(0)), axis=1, keepdims=True)
            most = jnp.maximum(most, count)
    fill_mine[...] = jnp.broadcast_to(jnp.max(most, axis=0, keepdims=True), fill_mine.shape)
    fills = [
        pltpu.make_async_remote_copy(
            src_ref=fill_mine,
            dst_ref=fill_other.at[index],
            send_sem=fill_send.at[index],
            recv_sem=fill_recv.at[index],
            device_id=other,
            device_id_type=MESH,
        )
        for index, other in enumerate(parts)
    ]
    for fill in fills:
        fill.start()

    make_bands(psf, first_view, radius, block_y, along_y, back_y, back_one, along_z, back_z)
    for view in range(views):
        for tap in range(tap_count):
            taps_x[view, tap] = psf[first_view + view, 0, tap]
    for sweep in range(ITERS):
        if sweep > 0:
            at = sweep - 1
            clear_missing(links, center.at[at], low.at[at], high.at[at])
        for step in (-1, 1):
            side = 0 if step == -1 else 1

            @pl.when(jnp.logical_not(links.exists(step, 0)))
            def _():
                in_x[sweep, side] = jnp.zeros(in_x.shape[2:], bf16)
                for other in range(2):
                    in_y[sweep, other, links.ghost(step)] = jnp.zeros(
                        (radius,) + in_y.shape[3:], bf16
                    )

            @pl.when(jnp.logical_not(links.exists(0, step)))
            def _():
                in_y[sweep, side] = jnp.zeros(in_y.shape[2:], bf16)

    for entry in range(padded.shape[0]):
        padded[entry] = jnp.zeros(padded.shape[1:], bf16)
    group = group_of(block_x)

    make_norm(
        psf,
        first_view,
        radius,
        tile_shape,
        block,
        xs,
        ys,
        counts,
        norm_spread,
        inverse_norm,
        scale,
    )
    links.finish(*start, links.directions)
    if views > 1:
        route.send(1, (1, 2))
    pass_along_y(start_center, start_low, start_high, along_y, passed_y, views)

    @pl.loop(0, block_x // group)
    def _(step):
        first = step * group
        for view in range(views):
            blurred = pass_along_xz(taps_x, passed_y, along_z[view], view, first, group)
            blurred = blurred.reshape(group, block_y, depth)
            chunk = pl.ds(first, group)
            per_blur[view, chunk] = scale[view, chunk] / (blurred + soft_floor)

    for fill in fills:
        fill.wait()
    greatest = fill_mine[...]
    for index in range(len(fills)):
        greatest = jnp.maximum(greatest, fill_other[index])
    fullest[0, 0] = jnp.max(greatest)

    def vert_copy(sweep, start, size):
        chunk = pl.ds(start, size)
        return pltpu.make_async_remote_copy(
            src_ref=acc.at[sweep, chunk],
            dst_ref=vert_in.at[sweep, chunk],
            send_sem=vert_send.at[sweep],
            recv_sem=vert_recv.at[sweep],
            device_id=partner,
            device_id_type=MESH,
        )

    first_chunk = radius // 4
    last_chunk = (radius + block_x - 1) // 4
    far_chunk = (radius + block_x) // 4
    edge_turns = planes // 4 - far_chunk + -(-radius // 4)
    rows = block_y + 2 * HALO_Y

    def adjoint(sweep, chosen, begins, ends, step, static):
        matrix = back_y[...] if len(chosen) == views else back_one[chosen[0]]
        last_plane = block_x + 2 * radius - 1
        for first in (4 * step, 4 * step + 2):
            if static and first > last_plane:
                continue
            columns = []
            for x in (first, first + 1):
                stack = []
                for view in chosen:
                    taps = range(tap_count)
                    if static:
                        taps = [tap for tap in taps if 0 <= x - tap < block_x]
                    value = None
                    for tap in taps:
                        term = taps_x[view, tap] * passed_z[view, x - tap]
                        value = term if value is None else value + term
                    stack.append(value.astype(bf16))
                columns.append(jnp.concatenate(stack, axis=0))
            both = jnp.concatenate(columns, axis=1)
            result = jnp.dot(matrix, both, preferred_element_type=f32)
            result = result[:rows] + result[rows:]
            for side in range(2):
                x = first + side
                lanes = slice(side * depth, (side + 1) * depth)
                middle, edges = result[:block_y, lanes], result[block_y:, lanes]
                if not begins:
                    middle = middle + acc[sweep, x]
                    edges = edges + acc_y[x]
                acc[sweep, x] = middle
                if ends:
                    out_y[sweep, 0, x] = edges[:HALO_Y].astype(bf16)
                    out_y[sweep, 1, x] = edges[HALO_Y:].astype(bf16)
                else:
                    acc_y[x] = edges

        if ends:
            if not static:
                vert_copy(sweep, 4 * step, 4).start()
            elif first_chunk <= step <= last_chunk:
                vert_copy(sweep, 4 * step, 4).start()

    inner_range = range(-(-radius // 4), (radius + block_x) // 4)
    outer_steps = [step for step in range(planes // 4) if step not in inner_range]
    whole = (-(-(tap_count - 1) // 4), block_x // 4)
    edge_steps = [(turn + far_chunk) % (planes // 4) for turn in range(edge_turns)]
    inner_steps = [
        step
        for step in range(planes // 4)
        if step not in edge_steps and not whole[0] <= step < whole[1]
    ]

    def adjoint_edges(*how):
        for step in edge_steps:
            adjoint(*how, step, True)

    middle = (whole[0] + whole[1]) // 2
    y_parts = (
        (radius, 4 * whole[0] - radius),
        (4 * whole[1], radius + block_x - 4 * whole[1]),
        (4 * whole[0], 4 * (middle - whole[0])),
        (4 * middle, 4 * (whole[1] - middle)),
    )

    def adjoint_inside(sweep, chosen, begins, ends):
        how = (sweep, chosen, begins, ends)
        for step in inner_steps:
            adjoint(*how, step, True)
        if ends:
            start_sums_y(sweep, (0, 1))

        @pl.loop(whole[0], middle)
        def _(step):
            adjoint(*how, step, False)

        if ends:
            start_sums_y(sweep, (2,))

        @pl.loop(middle, whole[1])
        def _(step):
            adjoint(*how, step, False)

        if ends:
            start_sums_y(sweep, (3,))

    def sums_y(sweep, dy, part):
        side = 0 if dy == -1 else 1
        span = pl.ds(*y_parts[part])
        return pltpu.make_async_remote_copy(
            src_ref=out_y.at[sweep, side, span],
            dst_ref=in_y.at[sweep, 1 - side, span],
            send_sem=part_send.at[sweep, side, part],
            recv_sem=part_recv.at[sweep, side, part],
            device_id=links.device(0, dy),
            device_id_type=MESH,
        )

    def start_sums_y(sweep, parts_now):
        for dy in (-1, 1):

            @pl.when(links.exists(0, dy))
            def _():
                for part in parts_now:
                    sums_y(sweep, dy, part).start()

    def finish_sums_y(sweep):
        for dy in (-1, 1):

            @pl.when(links.exists(0, dy))
            def _():
                for part in range(len(y_parts)):
                    sums_y(sweep, dy, part).wait_send()

            @pl.when(links.exists(0, -dy))
            def _():
                for part in range(len(y_parts)):
                    sums_y(sweep, dy, part).wait_recv()

    for sweep in range(ITERS):
        if sweep == 0:
            for view in range(views):
                groups = [
                    lambda at: tiles[view][at],
                    lambda at: rx_near[view][at],
                    lambda at: rx_far[view][0, at],
                    lambda at: rx_far[view][1, at],
                ]
                place = functools.partial(
                    place_view,
                    groups=groups,
                    tables=(slot, entry_x, entry_y),
                    padded=padded,
                    partial=partial,
                    refs=(scale, per_blur, back_z, observed, passed_z),
                )
                last = view + 1 == views
                if view == 0:
                    route.hand_on(view, 0)
                paced = view > 0 and not last
                for piece in (1, 2):
                    if paced:
                        route.sent(view, piece)
                        route.send(view + 1, (piece,))
                    if piece == 1:
                        route.hand_on(view, piece)
                if last:
                    route.near(view).wait_recv()
                    place(view, (0, 1), begins=True, ends=False)
                route.receive_far(view)
                if last:
                    place(view, (2, 3), begins=False, ends=True)
                else:
                    route.near(view).wait_recv()
                    place(view, (0, 1, 2, 3), begins=True, ends=True)
                    if view + 2 < views:
                        route.send(view + 2, (0,))
                    if view > 0:
                        route.hand_on(view + 1, 0)

                    adjoint_edges(sweep, (view,), view == 0, False)
                    adjoint_inside(sweep, (view,), view == 0, False)

                    if view == 0:
                        route.hand_on(view + 1, 0)

            chosen, begins = (views - 1,), views == 1
        else:
            at = sweep - 1
            pass_along_y_of(outer_steps, center.at[at], low.at[at], high.at[at], along_y, passed_y, views)

            @pl.loop(0, block_x // group, unroll=2)
            def _(step):
                first = step * group
                for view in range(views):
                    blurred = pass_along_xz(taps_x, passed_y, along_z[view], view, first, group)
                    measured = observed[view, pl.ds(first, group)].reshape(blurred.shape)
                    result = spread_quotient(measured, blurred, back_z[view])
                    passed_z[view, pl.ds(first, group)] = result.reshape(
                        group, block_y, depth
                    )

            chosen, begins = tuple(range(views)), True

        sums = (
            ghosts_of_sums(
                links, out_x.at[sweep], out_y.at[sweep], in_x.at[sweep], in_y.at[sweep]
            ),
            acc_send.at[sweep],
            acc_recv.at[sweep],
        )

        adjoint_edges(sweep, chosen, begins, True)

        @pl.loop(0, radius, unroll=radius)
        def _(x):
            out_x[sweep, 0, x] = acc[sweep, x].astype(bf16)
            out_x[sweep, 1, x] = acc[sweep, radius + block_x + x].astype(bf16)

        links.start(*sums, links.across_x())

        adjoint_inside(sweep, chosen, begins, True)

        forwards = [
            pltpu.make_async_remote_copy(
                src_ref=near.at[sweep],
                dst_ref=far.at[sweep],
                send_sem=far_send.at[sweep, index],
                recv_sem=far_recv.at[sweep, index],
                device_id=partner,
                device_id_type=pl.DeviceIdType.MESH,
            )
            for index, (near, far) in enumerate(((in_x, far_x), (in_y, far_y)))
        ]
        links.finish(*sums, [(-1, 0), (1, 0)])
        forwards[0].start()
        links.finish(*sums, [one for one in links.across_x() if one[1] != 0])
        finish_sums_y(sweep)
        forwards[1].start()
        vert_copy(sweep, 4 * first_chunk, 4 * (last_chunk - first_chunk + 1)).wait()

        @pl.loop(0, block_x, unroll=4)
        def _(x):
            acc[sweep, radius + x] = acc[sweep, radius + x] + vert_in[sweep, radius + x]

        for forward in forwards:
            forward.wait()

        def beyond_y(side, plane):
            return in_y[sweep, side, plane].astype(f32) + far_y[sweep, side, plane].astype(f32)

        @pl.loop(0, radius, unroll=radius)
        def _(x):
            for side, at, beside in ((0, radius + x, x), (1, block_x + x, radius + block_x + x)):
                plane = acc[sweep, at] + (
                    in_x[sweep, side, x].astype(f32) + far_x[sweep, side, x].astype(f32)
                )
                first = plane[:HALO_Y] + beyond_y(0, beside)
                last = plane[block_y - HALO_Y :] + beyond_y(1, beside)
                acc[sweep, at] = jnp.concatenate(
                    [first, plane[HALO_Y : block_y - HALO_Y], last], axis=0
                )

        def update(x):
            plane = acc[sweep, radius + x]
            first = plane[:HALO_Y] + beyond_y(0, radius + x)
            last = plane[block_y - HALO_Y :] + beyond_y(1, radius + x)
            combined = jnp.concatenate([first, plane[HALO_Y : block_y - HALO_Y], last], axis=0)
            before = initial[x] if sweep == 0 else estimate[x]
            after = before * (combined + damping) * inverse_norm[x]
            estimate[x] = after
            if sweep + 1 < ITERS:
                publish(
                    links, center.at[sweep], send_low.at[sweep], send_high.at[sweep], x, after
                )

        if sweep + 1 < ITERS:
            news = (
                ghosts_of_estimate(
                    links,
                    center.at[sweep],
                    low.at[sweep],
                    high.at[sweep],
                    send_low.at[sweep],
                    send_high.at[sweep],
                ),
                est_send.at[sweep],
                est_recv.at[sweep],
            )

            @pl.loop(0, radius, unroll=radius)
            def _(x):
                update(x)
                update(block_x - radius + x)

            links.start(*news, links.across_x())

            @pl.loop(radius, block_x - radius, unroll=3)
            def _(x):
                update(x)

            links.start(*news, links.along_y_only())
            links.finish(*news, links.along_y_only())
            pass_along_y_of(
                inner_range,
                center.at[sweep],
                low.at[sweep],
                high.at[sweep],
                along_y,
                passed_y,
                views,
            )
            links.finish(*news, links.across_x())
        else:

            @pl.loop(0, block_x, unroll=4)
            def _(x):
                update(x)

    route.drain(views)


def routed(tiles, tile_block, tile_x, tile_y, psf, initial):
    block_x, block_y, depth = initial.shape
    views, _, per_device = tiles.shape[:3]
    all_views, rows, tiles_row = tile_x.shape
    tile = tiles.shape[3:]
    radius = psf.shape[2] // 2
    planes = planes_of(block_x, radius)
    extended_x = block_x + 2 * radius
    wide = block_y + 2 * HALO_Y
    sizes = (lax.axis_size("gx"), lax.axis_size("gy"))
    part_count = lax.axis_size("groups")
    cap = far_slots(per_device)
    block = tile_block.reshape(tile_x.shape)
    tables = plan(views, per_device, block, tile_x, tile_y)
    vmem = pl.BlockSpec(memory_space=pltpu.VMEM)
    smem = pl.BlockSpec(memory_space=pltpu.SMEM)
    anywhere = pl.BlockSpec(memory_space=pl.ANY)
    dma = pltpu.SemaphoreType.DMA
    bf16 = jnp.bfloat16
    f32 = jnp.float32
    repeats = ITERS - 1
    volume = (views, block_x, block_y, depth)
    return pl.pallas_call(
        functools.partial(routed_kernel, sizes),
        out_shape=[
            jax.ShapeDtypeStruct(initial.shape, f32),
            jax.ShapeDtypeStruct((1, 1), f32),
        ],
        in_specs=[smem] * 2 + [anywhere] + [vmem] * 3 + [anywhere],
        out_specs=[vmem, smem],
        scratch_shapes=estimate_scratch(planes, block_x, block_y, depth)
        + [dma((8,)), dma((8,))]
        + [
            pltpu.VMEM((repeats,) + scratch.shape, scratch.dtype)
            for scratch in estimate_scratch(planes, block_x, block_y, depth)
        ]
        + [
            pltpu.VMEM((views, planes, block_y, depth), f32),
            pltpu.VMEM(volume, f32),
            pltpu.VMEM((ITERS, planes, block_y, depth), f32),
            pltpu.VMEM((planes, 2 * HALO_Y, depth), f32),
            pltpu.VMEM((ITERS, 2, radius, block_y, depth), bf16),
            pltpu.VMEM((ITERS, 2, planes, HALO_Y, depth), bf16),
            pltpu.VMEM((ITERS, 2, radius, block_y, depth), bf16),
            pltpu.VMEM((ITERS, 2, extended_x, HALO_Y, depth), bf16),
            pltpu.VMEM((ITERS, 2, radius, block_y, depth), bf16),
            pltpu.VMEM((ITERS, 2, extended_x, HALO_Y, depth), bf16),
            pltpu.VMEM((ITERS, planes, block_y, depth), f32),
            dma((repeats, 8)),
            dma((repeats, 8)),
            dma((ITERS, 8)),
            dma((ITERS, 8)),
            dma((ITERS,)),
            dma((ITERS,)),
            dma((ITERS, 2)),
            dma((ITERS, 2)),
            pltpu.SMEM((views, psf.shape[2]), f32),
            pltpu.VMEM((views * block_y, 2 * wide), bf16),
            pltpu.VMEM((2 * wide, views * block_y), bf16),
            pltpu.VMEM((views, 2 * wide, block_y), bf16),
            pltpu.VMEM((views, 2 * depth, depth), bf16),
            pltpu.VMEM((views, 2 * depth, depth), bf16),
            pltpu.VMEM((all_views, block_y + 16, block_x + 16), f32),
            pltpu.VMEM((all_views, block_y, block_x), f32),
            pltpu.VMEM(initial.shape, f32),
            pltpu.VMEM(volume, f32),
            pltpu.VMEM(volume, f32),
            pltpu.VMEM(volume, f32),
            dma((ITERS, 2, 4)),
            dma((ITERS, 2, 4)),
            pltpu.VMEM(initial.shape, f32),
            dma((views + 1,)),
            pltpu.VMEM((8, 128), f32),
            pltpu.VMEM((part_count - 1, 8, 128), f32),
            dma((part_count - 1,)),
            dma((part_count - 1,)),
            pltpu.VMEM((4 * PAIR_SLOTS, 2 * block_x - tile[0]) + tile[1:], bf16),
            pltpu.VMEM(volume[1:], f32),
            pltpu.VMEM((views, PAIR_SLOTS) + tile, bf16),
            pltpu.VMEM((views, cap) + tile, bf16),
        ]
        + [pltpu.VMEM(tiles.shape[2:], bf16)] * views
        + [pltpu.VMEM((PAIR_SLOTS,) + tile, bf16)] * views
        + [pltpu.VMEM((2, cap) + tile, bf16)] * views
        + [dma((views,)), dma((views,)), dma((views, 3)), dma((views, 2, 3)), dma((views, 2, 2))],
        compiler_params=pltpu.CompilerParams(
            collective_id=2, has_side_effects=True, vmem_limit_bytes=56 << 20
        ),
    )(psf, tables, tiles, block, tile_x, tile_y, initial)


def general(tiles, tile_block, tile_x, tile_y, psf, initial):
    column_count = lax.axis_size("gx")
    column_index = lax.axis_index("gx")
    row_index = lax.axis_index("gy")
    core_index = lax.axis_index("vert")
    local_views = tiles.shape[0]
    all_views = psf.shape[0]
    per_device = tiles.shape[2]
    tile_wide = tiles.shape[3]
    tile_tall = tiles.shape[4]
    block_x, block_y, depth = initial.shape
    capacity = max(2, 2 * per_device // column_count)
    radius = psf.shape[2] // 2
    first_view = core_index * local_views
    mine_psf = lax.dynamic_slice_in_dim(psf, first_view, local_views, 0)

    def my_rows(table):
        chosen = lax.dynamic_slice_in_dim(table, first_view, local_views, 0)
        chosen = lax.dynamic_slice_in_dim(chosen, row_index, 1, 1)[:, 0]
        return chosen.reshape(local_views, column_count, per_device)

    targets = my_rows(tile_block[:, :, :, 0])
    offsets_x = my_rows(tile_x)
    offsets_y = my_rows(tile_y)
    columns_iota = jnp.arange(column_count, dtype=jnp.int32)
    hits = (targets[..., None] == columns_iota).astype(jnp.int32)
    ranks = jnp.cumsum(hits, axis=2, dtype=jnp.int32)
    slot_ids = jnp.arange(capacity, dtype=jnp.int32) + 1
    sent_hits = jnp.swapaxes(lax.dynamic_slice_in_dim(hits, column_index, 1, 1)[:, 0], 1, 2)
    sent_ranks = jnp.swapaxes(lax.dynamic_slice_in_dim(ranks, column_index, 1, 1)[:, 0], 1, 2)
    chooser = sent_hits[:, :, None, :] * (
        sent_ranks[:, :, None, :] == slot_ids[None, None, :, None]
    ).astype(jnp.int32)
    outgoing = jnp.einsum(
        "vgkj,vjabz->gvkabz",
        chooser.astype(jnp.bfloat16),
        tiles[:, 0],
        preferred_element_type=jnp.bfloat16,
    )
    sizes = (column_count, lax.axis_size("gy"))
    halos = first_halos(sizes, radius, initial)
    outgoing, halos = lax.optimization_barrier((outgoing, halos))
    arrived = lax.all_to_all(outgoing, "gx", split_axis=0, concat_axis=0, tiled=True)
    from_hits = lax.dynamic_slice_in_dim(hits, column_index, 1, 3)[..., 0]
    from_ranks = lax.dynamic_slice_in_dim(ranks, column_index, 1, 3)[..., 0]
    picks = from_hits[:, :, None, :] * (
        from_ranks[:, :, None, :] == slot_ids[None, None, :, None]
    ).astype(jnp.int32)
    filled = jnp.sum(picks, axis=3).reshape(local_views, -1)
    corner_x = jnp.sum(picks * offsets_x[:, :, None, :], axis=3).reshape(local_views, -1)
    corner_y = jnp.sum(picks * offsets_y[:, :, None, :], axis=3).reshape(local_views, -1)

    row_iota = jnp.arange(tile_block.shape[1], dtype=jnp.int32)
    global_x = (tile_block[..., 0] * block_x + tile_x).reshape(all_views, -1)
    global_y = (row_iota[None, :, None] * block_y + tile_y).reshape(all_views, -1)
    near_x = jnp.arange(block_x + 2 * radius, dtype=jnp.int32) - radius
    near_y = jnp.arange(block_y + 2 * radius, dtype=jnp.int32) - radius
    cells_x = column_index * block_x + near_x
    cells_y = row_index * block_y + near_y
    cover_x = (
        (cells_x >= global_x[..., None]) & (cells_x < global_x[..., None] + tile_wide)
    ).astype(jnp.bfloat16)
    cover_y = (
        (cells_y >= global_y[..., None]) & (cells_y < global_y[..., None] + tile_tall)
    ).astype(jnp.bfloat16)
    counts = jnp.einsum("vti,vtj->vij", cover_x, cover_y, preferred_element_type=jnp.float32)
    coverage = jnp.minimum(counts, 1.0)
    iota_x = jnp.arange(block_x, dtype=jnp.int32)
    iota_y = jnp.arange(block_y, dtype=jnp.int32)
    iota_z = jnp.arange(depth, dtype=jnp.int32)
    adjoint_x = banded(psf[:, 0], iota_x[:, None] - near_x[None, :] + radius)
    adjoint_y = banded(psf[:, 1], iota_y[:, None] - near_y[None, :] + radius)
    exact = lax.Precision.HIGHEST
    spread = jnp.einsum("vij,vyj->viy", coverage, adjoint_y, precision=exact)
    spread = jnp.einsum("vxi,viy->vxy", adjoint_x, spread, precision=exact)
    profile = jnp.sum(banded(psf[:, 2], iota_z[:, None] - iota_z[None, :] + radius), axis=2)
    norm_field = jnp.einsum("vxy,vz->xyz", spread, profile, precision=exact)
    inverse_norm = 1.0 / (norm_field + damping)

    places_y = jnp.concatenate(
        [
            iota_y,
            jnp.arange(HALO_Y, dtype=jnp.int32) - HALO_Y,
            jnp.arange(HALO_Y, dtype=jnp.int32) + block_y,
        ]
    )
    band_y = banded(mine_psf[:, 1], places_y[None, :] - iota_y[:, None] + radius)
    high, low = split_high_low(band_y)
    flat = (local_views * block_y, places_y.shape[0])
    along_y = jnp.concatenate([high.reshape(flat), low.reshape(flat)], axis=1)
    back_y = jnp.concatenate([high.reshape(flat).T, low.reshape(flat).T], axis=0)
    band_z = banded(mine_psf[:, 2], iota_z[:, None] - iota_z[None, :] + radius)
    along_z = jnp.concatenate(split_high_low(band_z), axis=1)
    back_z = jnp.concatenate(split_high_low(jnp.swapaxes(band_z, 1, 2)), axis=1)
    taps_x = mine_psf[:, 0]
    blurred = first_blur(taps_x, halos, along_y, along_z, block_x)
    observed, spreads = place(filled, corner_x, corner_y, arrived, blurred, back_z, radius)
    return sweeps(
        sizes,
        taps_x,
        observed,
        spreads,
        initial,
        inverse_norm,
        along_y,
        back_y,
        along_z,
        back_z,
    )


def shards(tiles, tile_block, tile_x, tile_y, psf, initial):
    arguments = (tiles, tile_block, tile_x, tile_y, psf, initial)
    if lax.axis_size("gx") != 4:
        return general(*arguments)
    estimate, fullest = routed(*arguments)
    return lax.cond(
        fullest[0, 0] > far_slots(tiles.shape[2]),
        lambda result, *rest: general(*rest),
        lambda result, *rest: result,
        estimate,
        *arguments,
    )


def solution(mesh):
    in_specs = (
        P("vert", "gy", ("groups", "gx"), None, None, None),
        P(None, None, "groups", None),
        P(None, None, "groups"),
        P(None, None, "groups"),
        P(),
        P(("groups", "gx"), "gy", None),
    )
    out_specs = P(("groups", "gx"), "gy", None)
    return jax.shard_map(shards, mesh=mesh, in_specs=in_specs, out_specs=out_specs, check_vma=False)
```
